32 devices in a mesh: seq: 8 (over z, y), mp: 4 (over x, core).
Axes of the slice: x: 2, y: 2, z: 4, core: 2. Of those that a mesh axis runs over, the one named last changes fastest.
Arguments:
- hidden_entry_states: bfloat16 [1024, 512], P('seq'), may hold values from -6 to 6
- base_ids: int32 [1024], P('seq'), may hold values from 0 to 4
- mask_index: int32 [128], P('seq'), may hold values from 0 to 1023, as said below
- first_kernel: bfloat16 [9, 512, 512], P(None, None, 'mp'), may hold values from -0.09375 to 0.09375
- second_kernel: bfloat16 [9, 512, 512], P(None, None, 'mp'), may hold values from -0.09375 to 0.09375
- head_weight: bfloat16 [512, 5], replicated, may hold values from -0.5 to 0.5
Outputs:
- input_grad: bfloat16 [1024, 512], P('seq')
- first_kernel_gradient: float32 [9, 512, 512], P(None, 'seq', 'mp')
- second_kernel_gradient: float32 [9, 512, 512], P(None, 'seq', 'mp')
The draws below stay inside these ranges and needn't reach their ends.
Inputs may be any that keep to these rules, and one draw needn't show every extreme that they name: `mask_index`: each device's 16 entries are distinct positions within its own block of 128 bases, in no particular order.
All inputs are finite; a program needn't handle non-finite values.
Results may differ from the reference program's by a relative error of at most 0.014.
Values may be sent and summed in bfloat16 or wider, within the bound.
No kernel may reach another device: no remote copies, remote signals or barrier semaphores. Data moves between devices by JAX's collectives and lax.ppermute only.
A program may use at most 64 MiB of HBM per device.

```python
import jax
import jax.numpy as jnp
from jax import lax

D = 512
K = 9
DILATION_FIRST1 = 2048
DILATION_SECOND2 = 4096
VOCAB = 5
BLK = 128
BASES = 1024
MASK_DEV = 16


def draw_mask_index(key, part):
    block_count = BASES // BLK

    def pick_block(block_index):
        block_key = jax.random.fold_in(key, block_index)
        shuffled = jax.random.permutation(jax.random.fold_in(block_key, 1), BLK).astype(jnp.int32)
        needed = jnp.where(block_index == 0, 0, BLK - 1).astype(jnp.int32)
        special = jnp.logical_or(block_index == 0, block_index == block_count - 1)
        where_needed = jnp.argmax(shuffled == needed).astype(jnp.int32)
        swapped = shuffled.at[where_needed].set(shuffled[0]).at[0].set(needed)
        chosen = jnp.where(special, swapped, shuffled)[:MASK_DEV]
        order = jax.random.permutation(jax.random.fold_in(block_key, 2), MASK_DEV)
        return chosen[order] + block_index * BLK
    picked = jax.vmap(pick_block)(jnp.arange(block_count, dtype=jnp.int32))
    return picked.reshape(-1).astype(jnp.int32)


def set_ends(values, key, low, top_value):
    dims = values.shape
    place = [jax.random.randint(jax.random.fold_in(key, axis), (), 0, dims[axis]) for axis in range(len(dims))]
    values = values.at[tuple(place)].set(low)
    longest = dims.index(max(dims))
    place[longest] = (place[longest] + 1) % dims[longest]
    return values.at[tuple(place)].set(top_value)


def levels(stream_key, extent, shards, low, largest):
    def one(axis_at, parts):
        heights = jax.random.uniform(jax.random.fold_in(jax.random.fold_in(stream_key, 6), axis_at), (parts,), jnp.float32, low / len(shards), largest / len(shards))
        return jnp.repeat(jnp.exp(heights), extent[axis_at] // parts).reshape((-1,) + (1,) * (len(extent) - axis_at - 1))

    factor_of = one(*shards[0])
    for cut in shards[1:]:
        factor_of = factor_of * one(*cut)
    return factor_of


def gaussian(own_key, shape, deviation, limit, split=(), kind=jnp.bfloat16):
    factor_of = levels(own_key, shape, split, -0.22, 0.18) if split else 1.0
    drawn = jax.random.normal(own_key, shape, jnp.float32) * deviation * factor_of
    return jnp.minimum(jnp.maximum(drawn, -limit), limit).astype(kind)


def setup_inputs(seed: int = 0) -> dict:
    seeds = jax.random.split(jax.random.key(seed), 7)
    hidden_entry_states = gaussian(seeds[0], (BASES, D), 1.0, 6.0, ((0, 8),))
    base_ids = set_ends(jax.random.randint(seeds[1], (BASES,), 0, VOCAB), jax.random.fold_in(seeds[1], 1), 0, VOCAB - 1).astype(jnp.int32)
    mask_index = draw_mask_index(jax.random.fold_in(seeds[6], 71), 0)
    first_kernel = gaussian(seeds[3], (K, D, D), (K * D) ** -0.5, 0.09375, ((2, 4),))
    second_kernel = gaussian(seeds[4], (K, D, D), (K * D) ** -0.5, 0.09375, ((2, 4),))
    head_weight = gaussian(seeds[5], (D, VOCAB), (D // 4) ** -0.5, 0.5)
    return dict(hidden_entry_states=hidden_entry_states, base_ids=base_ids, mask_index=mask_index, first_kernel=first_kernel, second_kernel=second_kernel, head_weight=head_weight)


epsilon = 1e-05
root_half = 0.7071067811865476
inv_root_two_pi = 0.3989422804014327

def slide_rows(values, offset):
    row_count = values.shape[0]
    if offset == 0:
        return values
    if abs(offset) >= row_count:
        return jnp.zeros_like(values)
    filler = jnp.zeros((abs(offset),) + values.shape[1:], values.dtype)
    if offset > 0:
        return jnp.concatenate([values[offset:], filler], axis=0)
    return jnp.concatenate([filler, values[:row_count + offset]], axis=0)

def gelu_parts(conv_out):
    normal_cdf = 0.5 * (1.0 + lax.erf(conv_out * root_half))
    gelu_slope = normal_cdf + conv_out * inv_root_two_pi * jnp.exp(-0.5 * conv_out * conv_out)
    return (conv_out * normal_cdf, gelu_slope)

def norm_parts(activation):
    values = activation.astype(jnp.float32)
    centre = lax.optimization_barrier(jnp.mean(values, axis=-1, keepdims=True))
    centred = values - centre
    spread = lax.optimization_barrier(jnp.mean(centred * centred, axis=-1, keepdims=True))
    inverse = lax.rsqrt(spread + epsilon)
    return (centred * inverse, inverse)

def block_forward_pass(source, kernel, dilation):
    tap_count = kernel.shape[0]
    centre_tap = tap_count // 2
    conv_out = jnp.zeros((source.shape[0], kernel.shape[2]), jnp.float32)
    for tap_index in range(tap_count):
        moved = slide_rows(source, dilation * (tap_index - centre_tap))
        conv_out = conv_out + jnp.dot(moved, kernel[tap_index], preferred_element_type=jnp.float32)
    activation, gelu_slope = gelu_parts(conv_out)
    normed, inverse = norm_parts(activation.astype(jnp.bfloat16))
    result = (source.astype(jnp.float32) + normed).astype(jnp.bfloat16)
    return (result, (source, normed, inverse, gelu_slope))

def block_backward_pass(grad_out, saved, kernel, dilation):
    source, normed, inverse, gelu_slope = saved
    tap_count = kernel.shape[0]
    centre_tap = tap_count // 2
    mean_grad = lax.optimization_barrier(jnp.mean(grad_out, axis=-1, keepdims=True))
    mean_cross = lax.optimization_barrier(jnp.mean(grad_out * normed, axis=-1, keepdims=True))
    grad_act = inverse * (grad_out - mean_grad - normed * mean_cross)
    grad_conv = (grad_act * gelu_slope).astype(jnp.bfloat16)
    tap_grads = []
    grad_in = grad_out
    for tap_index in range(tap_count):
        offset = dilation * (tap_index - centre_tap)
        tap_grads.append(jnp.dot(slide_rows(source, offset).T, grad_conv, preferred_element_type=jnp.float32))
        back = jnp.dot(grad_conv, kernel[tap_index].T, preferred_element_type=jnp.float32)
        grad_in = grad_in + slide_rows(back, -offset)
    return (grad_in, jnp.stack(tap_grads, axis=0))

def reference(hidden_entry_states, base_ids, mask_index, first_kernel, second_kernel, head_weight):
    hidden_after_first, first_residuals = block_forward_pass(hidden_entry_states, first_kernel, DILATION_FIRST1)
    hidden_after_second, second_residuals = block_forward_pass(hidden_after_first, second_kernel, DILATION_SECOND2)
    mask_row = jnp.zeros((BASES,), jnp.float32).at[mask_index].set(1.0)
    logits = jnp.dot(hidden_after_second, head_weight, preferred_element_type=jnp.float32)
    exponent = jnp.exp(logits)
    probability = exponent / lax.optimization_barrier(jnp.sum(exponent, axis=1, keepdims=True))
    vocab_cols = lax.broadcasted_iota(jnp.int32, logits.shape, 1)
    onehot = (vocab_cols == base_ids[:, None]).astype(jnp.float32)
    dlogits = mask_row[:, None] * (probability - onehot)
    gradient_after_second = jnp.dot(dlogits, head_weight.astype(jnp.float32).T, precision=lax.Precision.HIGHEST)
    gradient_after_first, second_kernel_gradient = block_backward_pass(gradient_after_second, second_residuals, second_kernel, DILATION_SECOND2)
    gradient_before_first, first_kernel_gradient = block_backward_pass(gradient_after_first, first_residuals, first_kernel, DILATION_FIRST1)
    return (gradient_before_first.astype(jnp.bfloat16), first_kernel_gradient, second_kernel_gradient)
```

```python
import jax
import jax.numpy as jnp
from jax import lax
from jax.experimental import pallas as pl
from jax.experimental.pallas import tpu as pltpu
from jax.sharding import PartitionSpec as P

DILATION_FIRST1 = 2048
DILATION_SECOND2 = 4096


epsilon = 1e-05
root_half = 0.7071067811865476
inv_root_two_pi = 0.3989422804014327
ROW_CHUNK = 32


def gelu_parts(conv_out):
    normal_cdf = 0.5 * (1.0 + lax.erf(conv_out * root_half))
    gelu_slope = normal_cdf + conv_out * inv_root_two_pi * jnp.exp(-0.5 * conv_out * conv_out)
    return (conv_out * normal_cdf, gelu_slope)


def norm_parts(activation):
    values = activation.astype(jnp.float32)
    centre = jnp.mean(values, axis=-1, keepdims=True)
    centred = values - centre
    spread = jnp.mean(centred * centred, axis=-1, keepdims=True)
    inverse = lax.rsqrt(spread + epsilon)
    return (centred * inverse, inverse)


def active_hops(tap_count, dilation_blocks, seq_count):
    centre_tap = tap_count // 2
    hops = [(tap, dilation_blocks * (tap - centre_tap)) for tap in range(tap_count)]
    return [(tap, hop) for tap, hop in hops if abs(hop) < seq_count]


def shifted(x, axis, by):
    if by == 0:
        return x
    peers = lax.axis_size(axis)
    pairs = [(i, i + by) for i in range(peers) if 0 <= i + by < peers]
    return lax.ppermute(x, axis, pairs)


def loss_grad(hidden_top, targets, head_weight):
    logits = lax.dot_general(
        head_weight, hidden_top, (((0,), (1,)), ((), ())), preferred_element_type=jnp.float32
    )
    exponent = jnp.exp(logits)
    probability = exponent / jnp.sum(exponent, axis=0, keepdims=True)
    vocab_rows = lax.broadcasted_iota(jnp.int32, logits.shape, 0)
    onehot = (vocab_rows == targets[None, :]).astype(jnp.float32)
    weight = (targets >= 0).astype(jnp.float32)[None, :]
    dlogits = weight * (probability - onehot)
    return lax.dot_general(
        dlogits,
        head_weight.astype(jnp.float32),
        (((0,), (1,)), ((), ())),
        precision=lax.Precision.HIGHEST,
    )


def general_plan(hidden_entry_states, base_ids, mask_index, first_kernel, second_kernel, head_weight, first_hops, second_hops):
    seq_count = lax.axis_size("seq")
    rows_per_block, channels = hidden_entry_states.shape
    tap_count, _, own_width = first_kernel.shape
    mask_count = mask_index.shape[0]
    offsets = mask_index - lax.axis_index("seq") * rows_per_block
    positions = lax.broadcasted_iota(jnp.int32, (rows_per_block, mask_count), 0)
    masked = jnp.any(positions == offsets[None, :], axis=1)
    targets = jnp.where(masked, base_ids, -1)

    def used(kernel, hops):
        first_tap, last_tap = hops[0][0], hops[-1][0]
        return kernel[first_tap : last_tap + 1]

    def block_forward_pass(source, kernel, hops):
        stacked = jnp.concatenate([shifted(source, "seq", -hop) for _, hop in hops], axis=1)
        conv_out = jnp.dot(
            stacked,
            used(kernel, hops).reshape(len(hops) * channels, own_width),
            preferred_element_type=jnp.float32,
        )
        activation, gelu_slope = gelu_parts(conv_out)
        mixed_all = lax.all_gather(activation.astype(jnp.bfloat16), "mp", axis=1, tiled=True)
        normed, inverse = norm_parts(mixed_all)
        result = (source.astype(jnp.float32) + normed).astype(jnp.bfloat16)
        return (result, (source, normed, inverse, gelu_slope))

    def block_backward_pass(grad_out, saved, kernel, hops):
        source, normed, inverse, gelu_slope = saved
        mean_grad = jnp.mean(grad_out, axis=-1, keepdims=True)
        mean_cross = jnp.mean(grad_out * normed, axis=-1, keepdims=True)
        grad_act = inverse * (grad_out - mean_grad - normed * mean_cross)
        own_cols = lax.dynamic_slice_in_dim(
            grad_act, lax.axis_index("mp") * own_width, own_width, 1
        )
        grad_conv = (own_cols * gelu_slope).astype(jnp.bfloat16)
        tap_stack = jnp.stack([shifted(grad_conv, "seq", hop) for _, hop in hops], axis=0)
        input_part = jnp.einsum(
            "kro,kdo->rd", tap_stack, used(kernel, hops), preferred_element_type=jnp.float32
        )
        grad_in = grad_out + lax.psum(input_part.astype(jnp.bfloat16), "mp").astype(jnp.float32)
        kernel_part = jnp.einsum(
            "rd,kro->kdo", source, tap_stack, preferred_element_type=jnp.float32
        )
        by_owner = kernel_part.reshape(len(hops), seq_count, channels // seq_count, own_width)
        received = lax.all_to_all(
            by_owner.astype(jnp.bfloat16), "seq", split_axis=1, concat_axis=1, tiled=True
        ).astype(by_owner.dtype)
        first_tap, last_tap = hops[0][0], hops[-1][0]
        kernel_grad = jnp.pad(
            jnp.sum(received, axis=1),
            ((first_tap, tap_count - 1 - last_tap), (0, 0), (0, 0)),
        )
        return (grad_in, kernel_grad)

    hidden_one, saved_one = block_forward_pass(hidden_entry_states, first_kernel, first_hops)
    hidden_two, saved_two = block_forward_pass(hidden_one, second_kernel, second_hops)
    grad_two = loss_grad(hidden_two, targets, head_weight)
    grad_one, second_grad = block_backward_pass(grad_two, saved_two, second_kernel, second_hops)
    grad_zero, first_grad = block_backward_pass(grad_one, saved_one, first_kernel, first_hops)
    return (grad_zero.astype(jnp.bfloat16), first_grad, second_grad)


NT = (((1,), (1,)), ((), ()))
TN = (((0,), (0,)), ((), ()))


def dot(a, b, dims=(((1,), (0,)), ((), ()))):
    return lax.dot_general(a, b, dims, preferred_element_type=jnp.float32)


def column_block(me, offset, width):
    return pl.ds(pl.multiple_of((me ^ offset) * width, width), width)


def gather_by_offset(own, count):
    blocks = {0: own}
    bit = count // 2
    while bit:
        pairs = [(i, i ^ bit) for i in range(count)]
        for offset in list(blocks):
            blocks[offset ^ bit] = lax.ppermute(blocks[offset], "mp", pairs)
        bit //= 2
    return [blocks[offset] for offset in range(count)]


def chunks(rows):
    size = ROW_CHUNK if rows % ROW_CHUNK == 0 else rows
    return [pl.ds(start, size) for start in range(0, rows, size)]


def norm_backward(grad_out, normed, inverse, gelu_slope):
    mean_grad = jnp.mean(grad_out, axis=-1, keepdims=True)
    mean_cross = jnp.mean(grad_out * normed, axis=-1, keepdims=True)
    grad_act = inverse * (grad_out - mean_grad - normed * mean_cross)
    return (grad_act * gelu_slope).astype(jnp.bfloat16)


def block_forward(me, source_ref, kernel_refs, conv_ref, hidden_ref, normed_ref, inverse_ref, slope_ref):
    width = kernel_refs[0].shape[1]
    source = source_ref[...]
    for offset, kernel_ref in enumerate(kernel_refs):
        conv_ref[:, column_block(me, offset, width)] = dot(source, kernel_ref[...])
    for rows in chunks(source_ref.shape[0]):
        activation, gelu_slope = gelu_parts(conv_ref[rows, :])
        normed, inverse = norm_parts(activation.astype(jnp.bfloat16))
        slope_ref[rows, :] = gelu_slope
        normed_ref[rows, :] = normed
        inverse_ref[rows, :] = inverse
        hidden_ref[rows, :] = (source_ref[rows, :].astype(jnp.float32) + normed).astype(jnp.bfloat16)


def first_block_body(count, me_ref, source_ref, *refs):
    kernel_refs = refs[:count]
    hidden_ref, normed_ref, inverse_ref, slope_ref, conv_ref = refs[count:]
    block_forward(me_ref[0], source_ref, kernel_refs, conv_ref, hidden_ref, normed_ref, inverse_ref, slope_ref)


def kernel_part(source_ref, grad_conv_ref, me, part_ref, slot):
    width = part_ref.shape[3]
    own = grad_conv_ref[:, column_block(me, 0, width)]
    part = dot(source_ref[...], own, TN).astype(jnp.bfloat16)
    depth = part_ref.shape[2]
    for owner in range(part_ref.shape[0]):
        part_ref[owner, slot] = part[owner * depth : (owner + 1) * depth]


def input_part(grad_conv_ref, kernel_refs, me):
    width = kernel_refs[0].shape[1]
    total = None
    for offset, kernel_ref in enumerate(kernel_refs):
        term = dot(grad_conv_ref[:, column_block(me, offset, width)], kernel_ref[...], NT)
        total = term if total is None else total + term
    return total


def rest_body(count, me_ref, mask_ref, source_ref, hidden_one_ref, normed_one_ref, inverse_one_ref, slope_one_ref, ids_ref, head_ref, *refs):
    first_refs = refs[:count]
    second_refs = refs[count : 2 * count]
    input_grad_ref, part_ref = refs[2 * count : 2 * count + 2]
    conv_ref, hidden_two_ref, normed_two_ref, inverse_two_ref, slope_two_ref, grad_ref, grad_conv_ref = refs[2 * count + 2 :]
    me = me_ref[0]
    block_forward(me, hidden_one_ref, second_refs, conv_ref, hidden_two_ref, normed_two_ref, inverse_two_ref, slope_two_ref)

    head = head_ref[...]
    logits = dot(head, hidden_two_ref[...], NT)
    exponent = jnp.exp(logits)
    probability = exponent / jnp.sum(exponent, axis=0, keepdims=True)
    onehot = (lax.broadcasted_iota(jnp.int32, logits.shape, 0) == ids_ref[...]).astype(jnp.float32)
    positions = lax.broadcasted_iota(jnp.int32, ids_ref.shape, 1) + me_ref[1]
    weight = jnp.zeros(ids_ref.shape, jnp.float32)
    for entry in range(mask_ref.shape[0]):
        weight = jnp.where(positions == mask_ref[entry], 1.0, weight)
    grad_logits = weight * (probability - onehot)
    grad_ref[...] = lax.dot_general(
        grad_logits,
        head.astype(jnp.float32),
        TN,
        precision=lax.Precision.HIGHEST,
        preferred_element_type=jnp.float32,
    )

    all_rows = chunks(source_ref.shape[0])
    for rows in all_rows:
        grad_conv_ref[rows, :] = norm_backward(
            grad_ref[rows, :], normed_two_ref[rows, :], inverse_two_ref[rows, :], slope_two_ref[rows, :]
        )
    kernel_part(hidden_one_ref, grad_conv_ref, me, part_ref, 1)
    grad_ref[...] += input_part(grad_conv_ref, second_refs, me)
    for rows in all_rows:
        grad_conv_ref[rows, :] = norm_backward(
            grad_ref[rows, :], normed_one_ref[rows, :], inverse_one_ref[rows, :], slope_one_ref[rows, :]
        )
    kernel_part(source_ref, grad_conv_ref, me, part_ref, 0)
    input_grad_ref[...] = (grad_ref[...] + input_part(grad_conv_ref, first_refs, me)).astype(jnp.bfloat16)


def local_plan(hidden_entry_states, base_ids, mask_index, first_kernel, second_kernel, head_weight):
    seq_count = lax.axis_size("seq")
    mp_count = lax.axis_size("mp")
    rows, channels = hidden_entry_states.shape
    tap_count, _, own_width = first_kernel.shape
    centre_tap = tap_count // 2
    me = lax.axis_index("mp")
    where = jnp.stack([me, lax.axis_index("seq") * rows]).astype(jnp.int32)
    first = gather_by_offset(first_kernel[centre_tap], mp_count)
    second = gather_by_offset(second_kernel[centre_tap], mp_count)

    vmem = pl.BlockSpec(memory_space=pltpu.VMEM)
    smem = pl.BlockSpec(memory_space=pltpu.SMEM)
    wide = jax.ShapeDtypeStruct((rows, channels), jnp.float32)
    thin = jax.ShapeDtypeStruct((rows, 1), jnp.float32)
    half = jax.ShapeDtypeStruct((rows, channels), jnp.bfloat16)
    params = pltpu.CompilerParams(vmem_limit_bytes=16 * 1024 * 1024)
    hidden_one, normed_one, inverse_one, slope_one = pl.pallas_call(
        lambda *refs: first_block_body(mp_count, *refs),
        out_shape=(half, wide, thin, wide),
        in_specs=[smem] + [vmem] * (1 + mp_count),
        out_specs=(vmem,) * 4,
        scratch_shapes=[pltpu.VMEM((rows, channels), jnp.float32)],
        compiler_params=params,
        name="first_block",
    )(where, hidden_entry_states, *first)

    part_shape = jax.ShapeDtypeStruct((seq_count, 2, channels // seq_count, own_width), jnp.bfloat16)
    input_grad, parts = pl.pallas_call(
        lambda *refs: rest_body(mp_count, *refs),
        out_shape=(half, part_shape),
        in_specs=[smem, smem] + [vmem] * (7 + 2 * mp_count),
        out_specs=(vmem, vmem),
        scratch_shapes=[
            pltpu.VMEM((rows, channels), jnp.float32),
            pltpu.VMEM((rows, channels), jnp.bfloat16),
            pltpu.VMEM((rows, channels), jnp.float32),
            pltpu.VMEM((rows, 1), jnp.float32),
            pltpu.VMEM((rows, channels), jnp.float32),
            pltpu.VMEM((rows, channels), jnp.float32),
            pltpu.VMEM((rows, channels), jnp.bfloat16),
        ],
        compiler_params=params,
        name="rest",
    )(
        where,
        mask_index,
        hidden_entry_states,
        hidden_one,
        normed_one,
        inverse_one,
        slope_one,
        base_ids[None, :],
        head_weight.T,
        *first,
        *second,
    )
    received = lax.all_to_all(parts, "seq", split_axis=0, concat_axis=0, tiled=True)
    totals = jnp.sum(received.astype(jnp.float32), axis=0)
    edges = ((centre_tap, tap_count - 1 - centre_tap), (0, 0), (0, 0))
    return (input_grad, jnp.pad(totals[0:1], edges), jnp.pad(totals[1:2], edges))


def local(hidden_entry_states, base_ids, mask_index, first_kernel, second_kernel, head_weight):
    rows = hidden_entry_states.shape[0]
    tap_count = first_kernel.shape[0]
    seq_count = lax.axis_size("seq")
    mp_count = lax.axis_size("mp")
    first_hops = active_hops(tap_count, DILATION_FIRST1 // rows, seq_count)
    second_hops = active_hops(tap_count, DILATION_SECOND2 // rows, seq_count)
    args = (hidden_entry_states, base_ids, mask_index, first_kernel, second_kernel, head_weight)
    if len(first_hops) == 1 and len(second_hops) == 1 and mp_count & (mp_count - 1) == 0:
        return local_plan(*args)
    return general_plan(*args, first_hops, second_hops)


def solution(mesh):
    placed = (P("seq", None), P("seq"), P("seq"), P(None, None, "mp"), P(None, None, "mp"), P())
    return jax.shard_map(
        local,
        mesh=mesh,
        in_specs=placed,
        out_specs=(P("seq", None), P(None, "seq", "mp"), P(None, "seq", "mp")),
        check_vma=False,
    )
```

```python
import functools

import jax
import jax.numpy as jnp
from jax import lax
from jax.experimental import pallas as pl
from jax.experimental.pallas import tpu as pltpu
from jax.sharding import PartitionSpec as P

DILATION_FIRST1 = 2048
DILATION_SECOND2 = 4096


epsilon = 1e-05
root_half = 0.7071067811865476
inv_root_two_pi = 0.3989422804014327
ROW_CHUNK = 32
SIDE_ROWS = 16
VMEM_LIMIT = 24 * 1024 * 1024


def gelu_parts(conv_out):
    normal_cdf = 0.5 * (1.0 + lax.erf(conv_out * root_half))
    gelu_slope = normal_cdf + conv_out * inv_root_two_pi * jnp.exp(-0.5 * conv_out * conv_out)
    return (conv_out * normal_cdf, gelu_slope)


def norm_parts(activation):
    values = activation.astype(jnp.float32)
    centre = jnp.mean(values, axis=-1, keepdims=True)
    centred = values - centre
    spread = jnp.mean(centred * centred, axis=-1, keepdims=True)
    inverse = lax.rsqrt(spread + epsilon)
    return (centred * inverse, inverse)


def active_hops(tap_count, dilation_blocks, seq_count):
    centre_tap = tap_count // 2
    hops = [(tap, dilation_blocks * (tap - centre_tap)) for tap in range(tap_count)]
    return [(tap, hop) for tap, hop in hops if abs(hop) < seq_count]


def shifted(x, axis, by):
    if by == 0:
        return x
    peers = lax.axis_size(axis)
    pairs = [(i, i + by) for i in range(peers) if 0 <= i + by < peers]
    return lax.ppermute(x, axis, pairs)


def loss_grad(hidden_top, targets, head_weight):
    logits = lax.dot_general(
        head_weight, hidden_top, (((0,), (1,)), ((), ())), preferred_element_type=jnp.float32
    )
    exponent = jnp.exp(logits)
    probability = exponent / jnp.sum(exponent, axis=0, keepdims=True)
    vocab_rows = lax.broadcasted_iota(jnp.int32, logits.shape, 0)
    onehot = (vocab_rows == targets[None, :]).astype(jnp.float32)
    weight = (targets >= 0).astype(jnp.float32)[None, :]
    dlogits = weight * (probability - onehot)
    return lax.dot_general(
        dlogits,
        head_weight.astype(jnp.float32),
        (((0,), (1,)), ((), ())),
        precision=lax.Precision.HIGHEST,
    )


def general_plan(hidden_entry_states, base_ids, mask_index, first_kernel, second_kernel, head_weight, first_hops, second_hops):
    seq_count = lax.axis_size("seq")
    rows_per_block, channels = hidden_entry_states.shape
    tap_count, _, own_width = first_kernel.shape
    mask_count = mask_index.shape[0]
    offsets = mask_index - lax.axis_index("seq") * rows_per_block
    positions = lax.broadcasted_iota(jnp.int32, (rows_per_block, mask_count), 0)
    masked = jnp.any(positions == offsets[None, :], axis=1)
    targets = jnp.where(masked, base_ids, -1)

    def used(kernel, hops):
        first_tap, last_tap = hops[0][0], hops[-1][0]
        return kernel[first_tap : last_tap + 1]

    def block_forward_pass(source, kernel, hops):
        stacked = jnp.concatenate([shifted(source, "seq", -hop) for _, hop in hops], axis=1)
        conv_out = jnp.dot(
            stacked,
            used(kernel, hops).reshape(len(hops) * channels, own_width),
            preferred_element_type=jnp.float32,
        )
        activation, gelu_slope = gelu_parts(conv_out)
        mixed_all = lax.all_gather(activation.astype(jnp.bfloat16), "mp", axis=1, tiled=True)
        normed, inverse = norm_parts(mixed_all)
        result = (source.astype(jnp.float32) + normed).astype(jnp.bfloat16)
        return (result, (source, normed, inverse, gelu_slope))

    def block_backward_pass(grad_out, saved, kernel, hops):
        source, normed, inverse, gelu_slope = saved
        mean_grad = jnp.mean(grad_out, axis=-1, keepdims=True)
        mean_cross = jnp.mean(grad_out * normed, axis=-1, keepdims=True)
        grad_act = inverse * (grad_out - mean_grad - normed * mean_cross)
        own_cols = lax.dynamic_slice_in_dim(
            grad_act, lax.axis_index("mp") * own_width, own_width, 1
        )
        grad_conv = (own_cols * gelu_slope).astype(jnp.bfloat16)
        tap_stack = jnp.stack([shifted(grad_conv, "seq", hop) for _, hop in hops], axis=0)
        input_part = jnp.einsum(
            "kro,kdo->rd", tap_stack, used(kernel, hops), preferred_element_type=jnp.float32
        )
        grad_in = grad_out + lax.psum(input_part.astype(jnp.bfloat16), "mp").astype(jnp.float32)
        kernel_part = jnp.einsum(
            "rd,kro->kdo", source, tap_stack, preferred_element_type=jnp.float32
        )
        by_owner = kernel_part.reshape(len(hops), seq_count, channels // seq_count, own_width)
        received = lax.all_to_all(
            by_owner.astype(jnp.bfloat16), "seq", split_axis=1, concat_axis=1, tiled=True
        ).astype(by_owner.dtype)
        first_tap, last_tap = hops[0][0], hops[-1][0]
        kernel_grad = jnp.pad(
            jnp.sum(received, axis=1),
            ((first_tap, tap_count - 1 - last_tap), (0, 0), (0, 0)),
        )
        return (grad_in, kernel_grad)

    hidden_one, saved_one = block_forward_pass(hidden_entry_states, first_kernel, first_hops)
    hidden_two, saved_two = block_forward_pass(hidden_one, second_kernel, second_hops)
    grad_two = loss_grad(hidden_two, targets, head_weight)
    grad_one, second_grad = block_backward_pass(grad_two, saved_two, second_kernel, second_hops)
    grad_zero, first_grad = block_backward_pass(grad_one, saved_one, first_kernel, first_hops)
    return (grad_zero.astype(jnp.bfloat16), first_grad, second_grad)


NN = (((1,), (0,)), ((), ()))
NT = (((1,), (1,)), ((), ()))
TN = (((0,), (0,)), ((), ()))


def dot(a, b, dims=NN):
    return lax.dot_general(a, b, dims, preferred_element_type=jnp.float32)


def xor_pairs(count, offset):
    return [(i, i ^ offset) for i in range(count)]


def block_at(me, offset, width):
    return pl.ds(pl.multiple_of((me ^ offset) * width, width), width)


def own_order(me, ref, rows, count):
    width = ref.shape[1] // count
    return jnp.concatenate([ref[rows, block_at(me, o, width)] for o in range(count)], axis=1)


def square(me, kernel_refs):
    width = kernel_refs[0].shape[1]
    count = len(kernel_refs)
    columns = [
        jnp.concatenate([ref[block_at(me, o, width), :] for o in range(count)], axis=0)
        for ref in kernel_refs
    ]
    return jnp.concatenate(columns, axis=1)


def row_chunks(rows, size):
    size = size if rows % size == 0 else rows
    return [pl.ds(start, size) for start in range(0, rows, size)]


def prepare_body(centre_tap, where_ref, mask_ref, ids_ref, source_ref, first_ref, second_ref, own_first_ref, own_second_ref, both_ref, rows_ref, sems):
    rows = source_ref.shape[0]
    copies = [
        pltpu.make_async_copy(first_ref.at[centre_tap], own_first_ref, sems.at[0]),
        pltpu.make_async_copy(second_ref.at[centre_tap], own_second_ref, sems.at[1]),
        pltpu.make_async_copy(source_ref, rows_ref.at[pl.ds(0, rows)], sems.at[2]),
    ]
    for copy in copies:
        copy.start()
    positions = lax.broadcasted_iota(jnp.int32, ids_ref.shape, 1) + where_ref[1] * rows
    masked = jnp.zeros(ids_ref.shape, jnp.int32)
    for entry in range(mask_ref.shape[0]):
        masked = jnp.where(positions == mask_ref[entry], 1, masked)
    targets = jnp.where(masked == 1, ids_ref[...], -1).astype(jnp.float32)
    extra = rows_ref.shape[0] - rows
    rows_ref[rows:, :] = jnp.zeros((extra, rows_ref.shape[1]), jnp.bfloat16)
    rows_ref[rows:, 0:rows] = jnp.broadcast_to(targets, (extra, rows)).astype(jnp.bfloat16)
    for copy in copies:
        copy.wait()
    both_ref[0] = own_first_ref[...]
    both_ref[1] = own_second_ref[...]


def first_block_body(count, where_ref, own_ref, peer_ref, head_ref, *refs):
    kernel_refs = refs[:count]
    hidden_ref, normed_ref, scale_ref, hidden_flip_ref, source_flip_ref, head_out_ref = refs[count:]
    me = where_ref[0]
    half = hidden_ref.shape[0] // 2
    width = kernel_refs[0].shape[1]
    weights = square(me, kernel_refs)
    for part, ref in enumerate((own_ref, peer_ref)):
        conv_out = dot(own_order(me, ref, pl.ds(0, half), count), weights)
        for start in range(0, half, ROW_CHUNK):
            rows = pl.ds(part * half + start, ROW_CHUNK)
            activation, gelu_slope = gelu_parts(conv_out[start : start + ROW_CHUNK])
            normed, inverse = norm_parts(activation.astype(jnp.bfloat16))
            scale_ref[rows, :] = gelu_slope * inverse
            normed_ref[rows, :] = normed
            source = own_order(me, ref, pl.ds(start, ROW_CHUNK), count)
            hidden_ref[rows, :] = (source.astype(jnp.float32) + normed).astype(jnp.bfloat16)
        source_flip_ref[:, pl.ds(part * half, half)] = ref[pl.ds(0, half), :].T
    for offset in range(count):
        flipped = hidden_ref[:, pl.ds(offset * width, width)].T
        hidden_flip_ref[block_at(me, offset, width), :] = flipped
    head_out_ref[...] = jnp.zeros_like(head_out_ref)
    classes = head_ref.shape[0]
    head_out_ref[0:classes, :] = own_order(me, head_ref, pl.ds(0, classes), count)


def rest_body(count, classes, where_ref, own_ref, peer_ref, head_ref, hidden_one_ref, normed_one_ref, scale_one_ref, hidden_flip_ref, source_flip_ref, *refs):
    kernel_refs = refs[:count]
    self_ref = refs[count]
    sent_refs = refs[count + 1 : -7]
    grad_out_ref, grad_conv_out_ref = refs[-7:-5]
    normed_two_ref, scale_two_ref, hidden_two_ref, grad_ref, grad_conv_ref = refs[-5:]
    me, block = where_ref[0], where_ref[1]
    total_rows = hidden_one_ref.shape[0]
    half = total_rows // 2
    width = kernel_refs[0].shape[1]
    depth = self_ref.shape[1]
    weights = square(me, kernel_refs)
    for start in range(0, total_rows, half):
        conv_out = dot(hidden_one_ref[pl.ds(start, half), :], weights)
        for inner in range(0, half, ROW_CHUNK):
            rows = pl.ds(start + inner, ROW_CHUNK)
            activation, gelu_slope = gelu_parts(conv_out[inner : inner + ROW_CHUNK])
            normed, inverse = norm_parts(activation.astype(jnp.bfloat16))
            scale_two_ref[rows, :] = gelu_slope * inverse
            normed_two_ref[rows, :] = normed
            hidden_two_ref[rows, :] = (hidden_one_ref[rows, :].astype(jnp.float32) + normed).astype(jnp.bfloat16)

    head = head_ref[...]
    logits = dot(head, hidden_two_ref[...], NT)
    class_rows = lax.broadcasted_iota(jnp.int32, logits.shape, 0)
    exponent = jnp.where(class_rows < classes, jnp.exp(logits), 0.0)
    probability = exponent / jnp.sum(exponent, axis=0, keepdims=True)
    targets = jnp.concatenate(
        [ref[half : half + head.shape[0], 0:half] for ref in (own_ref, peer_ref)], axis=1
    ).astype(jnp.float32)
    onehot = (class_rows.astype(jnp.float32) == targets).astype(jnp.float32)
    weight = (targets >= 0.0).astype(jnp.float32)
    rest = jnp.where(class_rows < classes, weight * (probability - onehot), 0.0)
    terms = []
    for _ in range(3):
        term = rest.astype(jnp.bfloat16)
        terms.append(term)
        rest = rest - term.astype(jnp.float32)
    grad_ref[...] = dot(jnp.concatenate(terms, axis=0), jnp.concatenate([head] * 3, axis=0), TN)

    def norm_backward(normed_ref, scale_ref):
        for rows in row_chunks(total_rows, ROW_CHUNK):
            grad_out, normed = grad_ref[rows, :], normed_ref[rows, :]
            mean_grad = jnp.mean(grad_out, axis=-1, keepdims=True)
            mean_cross = jnp.mean(grad_out * normed, axis=-1, keepdims=True)
            grad_conv_ref[rows, :] = (
                (grad_out - mean_grad - normed * mean_cross) * scale_ref[rows, :]
            ).astype(jnp.bfloat16)

    def kernel_parts(flip_ref, slot):
        owners = 1 + len(sent_refs)
        sources = [
            flip_ref[pl.ds(pl.multiple_of((block ^ (2 * j)) * depth, depth), depth), :]
            for j in range(owners)
        ]
        part = dot(jnp.concatenate(sources, axis=0), grad_conv_ref[:, 0:width])
        self_ref[slot] = part[0:depth]
        for j, ref in enumerate(sent_refs):
            ref[slot] = part[(j + 1) * depth : (j + 2) * depth].astype(jnp.bfloat16)

    norm_backward(normed_two_ref, scale_two_ref)
    for start in range(0, total_rows, half):
        rows = pl.ds(start, half)
        grad_ref[rows, :] += dot(grad_conv_ref[rows, :], weights, NT)
    kernel_parts(hidden_flip_ref, 1)
    norm_backward(normed_one_ref, scale_one_ref)
    kernel_parts(source_flip_ref, 0)
    grad_out_ref[...] = grad_ref[pl.ds(0, half), :]
    grad_conv_out_ref[...] = grad_conv_ref[pl.ds(0, half), :]


def input_grad_body(count, where_ref, grad_ref, grad_conv_ref, *refs):
    kernel_refs = refs[:count]
    input_grad_ref, first_ref, second_ref = refs[count:]
    me = where_ref[0]
    width = kernel_refs[0].shape[1]
    total = grad_ref[...] + dot(grad_conv_ref[...], square(me, kernel_refs), NT)
    for offset in range(count):
        input_grad_ref[:, block_at(me, offset, width)] = total[
            :, offset * width : (offset + 1) * width
        ].astype(jnp.bfloat16)
    first_ref[...] = jnp.zeros_like(first_ref)
    second_ref[...] = jnp.zeros_like(second_ref)


def total_body(centre_tap, first_in_ref, second_in_ref, self_ref, *refs):
    received = refs[:-4]
    first_ref, second_ref, sum_ref, sems = refs[-4:]
    sum_ref[...] = self_ref[...] + sum(ref[...].astype(jnp.float32) for ref in received)
    copies = [
        pltpu.make_async_copy(sum_ref.at[slot], ref.at[centre_tap], sems.at[slot])
        for slot, ref in enumerate((first_ref, second_ref))
    ]
    for copy in copies:
        copy.start()
    for copy in copies:
        copy.wait()


def local_plan(hidden_entry_states, base_ids, mask_index, first_kernel, second_kernel, head_weight):
    seq_count = lax.axis_size("seq")
    mp_count = lax.axis_size("mp")
    rows, channels = hidden_entry_states.shape
    tap_count, _, width = first_kernel.shape
    classes = head_weight.shape[1]
    centre_tap = tap_count // 2
    depth = channels // seq_count
    where = jnp.stack([lax.axis_index("mp"), lax.axis_index("seq")]).astype(jnp.int32)

    vmem = pl.BlockSpec(memory_space=pltpu.VMEM)
    smem = pl.BlockSpec(memory_space=pltpu.SMEM)
    anywhere = pl.BlockSpec(memory_space=pl.ANY)

    def shape(dims, dtype=jnp.bfloat16):
        return jax.ShapeDtypeStruct(dims, dtype)

    def call(body, name, in_specs, out_shape, out_specs=None, scratch=(), aliases={}, flops=0, moved=0):
        return pl.pallas_call(
            body,
            out_shape=out_shape,
            in_specs=in_specs,
            out_specs=(vmem,) * len(out_shape) if out_specs is None else out_specs,
            scratch_shapes=list(scratch),
            input_output_aliases=aliases,
            compiler_params=pltpu.CompilerParams(vmem_limit_bytes=VMEM_LIMIT),
            cost_estimate=pl.CostEstimate(flops=flops, bytes_accessed=moved, transcendentals=0),
            name=name,
        )

    own_first, own_second, own_both, own_rows = call(
        functools.partial(prepare_body, centre_tap),
        "prepare",
        [smem, smem, vmem, anywhere, anywhere, anywhere],
        (shape((channels, width)), shape((channels, width)), shape((2, channels, width)), shape((rows + SIDE_ROWS, channels))),
        scratch=[pltpu.SemaphoreType.DMA((3,))],
    )(where, mask_index, base_ids[None, :], hidden_entry_states, first_kernel, second_kernel)

    first, second = {0: own_first}, {0: own_second}
    bit = far = mp_count // 2
    while bit:
        pairs = xor_pairs(mp_count, bit)
        for offset in list(first):
            if offset == 0 and bit != far:
                both = lax.ppermute(own_both, "mp", pairs)
                first[bit], second[bit] = both[0], both[1]
            else:
                first[offset ^ bit] = lax.ppermute(first[offset], "mp", pairs)
                second[offset ^ bit] = lax.ppermute(second[offset], "mp", pairs)
        bit //= 2
    first = [first[offset] for offset in range(mp_count)]
    second = [second[offset] for offset in range(mp_count)]
    peer_rows = lax.ppermute(own_rows, "seq", xor_pairs(seq_count, 1))

    pair_rows = 2 * rows
    wide = shape((pair_rows, channels), jnp.float32)
    half = shape((pair_rows, channels))
    flip = shape((channels, pair_rows))
    product = 2 * pair_rows * channels * channels
    hidden_one, normed_one, scale_one, hidden_flip, source_flip, head = call(
        functools.partial(first_block_body, mp_count),
        "first_block",
        [smem] + [vmem] * (3 + mp_count),
        (half, wide, wide, flip, flip, shape((SIDE_ROWS, channels))),
        flops=product,
        moved=4 * pair_rows * channels,
    )(where, own_rows, peer_rows, head_weight.T, *first)

    sent_count = seq_count // 2 - 1
    part = (2, depth, width)
    outs = call(
        functools.partial(rest_body, mp_count, classes),
        "rest",
        [smem] + [vmem] * (8 + mp_count),
        (shape(part, jnp.float32),) + (shape(part),) * sent_count + (shape((rows, channels), jnp.float32), shape((rows, channels))),
        scratch=[
            pltpu.VMEM((pair_rows, channels), jnp.float32),
            pltpu.VMEM((pair_rows, channels), jnp.float32),
            pltpu.VMEM((pair_rows, channels), jnp.bfloat16),
            pltpu.VMEM((pair_rows, channels), jnp.float32),
            pltpu.VMEM((pair_rows, channels), jnp.bfloat16),
        ],
        flops=3 * product,
        moved=16 * pair_rows * channels,
    )(where, own_rows, peer_rows, head, hidden_one, normed_one, scale_one, hidden_flip, source_flip, *second)
    own_part, sent, (grad_one, grad_conv) = outs[0], outs[1:-2], outs[-2:]

    received = [
        lax.ppermute(piece, "seq", xor_pairs(seq_count, 2 * (j + 1))) for j, piece in enumerate(sent)
    ]
    whole = shape((tap_count, depth, width), jnp.float32)
    input_grad, first_grad, second_grad = call(
        functools.partial(input_grad_body, mp_count),
        "input_grad",
        [smem] + [vmem] * (2 + mp_count),
        (shape((rows, channels)), whole, whole),
        flops=product // 2,
        moved=8 * rows * channels,
    )(where, grad_one, grad_conv, *first)
    first_grad, second_grad = call(
        functools.partial(total_body, centre_tap),
        "total",
        [anywhere, anywhere] + [vmem] * (1 + sent_count),
        (whole, whole),
        out_specs=(anywhere, anywhere),
        scratch=[pltpu.VMEM(part, jnp.float32), pltpu.SemaphoreType.DMA((2,))],
        aliases={0: 0, 1: 1},
    )(first_grad, second_grad, own_part, *received)
    return (input_grad, first_grad, second_grad)


def power_of_two(count):
    return count & (count - 1) == 0


def local(hidden_entry_states, base_ids, mask_index, first_kernel, second_kernel, head_weight):
    rows, channels = hidden_entry_states.shape
    tap_count, _, width = first_kernel.shape
    seq_count = lax.axis_size("seq")
    mp_count = lax.axis_size("mp")
    first_hops = active_hops(tap_count, DILATION_FIRST1 // rows, seq_count)
    second_hops = active_hops(tap_count, DILATION_SECOND2 // rows, seq_count)
    args = (hidden_entry_states, base_ids, mask_index, first_kernel, second_kernel, head_weight)
    fits = (
        power_of_two(mp_count)
        and power_of_two(seq_count)
        and seq_count > 1
        and width % 128 == 0
        and rows % 128 == 0
        and rows <= channels
        and (channels // seq_count) % 16 == 0
        and head_weight.shape[1] <= SIDE_ROWS
    )
    if len(first_hops) == 1 and len(second_hops) == 1 and fits:
        return local_plan(*args)
    return general_plan(*args, first_hops, second_hops)


def solution(mesh):
    placed = (P("seq", None), P("seq"), P("seq"), P(None, None, "mp"), P(None, None, "mp"), P())
    return jax.shard_map(
        local,
        mesh=mesh,
        in_specs=placed,
        out_specs=(P("seq", None), P(None, "seq", "mp"), P(None, "seq", "mp")),
        check_vma=False,
    )
```

```python
import functools

import jax
import jax.numpy as jnp
from jax import lax
from jax.experimental import pallas as pl
from jax.experimental.pallas import tpu as pltpu
from jax.sharding import PartitionSpec as P

DILATION_FIRST1 = 2048
DILATION_SECOND2 = 4096


epsilon = 1e-05
root_half = 0.7071067811865476
inv_root_two_pi = 0.3989422804014327
ROW_CHUNK = 32
SIDE_ROWS = 16
VMEM_LIMIT = 24 * 1024 * 1024


def gelu_parts(conv_out):
    normal_cdf = 0.5 * (1.0 + lax.erf(conv_out * root_half))
    gelu_slope = normal_cdf + conv_out * inv_root_two_pi * jnp.exp(-0.5 * conv_out * conv_out)
    return (conv_out * normal_cdf, gelu_slope)


def norm_parts(activation):
    values = activation.astype(jnp.float32)
    centre = jnp.mean(values, axis=-1, keepdims=True)
    centred = values - centre
    spread = jnp.mean(centred * centred, axis=-1, keepdims=True)
    inverse = lax.rsqrt(spread + epsilon)
    return (centred * inverse, inverse)


def active_hops(tap_count, dilation_blocks, seq_count):
    centre_tap = tap_count // 2
    hops = [(tap, dilation_blocks * (tap - centre_tap)) for tap in range(tap_count)]
    return [(tap, hop) for tap, hop in hops if abs(hop) < seq_count]


def shifted(x, axis, by):
    if by == 0:
        return x
    peers = lax.axis_size(axis)
    pairs = [(i, i + by) for i in range(peers) if 0 <= i + by < peers]
    return lax.ppermute(x, axis, pairs)


def loss_grad(hidden_top, targets, head_weight):
    logits = lax.dot_general(
        head_weight, hidden_top, (((0,), (1,)), ((), ())), preferred_element_type=jnp.float32
    )
    exponent = jnp.exp(logits)
    probability = exponent / jnp.sum(exponent, axis=0, keepdims=True)
    vocab_rows = lax.broadcasted_iota(jnp.int32, logits.shape, 0)
    onehot = (vocab_rows == targets[None, :]).astype(jnp.float32)
    weight = (targets >= 0).astype(jnp.float32)[None, :]
    dlogits = weight * (probability - onehot)
    return lax.dot_general(
        dlogits,
        head_weight.astype(jnp.float32),
        (((0,), (1,)), ((), ())),
        precision=lax.Precision.HIGHEST,
    )


def general_plan(hidden_entry_states, base_ids, mask_index, first_kernel, second_kernel, head_weight, first_hops, second_hops):
    seq_count = lax.axis_size("seq")
    rows_per_block, channels = hidden_entry_states.shape
    tap_count, _, own_width = first_kernel.shape
    mask_count = mask_index.shape[0]
    offsets = mask_index - lax.axis_index("seq") * rows_per_block
    positions = lax.broadcasted_iota(jnp.int32, (rows_per_block, mask_count), 0)
    masked = jnp.any(positions == offsets[None, :], axis=1)
    targets = jnp.where(masked, base_ids, -1)

    def used(kernel, hops):
        first_tap, last_tap = hops[0][0], hops[-1][0]
        return kernel[first_tap : last_tap + 1]

    def block_forward_pass(source, kernel, hops):
        stacked = jnp.concatenate([shifted(source, "seq", -hop) for _, hop in hops], axis=1)
        conv_out = jnp.dot(
            stacked,
            used(kernel, hops).reshape(len(hops) * channels, own_width),
            preferred_element_type=jnp.float32,
        )
        activation, gelu_slope = gelu_parts(conv_out)
        mixed_all = lax.all_gather(activation.astype(jnp.bfloat16), "mp", axis=1, tiled=True)
        normed, inverse = norm_parts(mixed_all)
        result = (source.astype(jnp.float32) + normed).astype(jnp.bfloat16)
        return (result, (source, normed, inverse, gelu_slope))

    def block_backward_pass(grad_out, saved, kernel, hops):
        source, normed, inverse, gelu_slope = saved
        mean_grad = jnp.mean(grad_out, axis=-1, keepdims=True)
        mean_cross = jnp.mean(grad_out * normed, axis=-1, keepdims=True)
        grad_act = inverse * (grad_out - mean_grad - normed * mean_cross)
        own_cols = lax.dynamic_slice_in_dim(
            grad_act, lax.axis_index("mp") * own_width, own_width, 1
        )
        grad_conv = (own_cols * gelu_slope).astype(jnp.bfloat16)
        tap_stack = jnp.stack([shifted(grad_conv, "seq", hop) for _, hop in hops], axis=0)
        input_part = jnp.einsum(
            "kro,kdo->rd", tap_stack, used(kernel, hops), preferred_element_type=jnp.float32
        )
        grad_in = grad_out + lax.psum(input_part.astype(jnp.bfloat16), "mp").astype(jnp.float32)
        kernel_part = jnp.einsum(
            "rd,kro->kdo", source, tap_stack, preferred_element_type=jnp.float32
        )
        by_owner = kernel_part.reshape(len(hops), seq_count, channels // seq_count, own_width)
        received = lax.all_to_all(
            by_owner.astype(jnp.bfloat16), "seq", split_axis=1, concat_axis=1, tiled=True
        ).astype(by_owner.dtype)
        first_tap, last_tap = hops[0][0], hops[-1][0]
        kernel_grad = jnp.pad(
            jnp.sum(received, axis=1),
            ((first_tap, tap_count - 1 - last_tap), (0, 0), (0, 0)),
        )
        return (grad_in, kernel_grad)

    hidden_one, saved_one = block_forward_pass(hidden_entry_states, first_kernel, first_hops)
    hidden_two, saved_two = block_forward_pass(hidden_one, second_kernel, second_hops)
    grad_two = loss_grad(hidden_two, targets, head_weight)
    grad_one, second_grad = block_backward_pass(grad_two, saved_two, second_kernel, second_hops)
    grad_zero, first_grad = block_backward_pass(grad_one, saved_one, first_kernel, first_hops)
    return (grad_zero.astype(jnp.bfloat16), first_grad, second_grad)


NN = (((1,), (0,)), ((), ()))
NT = (((1,), (1,)), ((), ()))
TN = (((0,), (0,)), ((), ()))


def dot(a, b, dims=NN):
    return lax.dot_general(a, b, dims, preferred_element_type=jnp.float32)


def swap(block, axis, offset):
    return lax.ppermute(block, axis, [(i, i ^ offset) for i in range(lax.axis_size(axis))])


def block_at(me, offset, width):
    return pl.ds(pl.multiple_of((me ^ offset) * width, width), width)


def own_order(me, ref, rows, count):
    width = ref.shape[1] // count
    return jnp.concatenate([ref[rows, block_at(me, o, width)] for o in range(count)], axis=1)


def matrices_body(centre_tap, first_ref, second_ref, both_ref, sems):
    copies = [
        pltpu.make_async_copy(ref.at[centre_tap], both_ref.at[slot], sems.at[slot])
        for slot, ref in enumerate((first_ref, second_ref))
    ]
    for copy in copies:
        copy.start()
    for copy in copies:
        copy.wait()


def rows_body(where_ref, mask_ref, ids_ref, source_ref, rows_ref, mask_at, ids_at, sems):
    rows = source_ref.shape[0]
    copies = [
        pltpu.make_async_copy(mask_ref, mask_at, sems.at[0]),
        pltpu.make_async_copy(ids_ref, ids_at, sems.at[1]),
        pltpu.make_async_copy(source_ref, rows_ref.at[pl.ds(0, rows)], sems.at[2]),
    ]
    for copy in copies:
        copy.start()
    copies[0].wait()
    copies[1].wait()
    positions = lax.broadcasted_iota(jnp.int32, ids_at.shape, 1) + where_ref[1] * rows
    masked = jnp.zeros(ids_at.shape, jnp.int32)
    for entry in range(mask_at.shape[0]):
        masked = jnp.where(positions == mask_at[entry], 1, masked)
    targets = jnp.where(masked == 1, ids_at[...], -1).astype(jnp.float32)
    extra = rows_ref.shape[0] - rows
    rows_ref[rows:, :] = jnp.zeros((extra, rows_ref.shape[1]), jnp.bfloat16)
    rows_ref[rows:, 0:rows] = jnp.broadcast_to(targets, (extra, rows)).astype(jnp.bfloat16)
    copies[2].wait()


def blank_body(first_ref, second_ref):
    first_ref[...] = jnp.zeros_like(first_ref)
    second_ref[...] = jnp.zeros_like(second_ref)


def stacked(blocks, axis):
    return blocks[0] if len(blocks) == 1 else jnp.concatenate(blocks, axis=axis)


def columns_of(me, matrix_refs, slot, count):
    width = matrix_refs[0].shape[2]
    return stacked(
        [
            stacked([ref[slot, block_at(me, o, width), :] for o in range(count)], 0)
            for ref in matrix_refs
        ],
        1,
    )


def early_body(count, where_ref, own_ref, peer_ref, head_ref, *refs):
    matrix_refs = refs[:-4]
    activation_ref, slope_ref, flip_ref, head_out_ref = refs[-4:]
    me = where_ref[0]
    half = activation_ref.shape[0] // 2
    weights = columns_of(me, matrix_refs, 0, count)
    for part, ref in enumerate((own_ref, peer_ref)):
        conv_out = dot(own_order(me, ref, pl.ds(0, half), count), weights)
        for start in range(0, half, ROW_CHUNK):
            rows = pl.ds(part * half + start, ROW_CHUNK)
            activation, gelu_slope = gelu_parts(conv_out[start : start + ROW_CHUNK])
            activation_ref[rows, :] = activation.astype(jnp.bfloat16)
            slope_ref[rows, :] = gelu_slope
        flip_ref[:, pl.ds(part * half, half)] = ref[pl.ds(0, half), :].T
    head_out_ref[...] = jnp.zeros_like(head_out_ref)
    classes = head_ref.shape[0]
    head_out_ref[0:classes, :] = own_order(me, head_ref, pl.ds(0, classes), count)


def main_body(count, sent_count, classes, where_ref, own_ref, peer_ref, activation_ref, slope_ref, source_flip_ref, head_ref, *refs):
    matrix_refs, refs = refs[:count], refs[count:]
    self_ref, sent_refs, refs = refs[0], refs[1 : 1 + sent_count], refs[1 + sent_count :]
    grad_out_ref, grad_conv_out_ref = refs[:2]
    hidden_one_ref, normed_one_ref, scale_one_ref, hidden_flip_ref, normed_two_ref, scale_two_ref, hidden_two_ref, grad_ref, grad_conv_ref = refs[2:]
    me, block = where_ref[0], where_ref[1]
    total_rows = grad_ref.shape[0]
    half = total_rows // 2
    width = self_ref.shape[2]
    depth = self_ref.shape[1]
    halves = (0, half)

    late = columns_of(me, matrix_refs[-1:], 0, count)
    for start, ref in zip(halves, (own_ref, peer_ref)):
        conv_out = dot(own_order(me, ref, pl.ds(0, half), count), late)
        for inner in range(0, half, ROW_CHUNK):
            rows = pl.ds(start + inner, ROW_CHUNK)
            activation, gelu_slope = gelu_parts(conv_out[inner : inner + ROW_CHUNK])
            normed, inverse = norm_parts(
                jnp.concatenate([activation_ref[rows, :], activation.astype(jnp.bfloat16)], axis=1)
            )
            scale_one_ref[rows, :] = jnp.concatenate([slope_ref[rows, :], gelu_slope], axis=1) * inverse
            normed_one_ref[rows, :] = normed
            source = own_order(me, ref, pl.ds(inner, ROW_CHUNK), count)
            hidden_one_ref[rows, :] = (source.astype(jnp.float32) + normed).astype(jnp.bfloat16)

    weights = columns_of(me, matrix_refs, 1, count)
    for start in halves:
        conv_out = dot(hidden_one_ref[pl.ds(start, half), :], weights)
        for inner in range(0, half, ROW_CHUNK):
            rows = pl.ds(start + inner, ROW_CHUNK)
            activation, gelu_slope = gelu_parts(conv_out[inner : inner + ROW_CHUNK])
            normed, inverse = norm_parts(activation.astype(jnp.bfloat16))
            scale_two_ref[rows, :] = gelu_slope * inverse
            normed_two_ref[rows, :] = normed
            hidden_two_ref[rows, :] = (hidden_one_ref[rows, :].astype(jnp.float32) + normed).astype(jnp.bfloat16)

    for offset in range(count):
        flipped = hidden_one_ref[:, pl.ds(offset * width, width)].T
        hidden_flip_ref[block_at(me, offset, width), :] = flipped

    head = head_ref[...]
    logits = dot(head, hidden_two_ref[...], NT)
    class_rows = lax.broadcasted_iota(jnp.int32, logits.shape, 0)
    exponent = jnp.where(class_rows < classes, jnp.exp(logits), 0.0)
    probability = exponent / jnp.sum(exponent, axis=0, keepdims=True)
    targets = jnp.concatenate(
        [ref[half : half + head.shape[0], 0:half] for ref in (own_ref, peer_ref)], axis=1
    ).astype(jnp.float32)
    onehot = (class_rows.astype(jnp.float32) == targets).astype(jnp.float32)
    weight = (targets >= 0.0).astype(jnp.float32)
    rest = jnp.where(class_rows < classes, weight * (probability - onehot), 0.0)
    terms = []
    for _ in range(3):
        term = rest.astype(jnp.bfloat16)
        terms.append(term)
        rest = rest - term.astype(jnp.float32)
    grad_ref[...] = dot(jnp.concatenate(terms, axis=0), jnp.concatenate([head] * 3, axis=0), TN)

    def norm_backward(normed_ref, scale_ref):
        for start in range(0, total_rows, ROW_CHUNK):
            rows = pl.ds(start, ROW_CHUNK)
            grad_out, normed = grad_ref[rows, :], normed_ref[rows, :]
            mean_grad = jnp.mean(grad_out, axis=-1, keepdims=True)
            mean_cross = jnp.mean(grad_out * normed, axis=-1, keepdims=True)
            grad_conv_ref[rows, :] = (
                (grad_out - mean_grad - normed * mean_cross) * scale_ref[rows, :]
            ).astype(jnp.bfloat16)

    def kernel_parts(flip_ref, slot):
        sources = [
            flip_ref[pl.ds(pl.multiple_of((block ^ (2 * j)) * depth, depth), depth), :]
            for j in range(1 + sent_count)
        ]
        part = dot(stacked(sources, 0), grad_conv_ref[:, 0:width])
        self_ref[slot] = part[0:depth]
        for j, ref in enumerate(sent_refs):
            ref[slot] = part[(j + 1) * depth : (j + 2) * depth].astype(jnp.bfloat16)

    norm_backward(normed_two_ref, scale_two_ref)
    for start in halves:
        rows = pl.ds(start, half)
        grad_ref[rows, :] += dot(grad_conv_ref[rows, :], weights, NT)
    kernel_parts(hidden_flip_ref, 1)
    norm_backward(normed_one_ref, scale_one_ref)
    kernel_parts(source_flip_ref, 0)
    grad_out_ref[...] = grad_ref[pl.ds(0, half), :]
    grad_conv_out_ref[...] = grad_conv_ref[pl.ds(0, half), :]


def input_grad_body(count, where_ref, grad_ref, grad_conv_ref, *refs):
    matrix_refs, input_grad_ref = refs[:count], refs[count]
    me = where_ref[0]
    width = matrix_refs[0].shape[2]
    total = grad_ref[...] + dot(grad_conv_ref[...], columns_of(me, matrix_refs, 0, count), NT)
    for offset in range(count):
        input_grad_ref[:, block_at(me, offset, width)] = total[
            :, offset * width : (offset + 1) * width
        ].astype(jnp.bfloat16)


def total_body(centre_tap, first_in_ref, second_in_ref, self_ref, *refs):
    received = refs[:-4]
    first_ref, second_ref, sum_ref, sems = refs[-4:]
    sum_ref[...] = self_ref[...] + sum(ref[...].astype(jnp.float32) for ref in received)
    copies = [
        pltpu.make_async_copy(sum_ref.at[slot], ref.at[centre_tap], sems.at[slot])
        for slot, ref in enumerate((first_ref, second_ref))
    ]
    for copy in copies:
        copy.start()
    for copy in copies:
        copy.wait()


def local_plan(hidden_entry_states, base_ids, mask_index, first_kernel, second_kernel, head_weight):
    seq_count = lax.axis_size("seq")
    mp_count = lax.axis_size("mp")
    rows, channels = hidden_entry_states.shape
    tap_count, _, width = first_kernel.shape
    classes = head_weight.shape[1]
    centre_tap = tap_count // 2
    depth = channels // seq_count
    where = jnp.stack([lax.axis_index("mp"), lax.axis_index("seq")]).astype(jnp.int32)

    vmem = pl.BlockSpec(memory_space=pltpu.VMEM)
    smem = pl.BlockSpec(memory_space=pltpu.SMEM)
    hbm = pl.BlockSpec(memory_space=pltpu.HBM)

    def shape(dims, dtype=jnp.bfloat16):
        return jax.ShapeDtypeStruct(dims, dtype)

    def in_hbm(array):
        return pltpu.with_memory_space_constraint(array, pltpu.HBM)

    def call(body, in_specs, out_shape, out_specs=None, scratch=(), aliases={}, flops=0, moved=0):
        return pl.pallas_call(
            body,
            out_shape=out_shape,
            in_specs=in_specs,
            out_specs=(vmem,) * len(out_shape) if out_specs is None else out_specs,
            scratch_shapes=list(scratch),
            input_output_aliases=aliases,
            compiler_params=pltpu.CompilerParams(vmem_limit_bytes=VMEM_LIMIT),
            cost_estimate=pl.CostEstimate(flops=flops, bytes_accessed=moved, transcendentals=0),
        )

    (own,) = call(
        functools.partial(matrices_body, centre_tap),
        [hbm] * 2,
        (shape((2, channels, width)),),
        scratch=[pltpu.SemaphoreType.DMA((2,))],
    )(in_hbm(first_kernel), in_hbm(second_kernel))
    blocks = {0: own}
    bit = mp_count // 2
    while bit:
        for offset in list(blocks):
            blocks[offset ^ bit] = swap(blocks[offset], "mp", bit)
        bit //= 2
    blocks = [blocks[offset] for offset in range(mp_count)]

    (own_rows,) = call(
        rows_body,
        [smem] + [hbm] * 3,
        (shape((rows + SIDE_ROWS, channels)),),
        scratch=[
            pltpu.SMEM(mask_index.shape, jnp.int32),
            pltpu.VMEM((1, rows), jnp.int32),
            pltpu.SemaphoreType.DMA((3,)),
        ],
    )(where, in_hbm(mask_index), in_hbm(base_ids[None, :]), in_hbm(hidden_entry_states))
    peer_rows = swap(own_rows, "seq", 1)
    whole = shape((tap_count, depth, width), jnp.float32)
    first_grad, second_grad = call(blank_body, [], (whole, whole))()

    pair_rows = 2 * rows
    early = channels - width
    product = 2 * pair_rows * channels * channels
    activation, slope, source_flip, head = call(
        functools.partial(early_body, mp_count),
        [smem] + [vmem] * (2 + mp_count),
        (
            shape((pair_rows, early)),
            shape((pair_rows, early), jnp.float32),
            shape((channels, pair_rows)),
            shape((SIDE_ROWS, channels)),
        ),
        flops=product,
        moved=8 * pair_rows * channels,
    )(where, own_rows, peer_rows, head_weight.T, *blocks[:-1])

    sent_count = seq_count // 2 - 1
    part = (2, depth, width)
    outs = call(
        functools.partial(main_body, mp_count, sent_count, classes),
        [smem] + [vmem] * (6 + mp_count),
        (shape(part, jnp.float32),)
        + (shape(part),) * sent_count
        + (shape((rows, channels), jnp.float32), shape((rows, channels))),
        scratch=[
            pltpu.VMEM((pair_rows, channels), jnp.bfloat16),
            pltpu.VMEM((pair_rows, channels), jnp.float32),
            pltpu.VMEM((pair_rows, channels), jnp.float32),
            pltpu.VMEM((channels, pair_rows), jnp.bfloat16),
            pltpu.VMEM((pair_rows, channels), jnp.float32),
            pltpu.VMEM((pair_rows, channels), jnp.float32),
            pltpu.VMEM((pair_rows, channels), jnp.bfloat16),
            pltpu.VMEM((pair_rows, channels), jnp.float32),
            pltpu.VMEM((pair_rows, channels), jnp.bfloat16),
        ],
        flops=3 * product,
        moved=16 * pair_rows * channels,
    )(where, own_rows, peer_rows, activation, slope, source_flip, head, *blocks)
    own_part, sent, (grad_one, grad_conv) = outs[0], outs[1:-2], outs[-2:]

    received = [swap(piece, "seq", 2 * (j + 1)) for j, piece in enumerate(sent)]
    (input_grad,) = call(
        functools.partial(input_grad_body, mp_count),
        [smem] + [vmem] * (2 + mp_count),
        (shape((rows, channels)),),
        flops=product // 2,
        moved=8 * rows * channels,
    )(where, grad_one, grad_conv, *blocks)
    first_grad, second_grad = call(
        functools.partial(total_body, centre_tap),
        [hbm, hbm] + [vmem] * (1 + sent_count),
        (whole, whole),
        out_specs=(hbm, hbm),
        scratch=[pltpu.VMEM(part, jnp.float32), pltpu.SemaphoreType.DMA((2,))],
        aliases={0: 0, 1: 1},
    )(first_grad, second_grad, own_part, *received)
    return (input_grad, first_grad, second_grad)


def power_of_two(count):
    return count & (count - 1) == 0


def local(hidden_entry_states, base_ids, mask_index, first_kernel, second_kernel, head_weight):
    rows, channels = hidden_entry_states.shape
    tap_count, _, width = first_kernel.shape
    seq_count = lax.axis_size("seq")
    mp_count = lax.axis_size("mp")
    first_hops = active_hops(tap_count, DILATION_FIRST1 // rows, seq_count)
    second_hops = active_hops(tap_count, DILATION_SECOND2 // rows, seq_count)
    args = (hidden_entry_states, base_ids, mask_index, first_kernel, second_kernel, head_weight)
    fits = (
        power_of_two(mp_count)
        and power_of_two(seq_count)
        and mp_count > 1
        and seq_count > 1
        and width % 128 == 0
        and rows % 128 == 0
        and rows <= channels
        and (channels // seq_count) % 16 == 0
        and head_weight.shape[1] <= SIDE_ROWS
    )
    if len(first_hops) == 1 and len(second_hops) == 1 and fits:
        return local_plan(*args)
    return general_plan(*args, first_hops, second_hops)


def solution(mesh):
    placed = (P("seq", None), P("seq"), P("seq"), P(None, None, "mp"), P(None, None, "mp"), P())
    return jax.shard_map(
        local,
        mesh=mesh,
        in_specs=placed,
        out_specs=(P("seq", None), P(None, "seq", "mp"), P(None, "seq", "mp")),
        check_vma=False,
    )
```

```python
import functools

import jax
import jax.numpy as jnp
from jax import lax
from jax.experimental import pallas as pl
from jax.experimental.pallas import tpu as pltpu
from jax.sharding import PartitionSpec as P

DILATION_FIRST1 = 2048
DILATION_SECOND2 = 4096


epsilon = 1e-05
root_half = 0.7071067811865476
inv_root_two_pi = 0.3989422804014327
half_log2_e = -0.7213475204444817
log2_inv_root_two_pi = -1.3257480647361593
SIDE_ROWS = 16
VMEM_LIMIT = 24 * 1024 * 1024


def gelu_parts(conv_out):
    normal_cdf = 0.5 * (1.0 + lax.erf(conv_out * root_half))
    gelu_slope = normal_cdf + conv_out * inv_root_two_pi * jnp.exp(-0.5 * conv_out * conv_out)
    return (conv_out * normal_cdf, gelu_slope)


def norm_parts(activation):
    values = activation.astype(jnp.float32)
    centre = jnp.mean(values, axis=-1, keepdims=True)
    centred = values - centre
    spread = jnp.mean(centred * centred, axis=-1, keepdims=True)
    inverse = lax.rsqrt(spread + epsilon)
    return (centred * inverse, inverse)


def gelu_and_slope(conv_out):
    normal_cdf = 0.5 + 0.5 * lax.erf(conv_out * root_half)
    density = jnp.exp2(conv_out * conv_out * half_log2_e + log2_inv_root_two_pi)
    return (conv_out * normal_cdf, normal_cdf + conv_out * density)


def active_hops(tap_count, dilation_blocks, seq_count):
    centre_tap = tap_count // 2
    hops = [(tap, dilation_blocks * (tap - centre_tap)) for tap in range(tap_count)]
    return [(tap, hop) for tap, hop in hops if abs(hop) < seq_count]


def shifted(x, axis, by):
    if by == 0:
        return x
    peers = lax.axis_size(axis)
    pairs = [(i, i + by) for i in range(peers) if 0 <= i + by < peers]
    return lax.ppermute(x, axis, pairs)


def loss_grad(hidden_top, targets, head_weight):
    logits = lax.dot_general(
        head_weight, hidden_top, (((0,), (1,)), ((), ())), preferred_element_type=jnp.float32
    )
    exponent = jnp.exp(logits)
    probability = exponent / jnp.sum(exponent, axis=0, keepdims=True)
    vocab_rows = lax.broadcasted_iota(jnp.int32, logits.shape, 0)
    onehot = (vocab_rows == targets[None, :]).astype(jnp.float32)
    weight = (targets >= 0).astype(jnp.float32)[None, :]
    dlogits = weight * (probability - onehot)
    return lax.dot_general(
        dlogits,
        head_weight.astype(jnp.float32),
        (((0,), (1,)), ((), ())),
        precision=lax.Precision.HIGHEST,
    )


def general_plan(hidden_entry_states, base_ids, mask_index, first_kernel, second_kernel, head_weight, first_hops, second_hops):
    seq_count = lax.axis_size("seq")
    rows_per_block, channels = hidden_entry_states.shape
    tap_count, _, own_width = first_kernel.shape
    mask_count = mask_index.shape[0]
    offsets = mask_index - lax.axis_index("seq") * rows_per_block
    positions = lax.broadcasted_iota(jnp.int32, (rows_per_block, mask_count), 0)
    masked = jnp.any(positions == offsets[None, :], axis=1)
    targets = jnp.where(masked, base_ids, -1)

    def used(kernel, hops):
        first_tap, last_tap = hops[0][0], hops[-1][0]
        return kernel[first_tap : last_tap + 1]

    def block_forward_pass(source, kernel, hops):
        stacked = jnp.concatenate([shifted(source, "seq", -hop) for _, hop in hops], axis=1)
        conv_out = jnp.dot(
            stacked,
            used(kernel, hops).reshape(len(hops) * channels, own_width),
            preferred_element_type=jnp.float32,
        )
        activation, gelu_slope = gelu_parts(conv_out)
        mixed_all = lax.all_gather(activation.astype(jnp.bfloat16), "mp", axis=1, tiled=True)
        normed, inverse = norm_parts(mixed_all)
        result = (source.astype(jnp.float32) + normed).astype(jnp.bfloat16)
        return (result, (source, normed, inverse, gelu_slope))

    def block_backward_pass(grad_out, saved, kernel, hops):
        source, normed, inverse, gelu_slope = saved
        mean_grad = jnp.mean(grad_out, axis=-1, keepdims=True)
        mean_cross = jnp.mean(grad_out * normed, axis=-1, keepdims=True)
        grad_act = inverse * (grad_out - mean_grad - normed * mean_cross)
        own_cols = lax.dynamic_slice_in_dim(
            grad_act, lax.axis_index("mp") * own_width, own_width, 1
        )
        grad_conv = (own_cols * gelu_slope).astype(jnp.bfloat16)
        tap_stack = jnp.stack([shifted(grad_conv, "seq", hop) for _, hop in hops], axis=0)
        input_part = jnp.einsum(
            "kro,kdo->rd", tap_stack, used(kernel, hops), preferred_element_type=jnp.float32
        )
        grad_in = grad_out + lax.psum(input_part.astype(jnp.bfloat16), "mp").astype(jnp.float32)
        kernel_part = jnp.einsum(
            "rd,kro->kdo", source, tap_stack, preferred_element_type=jnp.float32
        )
        by_owner = kernel_part.reshape(len(hops), seq_count, channels // seq_count, own_width)
        received = lax.all_to_all(
            by_owner.astype(jnp.bfloat16), "seq", split_axis=1, concat_axis=1, tiled=True
        ).astype(by_owner.dtype)
        first_tap, last_tap = hops[0][0], hops[-1][0]
        kernel_grad = jnp.pad(
            jnp.sum(received, axis=1),
            ((first_tap, tap_count - 1 - last_tap), (0, 0), (0, 0)),
        )
        return (grad_in, kernel_grad)

    hidden_one, saved_one = block_forward_pass(hidden_entry_states, first_kernel, first_hops)
    hidden_two, saved_two = block_forward_pass(hidden_one, second_kernel, second_hops)
    grad_two = loss_grad(hidden_two, targets, head_weight)
    grad_one, second_grad = block_backward_pass(grad_two, saved_two, second_kernel, second_hops)
    grad_zero, first_grad = block_backward_pass(grad_one, saved_one, first_kernel, first_hops)
    return (grad_zero.astype(jnp.bfloat16), first_grad, second_grad)


NN = (((1,), (0,)), ((), ()))
NT = (((1,), (1,)), ((), ()))
TN = (((0,), (0,)), ((), ()))


def dot(a, b, dims=NN):
    return lax.dot_general(a, b, dims, preferred_element_type=jnp.float32)


def swap(block, axis, offset):
    return lax.ppermute(block, axis, [(i, i ^ offset) for i in range(lax.axis_size(axis))])


def turn_pairs(block, axis, turn):
    count = lax.axis_size(axis)
    return lax.ppermute(block, axis, [(i, (i + 2 * turn) % count) for i in range(count)])


def block_at(me, offset, width):
    return pl.ds(pl.multiple_of((me ^ offset) * width, width), width)


def own_order(me, ref, rows, count):
    width = ref.shape[1] // count
    return jnp.concatenate([ref[rows, block_at(me, o, width)] for o in range(count)], axis=1)


def matrices_body(centre_tap, first_ref, second_ref, both_ref, sems):
    copies = [
        pltpu.make_async_copy(ref.at[centre_tap], both_ref.at[slot], sems.at[slot])
        for slot, ref in enumerate((first_ref, second_ref))
    ]
    for copy in copies:
        copy.start()
    for copy in copies:
        copy.wait()


def targets_body(where_ref, mask_ref, ids_ref, targets_ref, mask_at, ids_at, sems):
    copies = [
        pltpu.make_async_copy(mask_ref, mask_at, sems.at[0]),
        pltpu.make_async_copy(ids_ref, ids_at, sems.at[1]),
    ]
    for copy in copies:
        copy.start()
    for copy in copies:
        copy.wait()
    positions = lax.broadcasted_iota(jnp.int32, ids_at.shape, 1) + where_ref[1] * ids_at.shape[1]
    masked = jnp.zeros(ids_at.shape, jnp.int32)
    for entry in range(mask_at.shape[0]):
        masked = jnp.where(positions == mask_at[entry], 1, masked)
    targets = jnp.where(masked == 1, ids_at[...], -1).astype(jnp.float32)
    targets_ref[...] = jnp.broadcast_to(targets, targets_ref.shape).astype(jnp.bfloat16)


def blank_body(first_ref, second_ref):
    first_ref[...] = jnp.zeros_like(first_ref)
    second_ref[...] = jnp.zeros_like(second_ref)


def stacked(blocks, axis):
    return blocks[0] if len(blocks) == 1 else jnp.concatenate(blocks, axis=axis)


def columns_of(me, matrix_refs, slot, count):
    width = matrix_refs[0].shape[2]
    return stacked(
        [
            stacked([ref[slot, block_at(me, o, width), :] for o in range(count)], 0)
            for ref in matrix_refs
        ],
        1,
    )


def early_body(count, where_ref, own_ref, peer_ref, head_ref, *refs):
    matrix_refs = refs[:-4]
    activation_ref, slope_ref, flip_ref, head_out_ref = refs[-4:]
    me = where_ref[0]
    half = own_ref.shape[0]
    weights = columns_of(me, matrix_refs, 0, count)
    for part, ref in enumerate((own_ref, peer_ref)):
        rows = pl.ds(part * half, half)
        conv_out = dot(own_order(me, ref, pl.ds(0, half), count), weights)
        activation_ref[rows, :], slope_ref[rows, :] = gelu_and_slope(conv_out)
        flip_ref[:, rows] = ref[...].T
    head_out_ref[...] = jnp.zeros_like(head_out_ref)
    classes = head_ref.shape[0]
    head_out_ref[0:classes, :] = own_order(me, head_ref, pl.ds(0, classes), count)


def owner_of(block, blocks, turn):
    return lax.rem(lax.div(block, 2) + turn, blocks // 2) * 2 + lax.rem(block, 2)


def main_body(count, blocks, classes, where_ref, own_ref, peer_ref, own_targets_ref, peer_targets_ref, activation_ref, slope_ref, source_flip_ref, head_ref, *refs):
    turns = blocks // 2
    matrix_refs, refs = refs[:count], refs[count:]
    self_ref, sent_refs, refs = refs[0], refs[1:turns], refs[turns:]
    grad_out_ref, grad_conv_out_ref = refs[:2]
    hidden_one_ref, normed_one_ref, scale_one_ref, hidden_flip_ref, normed_two_ref, scale_two_ref, hidden_two_ref, grad_ref, grad_conv_ref = refs[2:]
    me, block = where_ref[0], where_ref[1]
    half = own_ref.shape[0]
    _, depth, width = self_ref.shape
    source_refs = (own_ref, peer_ref)
    target_refs = (own_targets_ref, peer_targets_ref)
    late = columns_of(me, matrix_refs[-1:], 0, count)
    weights = columns_of(me, matrix_refs, 1, count)
    head = head_ref[...]

    def first_block(part):
        rows = pl.ds(part * half, half)
        source = own_order(me, source_refs[part], pl.ds(0, half), count)
        activation, gelu_slope = gelu_and_slope(dot(source, late))
        normed, inverse = norm_parts(jnp.concatenate([activation_ref[rows, :], activation], axis=1))
        scale_one_ref[rows, :] = jnp.concatenate([slope_ref[rows, :], gelu_slope], axis=1) * inverse
        normed_one_ref[rows, :] = normed
        hidden_one_ref[rows, :] = (source.astype(jnp.float32) + normed).astype(jnp.bfloat16)

    def second_block(part):
        rows = pl.ds(part * half, half)
        source = hidden_one_ref[rows, :]
        activation, gelu_slope = gelu_and_slope(dot(source, weights))
        normed, inverse = norm_parts(activation)
        scale_two_ref[rows, :] = gelu_slope * inverse
        normed_two_ref[rows, :] = normed
        hidden_two_ref[rows, :] = (source.astype(jnp.float32) + normed).astype(jnp.bfloat16)

    def flip_hidden(part):
        rows = pl.ds(part * half, half)
        for offset in range(count):
            flipped = hidden_one_ref[rows, pl.ds(offset * width, width)].T
            hidden_flip_ref[block_at(me, offset, width), rows] = flipped

    def loss_backward(part):
        rows = pl.ds(part * half, half)
        logits = dot(head, hidden_two_ref[rows, :], NT)
        class_rows = lax.broadcasted_iota(jnp.int32, logits.shape, 0)
        exponent = jnp.where(class_rows < classes, jnp.exp(logits), 0.0)
        probability = exponent / jnp.sum(exponent, axis=0, keepdims=True)
        targets = target_refs[part][...].astype(jnp.float32)
        onehot = (class_rows.astype(jnp.float32) == targets).astype(jnp.float32)
        weight = (targets >= 0.0).astype(jnp.float32)
        rest = jnp.where(class_rows < classes, weight * (probability - onehot), 0.0)
        terms = []
        for _ in range(3):
            term = rest.astype(jnp.bfloat16)
            terms.append(term)
            rest = rest - term.astype(jnp.float32)
        grad_ref[rows, :] = dot(jnp.concatenate(terms, axis=0), jnp.concatenate([head] * 3, axis=0), TN)

    def norm_backward(part, normed_ref, scale_ref):
        rows = pl.ds(part * half, half)
        grad_out, normed = grad_ref[rows, :], normed_ref[rows, :]
        mean_grad = jnp.mean(grad_out, axis=-1, keepdims=True)
        mean_cross = jnp.mean(grad_out * normed, axis=-1, keepdims=True)
        grad_conv_ref[rows, :] = (
            (grad_out - mean_grad - normed * mean_cross) * scale_ref[rows, :]
        ).astype(jnp.bfloat16)

    def input_backward(part):
        rows = pl.ds(part * half, half)
        grad_ref[rows, :] += dot(grad_conv_ref[rows, :], weights, NT)

    def kernel_parts(flip_ref, slot):
        sources = [
            flip_ref[pl.ds(pl.multiple_of(owner_of(block, blocks, turn) * depth, depth), depth), :]
            for turn in range(turns)
        ]
        part = dot(stacked(sources, 0), grad_conv_ref[:, 0:width])
        self_ref[slot] = part[0:depth]
        for turn, ref in enumerate(sent_refs, 1):
            ref[slot] = part[turn * depth : (turn + 1) * depth].astype(jnp.bfloat16)

    first_block(0)
    first_block(1)
    second_block(0)
    second_block(1)
    loss_backward(0)
    norm_backward(0, normed_two_ref, scale_two_ref)
    loss_backward(1)
    norm_backward(1, normed_two_ref, scale_two_ref)
    input_backward(0)
    input_backward(1)
    flip_hidden(0)
    flip_hidden(1)
    kernel_parts(hidden_flip_ref, 1)
    norm_backward(0, normed_one_ref, scale_one_ref)
    norm_backward(1, normed_one_ref, scale_one_ref)
    kernel_parts(source_flip_ref, 0)
    grad_out_ref[...] = grad_ref[pl.ds(0, half), :]
    grad_conv_out_ref[...] = grad_conv_ref[pl.ds(0, half), :]


def input_grad_body(count, where_ref, grad_ref, grad_conv_ref, *refs):
    matrix_refs, input_grad_ref = refs[:count], refs[count]
    me = where_ref[0]
    width = matrix_refs[0].shape[2]
    total = grad_ref[...] + dot(grad_conv_ref[...], columns_of(me, matrix_refs, 0, count), NT)
    for offset in range(count):
        input_grad_ref[:, block_at(me, offset, width)] = total[
            :, offset * width : (offset + 1) * width
        ].astype(jnp.bfloat16)


def total_body(centre_tap, first_in_ref, second_in_ref, input_grad_ref, self_ref, *refs):
    received = refs[:-5]
    first_ref, second_ref, grad_out_ref, sum_ref, sems = refs[-5:]
    copies = [pltpu.make_async_copy(input_grad_ref, grad_out_ref, sems.at[2])]
    copies[0].start()
    sum_ref[...] = self_ref[...] + sum(ref[...].astype(jnp.float32) for ref in received)
    for slot, ref in enumerate((first_ref, second_ref)):
        copies.append(pltpu.make_async_copy(sum_ref.at[slot], ref.at[centre_tap], sems.at[slot]))
        copies[-1].start()
    for copy in copies:
        copy.wait()


def local_plan(hidden_entry_states, base_ids, mask_index, first_kernel, second_kernel, head_weight):
    seq_count = lax.axis_size("seq")
    mp_count = lax.axis_size("mp")
    rows, channels = hidden_entry_states.shape
    tap_count, _, width = first_kernel.shape
    classes = head_weight.shape[1]
    centre_tap = tap_count // 2
    depth = channels // seq_count
    where = jnp.stack([lax.axis_index("mp"), lax.axis_index("seq")]).astype(jnp.int32)

    vmem = pl.BlockSpec(memory_space=pltpu.VMEM)
    smem = pl.BlockSpec(memory_space=pltpu.SMEM)
    hbm = pl.BlockSpec(memory_space=pltpu.HBM)

    def shape(dims, dtype=jnp.bfloat16):
        return jax.ShapeDtypeStruct(dims, dtype)

    def in_hbm(array):
        return pltpu.with_memory_space_constraint(array, pltpu.HBM)

    def call(body, in_specs, out_shape, out_specs=None, scratch=(), aliases={}, flops=0, moved=0):
        return pl.pallas_call(
            body,
            out_shape=out_shape,
            in_specs=in_specs,
            out_specs=(vmem,) * len(out_shape) if out_specs is None else out_specs,
            scratch_shapes=list(scratch),
            input_output_aliases=aliases,
            compiler_params=pltpu.CompilerParams(vmem_limit_bytes=VMEM_LIMIT),
            cost_estimate=pl.CostEstimate(flops=flops, bytes_accessed=moved, transcendentals=0),
        )

    (own,) = call(
        functools.partial(matrices_body, centre_tap),
        [hbm] * 2,
        (shape((2, channels, width)),),
        scratch=[pltpu.SemaphoreType.DMA((2,))],
    )(in_hbm(first_kernel), in_hbm(second_kernel))
    blocks = {0: own}
    bit = mp_count // 2
    while bit:
        for offset in list(blocks):
            blocks[offset ^ bit] = swap(blocks[offset], "mp", bit)
        bit //= 2
    blocks = [blocks[offset] for offset in range(mp_count)]

    peer_rows = swap(hidden_entry_states, "seq", 1)
    (own_targets,) = call(
        targets_body,
        [smem] + [hbm] * 2,
        (shape((SIDE_ROWS, rows)),),
        scratch=[
            pltpu.SMEM(mask_index.shape, jnp.int32),
            pltpu.VMEM((1, rows), jnp.int32),
            pltpu.SemaphoreType.DMA((2,)),
        ],
    )(where, in_hbm(mask_index), in_hbm(base_ids[None, :]))
    peer_targets = swap(own_targets, "seq", 1)
    whole = shape((tap_count, depth, width), jnp.float32)
    first_grad, second_grad = call(blank_body, [], (whole, whole))()

    pair_rows = 2 * rows
    early = channels - width
    product = 2 * pair_rows * channels * channels
    activation, slope, source_flip, head = call(
        functools.partial(early_body, mp_count),
        [smem] + [vmem] * (2 + mp_count),
        (
            shape((pair_rows, early), jnp.float32),
            shape((pair_rows, early), jnp.float32),
            shape((channels, pair_rows)),
            shape((SIDE_ROWS, channels)),
        ),
        flops=product,
        moved=8 * pair_rows * channels,
    )(where, hidden_entry_states, peer_rows, head_weight.T, *blocks[:-1])

    turns = seq_count // 2
    part = (2, depth, width)
    outs = call(
        functools.partial(main_body, mp_count, seq_count, classes),
        [smem] + [vmem] * (8 + mp_count),
        (shape(part, jnp.float32),)
        + (shape(part),) * (turns - 1)
        + (shape((rows, channels), jnp.float32), shape((rows, channels))),
        scratch=[
            pltpu.VMEM((pair_rows, channels), jnp.bfloat16),
            pltpu.VMEM((pair_rows, channels), jnp.float32),
            pltpu.VMEM((pair_rows, channels), jnp.float32),
            pltpu.VMEM((channels, pair_rows), jnp.bfloat16),
            pltpu.VMEM((pair_rows, channels), jnp.float32),
            pltpu.VMEM((pair_rows, channels), jnp.float32),
            pltpu.VMEM((pair_rows, channels), jnp.bfloat16),
            pltpu.VMEM((pair_rows, channels), jnp.float32),
            pltpu.VMEM((pair_rows, channels), jnp.bfloat16),
        ],
        flops=3 * product,
        moved=16 * pair_rows * channels,
    )(where, hidden_entry_states, peer_rows, own_targets, peer_targets, activation, slope, source_flip, head, *blocks)
    own_part, sent, (grad_one, grad_conv) = outs[0], outs[1:-2], outs[-2:]

    received = [turn_pairs(piece, "seq", turn) for turn, piece in enumerate(sent, 1)]
    (input_grad,) = call(
        functools.partial(input_grad_body, mp_count),
        [smem] + [vmem] * (2 + mp_count),
        (shape((rows, channels)),),
        flops=product // 2,
        moved=8 * rows * channels,
    )(where, grad_one, grad_conv, *blocks)
    first_grad, second_grad, input_grad = call(
        functools.partial(total_body, centre_tap),
        [hbm, hbm] + [vmem] * (1 + turns),
        (whole, whole, shape((rows, channels))),
        out_specs=(hbm,) * 3,
        scratch=[pltpu.VMEM(part, jnp.float32), pltpu.SemaphoreType.DMA((3,))],
        aliases={0: 0, 1: 1},
    )(first_grad, second_grad, input_grad, own_part, *received)
    return (input_grad, first_grad, second_grad)


def power_of_two(count):
    return count & (count - 1) == 0


def local(hidden_entry_states, base_ids, mask_index, first_kernel, second_kernel, head_weight):
    rows, channels = hidden_entry_states.shape
    tap_count, _, width = first_kernel.shape
    seq_count = lax.axis_size("seq")
    mp_count = lax.axis_size("mp")
    first_hops = active_hops(tap_count, DILATION_FIRST1 // rows, seq_count)
    second_hops = active_hops(tap_count, DILATION_SECOND2 // rows, seq_count)
    args = (hidden_entry_states, base_ids, mask_index, first_kernel, second_kernel, head_weight)
    fits = (
        power_of_two(mp_count)
        and power_of_two(seq_count)
        and mp_count > 1
        and seq_count > 1
        and width % 128 == 0
        and rows % 128 == 0
        and rows <= channels
        and (channels // seq_count) % 16 == 0
        and head_weight.shape[1] <= SIDE_ROWS
    )
    if len(first_hops) == 1 and len(second_hops) == 1 and fits:
        return local_plan(*args)
    return general_plan(*args, first_hops, second_hops)


def solution(mesh):
    placed = (P("seq", None), P("seq"), P("seq"), P(None, None, "mp"), P(None, None, "mp"), P())
    return jax.shard_map(
        local,
        mesh=mesh,
        in_specs=placed,
        out_specs=(P("seq", None), P(None, "seq", "mp"), P(None, "seq", "mp")),
        check_vma=False,
    )
```

```python
import functools

import jax
import jax.numpy as jnp
from jax import lax
from jax.experimental import pallas as pl
from jax.experimental.pallas import tpu as pltpu
from jax.sharding import PartitionSpec as P

DILATION_FIRST1 = 2048
DILATION_SECOND2 = 4096


epsilon = 1e-05
root_half = 0.7071067811865476
inv_root_two_pi = 0.3989422804014327
half_log2_e = -0.7213475204444817
log2_inv_root_two_pi = -1.3257480647361593
SIDE_ROWS = 16
VMEM_LIMIT = 24 * 1024 * 1024


def gelu_parts(conv_out):
    normal_cdf = 0.5 * (1.0 + lax.erf(conv_out * root_half))
    gelu_slope = normal_cdf + conv_out * inv_root_two_pi * jnp.exp(-0.5 * conv_out * conv_out)
    return (conv_out * normal_cdf, gelu_slope)


def norm_parts(activation):
    values = activation.astype(jnp.float32)
    centre = jnp.mean(values, axis=-1, keepdims=True)
    centred = values - centre
    spread = jnp.mean(centred * centred, axis=-1, keepdims=True)
    inverse = lax.rsqrt(spread + epsilon)
    return (centred * inverse, inverse)


def gelu_and_slope(conv_out):
    normal_cdf = 0.5 + 0.5 * lax.erf(conv_out * root_half)
    density = jnp.exp2(conv_out * conv_out * half_log2_e + log2_inv_root_two_pi)
    return (conv_out * normal_cdf, normal_cdf + conv_out * density)


def active_hops(tap_count, dilation_blocks, seq_count):
    centre_tap = tap_count // 2
    hops = [(tap, dilation_blocks * (tap - centre_tap)) for tap in range(tap_count)]
    return [(tap, hop) for tap, hop in hops if abs(hop) < seq_count]


def shifted(x, axis, by):
    if by == 0:
        return x
    peers = lax.axis_size(axis)
    pairs = [(i, i + by) for i in range(peers) if 0 <= i + by < peers]
    return lax.ppermute(x, axis, pairs)


def loss_grad(hidden_top, targets, head_weight):
    logits = lax.dot_general(
        head_weight, hidden_top, (((0,), (1,)), ((), ())), preferred_element_type=jnp.float32
    )
    exponent = jnp.exp(logits)
    probability = exponent / jnp.sum(exponent, axis=0, keepdims=True)
    vocab_rows = lax.broadcasted_iota(jnp.int32, logits.shape, 0)
    onehot = (vocab_rows == targets[None, :]).astype(jnp.float32)
    weight = (targets >= 0).astype(jnp.float32)[None, :]
    dlogits = weight * (probability - onehot)
    return lax.dot_general(
        dlogits,
        head_weight.astype(jnp.float32),
        (((0,), (1,)), ((), ())),
        precision=lax.Precision.HIGHEST,
    )


def general_plan(hidden_entry_states, base_ids, mask_index, first_kernel, second_kernel, head_weight, first_hops, second_hops):
    seq_count = lax.axis_size("seq")
    rows_per_block, channels = hidden_entry_states.shape
    tap_count, _, own_width = first_kernel.shape
    mask_count = mask_index.shape[0]
    offsets = mask_index - lax.axis_index("seq") * rows_per_block
    positions = lax.broadcasted_iota(jnp.int32, (rows_per_block, mask_count), 0)
    masked = jnp.any(positions == offsets[None, :], axis=1)
    targets = jnp.where(masked, base_ids, -1)

    def used(kernel, hops):
        first_tap, last_tap = hops[0][0], hops[-1][0]
        return kernel[first_tap : last_tap + 1]

    def block_forward_pass(source, kernel, hops):
        stacked = jnp.concatenate([shifted(source, "seq", -hop) for _, hop in hops], axis=1)
        conv_out = jnp.dot(
            stacked,
            used(kernel, hops).reshape(len(hops) * channels, own_width),
            preferred_element_type=jnp.float32,
        )
        activation, gelu_slope = gelu_parts(conv_out)
        mixed_all = lax.all_gather(activation.astype(jnp.bfloat16), "mp", axis=1, tiled=True)
        normed, inverse = norm_parts(mixed_all)
        result = (source.astype(jnp.float32) + normed).astype(jnp.bfloat16)
        return (result, (source, normed, inverse, gelu_slope))

    def block_backward_pass(grad_out, saved, kernel, hops):
        source, normed, inverse, gelu_slope = saved
        mean_grad = jnp.mean(grad_out, axis=-1, keepdims=True)
        mean_cross = jnp.mean(grad_out * normed, axis=-1, keepdims=True)
        grad_act = inverse * (grad_out - mean_grad - normed * mean_cross)
        own_cols = lax.dynamic_slice_in_dim(
            grad_act, lax.axis_index("mp") * own_width, own_width, 1
        )
        grad_conv = (own_cols * gelu_slope).astype(jnp.bfloat16)
        tap_stack = jnp.stack([shifted(grad_conv, "seq", hop) for _, hop in hops], axis=0)
        input_part = jnp.einsum(
            "kro,kdo->rd", tap_stack, used(kernel, hops), preferred_element_type=jnp.float32
        )
        grad_in = grad_out + lax.psum(input_part.astype(jnp.bfloat16), "mp").astype(jnp.float32)
        kernel_part = jnp.einsum(
            "rd,kro->kdo", source, tap_stack, preferred_element_type=jnp.float32
        )
        by_owner = kernel_part.reshape(len(hops), seq_count, channels // seq_count, own_width)
        received = lax.all_to_all(
            by_owner.astype(jnp.bfloat16), "seq", split_axis=1, concat_axis=1, tiled=True
        ).astype(by_owner.dtype)
        first_tap, last_tap = hops[0][0], hops[-1][0]
        kernel_grad = jnp.pad(
            jnp.sum(received, axis=1),
            ((first_tap, tap_count - 1 - last_tap), (0, 0), (0, 0)),
        )
        return (grad_in, kernel_grad)

    hidden_one, saved_one = block_forward_pass(hidden_entry_states, first_kernel, first_hops)
    hidden_two, saved_two = block_forward_pass(hidden_one, second_kernel, second_hops)
    grad_two = loss_grad(hidden_two, targets, head_weight)
    grad_one, second_grad = block_backward_pass(grad_two, saved_two, second_kernel, second_hops)
    grad_zero, first_grad = block_backward_pass(grad_one, saved_one, first_kernel, first_hops)
    return (grad_zero.astype(jnp.bfloat16), first_grad, second_grad)


NN = (((1,), (0,)), ((), ()))
NT = (((1,), (1,)), ((), ()))
TN = (((0,), (0,)), ((), ()))


def dot(a, b, dims=NN):
    return lax.dot_general(a, b, dims, preferred_element_type=jnp.float32)


def swap(block, axis, offset):
    return lax.ppermute(block, axis, [(i, i ^ offset) for i in range(lax.axis_size(axis))])


def block_at(me, offset, width):
    return pl.ds(pl.multiple_of((me ^ offset) * width, width), width)


def stacked(blocks, axis):
    return blocks[0] if len(blocks) == 1 else jnp.concatenate(blocks, axis=axis)


def own_order(me, refs, count):
    width = refs[0].shape[1] // count
    return stacked(
        [stacked([ref[:, block_at(me, o, width)] for o in range(count)], 1) for ref in refs], 0
    )


def first_copies_body(centre_tap, where_ref, first_ref, second_ref, source_ref, both_ref, share_ref, sems):
    share = share_ref.shape[0]
    start = pl.multiple_of(lax.rem(where_ref[0], 2) * share, share)
    copies = [
        pltpu.make_async_copy(first_ref.at[centre_tap], both_ref.at[0], sems.at[0]),
        pltpu.make_async_copy(second_ref.at[centre_tap], both_ref.at[1], sems.at[1]),
        pltpu.make_async_copy(source_ref.at[pl.ds(start, share)], share_ref, sems.at[2]),
    ]
    for copy in copies:
        copy.start()
    for copy in copies:
        copy.wait()


def targets_body(where_ref, mask_ref, ids_ref, own_ref, sent_ref, mask_at, ids_at, sems):
    copies = [
        pltpu.make_async_copy(mask_ref, mask_at, sems.at[0]),
        pltpu.make_async_copy(ids_ref, ids_at, sems.at[1]),
    ]
    for copy in copies:
        copy.start()
    for copy in copies:
        copy.wait()
    rows = ids_at.shape[1]
    positions = lax.broadcasted_iota(jnp.int32, ids_at.shape, 1) + where_ref[1] * rows
    masked = jnp.zeros(ids_at.shape, jnp.int32)
    for entry in range(mask_at.shape[0]):
        masked = jnp.where(positions == mask_at[entry], 1, masked)
    targets = jnp.where(masked == 1, ids_at[...], -1).astype(jnp.float32)
    targets = jnp.broadcast_to(targets, own_ref.shape)
    turned = pltpu.roll(targets, rows // 2, 1)
    own_ref[...] = targets.astype(jnp.bfloat16)
    sent_ref[...] = jnp.where(lax.rem(where_ref[0], 2) == 1, turned, targets).astype(jnp.bfloat16)


def blank_body(first_ref, second_ref):
    first_ref[...] = jnp.zeros_like(first_ref)
    second_ref[...] = jnp.zeros_like(second_ref)


def columns_of(me, matrix_refs, slot, count):
    width = matrix_refs[0].shape[2]
    return stacked(
        [
            stacked([ref[slot, block_at(me, o, width), :] for o in range(count)], 0)
            for ref in matrix_refs
        ],
        1,
    )


def early_body(count, where_ref, own_ref, far_ref, near_ref, head_ref, *refs):
    matrix_refs = refs[:-4]
    activation_ref, slope_ref, flip_ref, head_out_ref = refs[-4:]
    me = where_ref[0]
    half = own_ref.shape[0]
    weights = columns_of(me, matrix_refs, 0, count)
    for part, source_refs in enumerate(((own_ref,), (far_ref, near_ref))):
        rows = pl.ds(part * half, half)
        conv_out = dot(own_order(me, source_refs, count), weights)
        activation_ref[rows, :], slope_ref[rows, :] = gelu_and_slope(conv_out)
        flip_ref[:, rows] = stacked([ref[...] for ref in source_refs], 0).T
    head_out_ref[...] = jnp.zeros_like(head_out_ref)
    classes = head_ref.shape[0]
    head_out_ref[0:classes, :] = own_order(me, (head_ref,), count)


def main_body(count, blocks, classes, where_ref, own_ref, far_ref, near_ref, own_targets_ref, peer_targets_ref, activation_ref, slope_ref, source_flip_ref, head_ref, *refs):
    turns = blocks // 2
    matrix_refs, refs = refs[:count], refs[count:]
    self_ref, sent_refs, refs = refs[0], refs[1:turns], refs[turns:]
    grad_out_ref, grad_conv_out_ref = refs[:2]
    hidden_one_ref, normed_one_ref, scale_one_ref, hidden_flip_ref, normed_two_ref, scale_two_ref, hidden_two_ref, grad_ref, grad_conv_ref = refs[2:]
    me, block = where_ref[0], where_ref[1]
    half = own_ref.shape[0]
    _, depth, width = self_ref.shape
    source_refs = ((own_ref,), (far_ref, near_ref))
    target_refs = (own_targets_ref, peer_targets_ref)
    late = columns_of(me, matrix_refs[-1:], 0, count)
    weights = columns_of(me, matrix_refs, 1, count)
    head = head_ref[...]

    def first_block(part):
        rows = pl.ds(part * half, half)
        source = own_order(me, source_refs[part], count)
        activation, gelu_slope = gelu_and_slope(dot(source, late))
        normed, inverse = norm_parts(jnp.concatenate([activation_ref[rows, :], activation], axis=1))
        scale_one_ref[rows, :] = jnp.concatenate([slope_ref[rows, :], gelu_slope], axis=1) * inverse
        normed_one_ref[rows, :] = normed
        hidden_one_ref[rows, :] = (source.astype(jnp.float32) + normed).astype(jnp.bfloat16)

    def second_block(part):
        rows = pl.ds(part * half, half)
        source = hidden_one_ref[rows, :]
        activation, gelu_slope = gelu_and_slope(dot(source, weights))
        normed, inverse = norm_parts(activation)
        scale_two_ref[rows, :] = gelu_slope * inverse
        normed_two_ref[rows, :] = normed
        hidden_two_ref[rows, :] = (source.astype(jnp.float32) + normed).astype(jnp.bfloat16)

    def flip_hidden(part):
        rows = pl.ds(part * half, half)
        for offset in range(count):
            flipped = hidden_one_ref[rows, pl.ds(offset * width, width)].T
            hidden_flip_ref[block_at(me, offset, width), rows] = flipped

    def loss_backward(part):
        rows = pl.ds(part * half, half)
        logits = dot(head, hidden_two_ref[rows, :], NT)
        class_rows = lax.broadcasted_iota(jnp.int32, logits.shape, 0)
        exponent = jnp.where(class_rows < classes, jnp.exp(logits), 0.0)
        probability = exponent / jnp.sum(exponent, axis=0, keepdims=True)
        targets = target_refs[part][...].astype(jnp.float32)
        onehot = (class_rows.astype(jnp.float32) == targets).astype(jnp.float32)
        weight = (targets >= 0.0).astype(jnp.float32)
        rest = jnp.where(class_rows < classes, weight * (probability - onehot), 0.0)
        terms = []
        for _ in range(3):
            term = rest.astype(jnp.bfloat16)
            terms.append(term)
            rest = rest - term.astype(jnp.float32)
        grad_ref[rows, :] = dot(jnp.concatenate(terms, axis=0), jnp.concatenate([head] * 3, axis=0), TN)

    def norm_backward(part, normed_ref, scale_ref):
        rows = pl.ds(part * half, half)
        grad_out, normed = grad_ref[rows, :], normed_ref[rows, :]
        mean_grad = jnp.mean(grad_out, axis=-1, keepdims=True)
        mean_cross = jnp.mean(grad_out * normed, axis=-1, keepdims=True)
        grad_conv_ref[rows, :] = (
            (grad_out - mean_grad - normed * mean_cross) * scale_ref[rows, :]
        ).astype(jnp.bfloat16)

    def input_backward(part):
        rows = pl.ds(part * half, half)
        grad_ref[rows, :] += dot(grad_conv_ref[rows, :], weights, NT)

    def kernel_parts(flip_ref, slot):
        sources = [
            flip_ref[pl.ds(pl.multiple_of((block ^ turn) * depth, depth), depth), :]
            for turn in range(turns)
        ]
        part = dot(stacked(sources, 0), grad_conv_ref[:, 0:width])
        self_ref[slot] = part[0:depth]
        for turn, ref in enumerate(sent_refs, 1):
            ref[slot] = part[turn * depth : (turn + 1) * depth].astype(jnp.bfloat16)

    first_block(0)
    first_block(1)
    second_block(0)
    second_block(1)
    loss_backward(0)
    norm_backward(0, normed_two_ref, scale_two_ref)
    loss_backward(1)
    norm_backward(1, normed_two_ref, scale_two_ref)
    input_backward(0)
    input_backward(1)
    flip_hidden(0)
    flip_hidden(1)
    kernel_parts(hidden_flip_ref, 1)
    norm_backward(0, normed_one_ref, scale_one_ref)
    norm_backward(1, normed_one_ref, scale_one_ref)
    kernel_parts(source_flip_ref, 0)
    grad_out_ref[...] = grad_ref[pl.ds(0, half), :]
    grad_conv_out_ref[...] = grad_conv_ref[pl.ds(0, half), :]


def input_grad_body(count, where_ref, grad_ref, grad_conv_ref, *refs):
    matrix_refs, input_grad_ref = refs[:count], refs[count]
    me = where_ref[0]
    width = matrix_refs[0].shape[2]
    total = grad_ref[...] + dot(grad_conv_ref[...], columns_of(me, matrix_refs, 0, count), NT)
    for offset in range(count):
        input_grad_ref[:, block_at(me, offset, width)] = total[
            :, offset * width : (offset + 1) * width
        ].astype(jnp.bfloat16)


def total_body(centre_tap, first_in_ref, second_in_ref, input_grad_ref, self_ref, *refs):
    received = refs[:-5]
    first_ref, second_ref, grad_out_ref, sum_ref, sems = refs[-5:]
    copies = [pltpu.make_async_copy(input_grad_ref, grad_out_ref, sems.at[2])]
    copies[0].start()
    sum_ref[...] = self_ref[...] + sum(ref[...].astype(jnp.float32) for ref in received)
    for slot, ref in enumerate((first_ref, second_ref)):
        copies.append(pltpu.make_async_copy(sum_ref.at[slot], ref.at[centre_tap], sems.at[slot]))
        copies[-1].start()
    for copy in copies:
        copy.wait()


def local_plan(hidden_entry_states, base_ids, mask_index, first_kernel, second_kernel, head_weight):
    seq_count = lax.axis_size("seq")
    mp_count = lax.axis_size("mp")
    rows, channels = hidden_entry_states.shape
    tap_count, _, width = first_kernel.shape
    classes = head_weight.shape[1]
    centre_tap = tap_count // 2
    depth = channels // seq_count
    where = jnp.stack([lax.axis_index("mp"), lax.axis_index("seq")]).astype(jnp.int32)

    vmem = pl.BlockSpec(memory_space=pltpu.VMEM)
    smem = pl.BlockSpec(memory_space=pltpu.SMEM)
    hbm = pl.BlockSpec(memory_space=pltpu.HBM)

    def shape(dims, dtype=jnp.bfloat16):
        return jax.ShapeDtypeStruct(dims, dtype)

    def in_hbm(array):
        return pltpu.with_memory_space_constraint(array, pltpu.HBM)

    def call(body, in_specs, out_shape, out_specs=None, scratch=(), aliases={}, flops=0, moved=0):
        return pl.pallas_call(
            body,
            out_shape=out_shape,
            in_specs=in_specs,
            out_specs=(vmem,) * len(out_shape) if out_specs is None else out_specs,
            scratch_shapes=list(scratch),
            input_output_aliases=aliases,
            compiler_params=pltpu.CompilerParams(vmem_limit_bytes=VMEM_LIMIT),
            cost_estimate=pl.CostEstimate(flops=flops, bytes_accessed=moved, transcendentals=0),
        )

    own, own_share = call(
        functools.partial(first_copies_body, centre_tap),
        [smem] + [hbm] * 3,
        (shape((2, channels, width)), shape((rows // 2, channels))),
        scratch=[pltpu.SemaphoreType.DMA((3,))],
    )(where, in_hbm(first_kernel), in_hbm(second_kernel), in_hbm(hidden_entry_states))
    blocks = {0: own}
    bit = mp_count // 2
    while bit:
        for offset in list(blocks):
            blocks[offset ^ bit] = swap(blocks[offset], "mp", bit)
        bit //= 2
    blocks = [blocks[offset] for offset in range(mp_count)]

    apart = seq_count // 2
    far_rows = swap(own_share, "seq", apart)
    near_rows = swap(far_rows, "mp", 1)
    own_targets, sent_targets = call(
        targets_body,
        [smem] + [hbm] * 2,
        (shape((SIDE_ROWS, rows)),) * 2,
        scratch=[
            pltpu.SMEM(mask_index.shape, jnp.int32),
            pltpu.VMEM((1, rows), jnp.int32),
            pltpu.SemaphoreType.DMA((2,)),
        ],
    )(where, in_hbm(mask_index), in_hbm(base_ids[None, :]))
    peer_targets = swap(sent_targets, "seq", apart)
    whole = shape((tap_count, depth, width), jnp.float32)
    first_grad, second_grad = call(blank_body, [], (whole, whole))()

    pair_rows = 2 * rows
    early = channels - width
    product = 2 * pair_rows * channels * channels
    activation, slope, source_flip, head = call(
        functools.partial(early_body, mp_count),
        [smem] + [vmem] * (3 + mp_count),
        (
            shape((pair_rows, early), jnp.float32),
            shape((pair_rows, early), jnp.float32),
            shape((channels, pair_rows)),
            shape((SIDE_ROWS, channels)),
        ),
        flops=product,
        moved=8 * pair_rows * channels,
    )(where, hidden_entry_states, far_rows, near_rows, head_weight.T, *blocks[:-1])

    turns = seq_count // 2
    part = (2, depth, width)
    outs = call(
        functools.partial(main_body, mp_count, seq_count, classes),
        [smem] + [vmem] * (9 + mp_count),
        (shape(part, jnp.float32),)
        + (shape(part),) * (turns - 1)
        + (shape((rows, channels), jnp.float32), shape((rows, channels))),
        scratch=[
            pltpu.VMEM((pair_rows, channels), jnp.bfloat16),
            pltpu.VMEM((pair_rows, channels), jnp.float32),
            pltpu.VMEM((pair_rows, channels), jnp.float32),
            pltpu.VMEM((channels, pair_rows), jnp.bfloat16),
            pltpu.VMEM((pair_rows, channels), jnp.float32),
            pltpu.VMEM((pair_rows, channels), jnp.float32),
            pltpu.VMEM((pair_rows, channels), jnp.bfloat16),
            pltpu.VMEM((pair_rows, channels), jnp.float32),
            pltpu.VMEM((pair_rows, channels), jnp.bfloat16),
        ],
        flops=3 * product,
        moved=16 * pair_rows * channels,
    )(where, hidden_entry_states, far_rows, near_rows, own_targets, peer_targets, activation, slope, source_flip, head, *blocks)
    own_part, sent, (grad_one, grad_conv) = outs[0], outs[1:-2], outs[-2:]

    received = [swap(piece, "seq", turn) for turn, piece in enumerate(sent, 1)]
    (input_grad,) = call(
        functools.partial(input_grad_body, mp_count),
        [smem] + [vmem] * (2 + mp_count),
        (shape((rows, channels)),),
        flops=product // 2,
        moved=8 * rows * channels,
    )(where, grad_one, grad_conv, *blocks)
    first_grad, second_grad, input_grad = call(
        functools.partial(total_body, centre_tap),
        [hbm, hbm] + [vmem] * (1 + turns),
        (whole, whole, shape((rows, channels))),
        out_specs=(hbm,) * 3,
        scratch=[pltpu.VMEM(part, jnp.float32), pltpu.SemaphoreType.DMA((3,))],
        aliases={0: 0, 1: 1},
    )(first_grad, second_grad, input_grad, own_part, *received)
    return (input_grad, first_grad, second_grad)


def power_of_two(count):
    return count & (count - 1) == 0


def local(hidden_entry_states, base_ids, mask_index, first_kernel, second_kernel, head_weight):
    rows, channels = hidden_entry_states.shape
    tap_count, _, width = first_kernel.shape
    seq_count = lax.axis_size("seq")
    mp_count = lax.axis_size("mp")
    first_hops = active_hops(tap_count, DILATION_FIRST1 // rows, seq_count)
    second_hops = active_hops(tap_count, DILATION_SECOND2 // rows, seq_count)
    args = (hidden_entry_states, base_ids, mask_index, first_kernel, second_kernel, head_weight)
    fits = (
        power_of_two(mp_count)
        and power_of_two(seq_count)
        and mp_count > 1
        and seq_count > 1
        and width % 128 == 0
        and rows % 128 == 0
        and rows <= channels
        and (channels // seq_count) % 16 == 0
        and head_weight.shape[1] <= SIDE_ROWS
    )
    if len(first_hops) == 1 and len(second_hops) == 1 and fits:
        return local_plan(*args)
    return general_plan(*args, first_hops, second_hops)


def solution(mesh):
    placed = (P("seq", None), P("seq"), P("seq"), P(None, None, "mp"), P(None, None, "mp"), P())
    return jax.shard_map(
        local,
        mesh=mesh,
        in_specs=placed,
        out_specs=(P("seq", None), P(None, "seq", "mp"), P(None, "seq", "mp")),
        check_vma=False,
    )
```

```python
import functools

import jax
import jax.numpy as jnp
from jax import lax
from jax.experimental import pallas as pl
from jax.experimental.pallas import tpu as pltpu
from jax.sharding import PartitionSpec as P

DILATION_FIRST1 = 2048
DILATION_SECOND2 = 4096


epsilon = 1e-05
root_half = 0.7071067811865476
inv_root_two_pi = 0.3989422804014327
half_log2_e = -0.7213475204444817
log2_inv_root_two_pi = -1.3257480647361593
SIDE_ROWS = 16
VMEM_LIMIT = 24 * 1024 * 1024


def gelu_parts(conv_out):
    normal_cdf = 0.5 * (1.0 + lax.erf(conv_out * root_half))
    gelu_slope = normal_cdf + conv_out * inv_root_two_pi * jnp.exp(-0.5 * conv_out * conv_out)
    return (conv_out * normal_cdf, gelu_slope)


def norm_parts(activation):
    values = activation.astype(jnp.float32)
    centre = jnp.mean(values, axis=-1, keepdims=True)
    centred = values - centre
    spread = jnp.mean(centred * centred, axis=-1, keepdims=True)
    inverse = lax.rsqrt(spread + epsilon)
    return (centred * inverse, inverse)


def gelu_and_slope(conv_out):
    normal_cdf = 0.5 + 0.5 * lax.erf(conv_out * root_half)
    density = jnp.exp2(conv_out * conv_out * half_log2_e + log2_inv_root_two_pi)
    return (conv_out * normal_cdf, normal_cdf + conv_out * density)


def active_hops(tap_count, dilation_blocks, seq_count):
    centre_tap = tap_count // 2
    hops = [(tap, dilation_blocks * (tap - centre_tap)) for tap in range(tap_count)]
    return [(tap, hop) for tap, hop in hops if abs(hop) < seq_count]


def shifted(x, axis, by):
    if by == 0:
        return x
    peers = lax.axis_size(axis)
    pairs = [(i, i + by) for i in range(peers) if 0 <= i + by < peers]
    return lax.ppermute(x, axis, pairs)


def loss_grad(hidden_top, targets, head_weight):
    logits = lax.dot_general(
        head_weight, hidden_top, (((0,), (1,)), ((), ())), preferred_element_type=jnp.float32
    )
    exponent = jnp.exp(logits)
    probability = exponent / jnp.sum(exponent, axis=0, keepdims=True)
    vocab_rows = lax.broadcasted_iota(jnp.int32, logits.shape, 0)
    onehot = (vocab_rows == targets[None, :]).astype(jnp.float32)
    weight = (targets >= 0).astype(jnp.float32)[None, :]
    dlogits = weight * (probability - onehot)
    return lax.dot_general(
        dlogits,
        head_weight.astype(jnp.float32),
        (((0,), (1,)), ((), ())),
        precision=lax.Precision.HIGHEST,
    )


def general_plan(hidden_entry_states, base_ids, mask_index, first_kernel, second_kernel, head_weight, first_hops, second_hops):
    seq_count = lax.axis_size("seq")
    rows_per_block, channels = hidden_entry_states.shape
    tap_count, _, own_width = first_kernel.shape
    mask_count = mask_index.shape[0]
    offsets = mask_index - lax.axis_index("seq") * rows_per_block
    positions = lax.broadcasted_iota(jnp.int32, (rows_per_block, mask_count), 0)
    masked = jnp.any(positions == offsets[None, :], axis=1)
    targets = jnp.where(masked, base_ids, -1)

    def used(kernel, hops):
        first_tap, last_tap = hops[0][0], hops[-1][0]
        return kernel[first_tap : last_tap + 1]

    def block_forward_pass(source, kernel, hops):
        stacked = jnp.concatenate([shifted(source, "seq", -hop) for _, hop in hops], axis=1)
        conv_out = jnp.dot(
            stacked,
            used(kernel, hops).reshape(len(hops) * channels, own_width),
            preferred_element_type=jnp.float32,
        )
        activation, gelu_slope = gelu_parts(conv_out)
        mixed_all = lax.all_gather(activation.astype(jnp.bfloat16), "mp", axis=1, tiled=True)
        normed, inverse = norm_parts(mixed_all)
        result = (source.astype(jnp.float32) + normed).astype(jnp.bfloat16)
        return (result, (source, normed, inverse, gelu_slope))

    def block_backward_pass(grad_out, saved, kernel, hops):
        source, normed, inverse, gelu_slope = saved
        mean_grad = jnp.mean(grad_out, axis=-1, keepdims=True)
        mean_cross = jnp.mean(grad_out * normed, axis=-1, keepdims=True)
        grad_act = inverse * (grad_out - mean_grad - normed * mean_cross)
        own_cols = lax.dynamic_slice_in_dim(
            grad_act, lax.axis_index("mp") * own_width, own_width, 1
        )
        grad_conv = (own_cols * gelu_slope).astype(jnp.bfloat16)
        tap_stack = jnp.stack([shifted(grad_conv, "seq", hop) for _, hop in hops], axis=0)
        input_part = jnp.einsum(
            "kro,kdo->rd", tap_stack, used(kernel, hops), preferred_element_type=jnp.float32
        )
        grad_in = grad_out + lax.psum(input_part.astype(jnp.bfloat16), "mp").astype(jnp.float32)
        kernel_part = jnp.einsum(
            "rd,kro->kdo", source, tap_stack, preferred_element_type=jnp.float32
        )
        by_owner = kernel_part.reshape(len(hops), seq_count, channels // seq_count, own_width)
        received = lax.all_to_all(
            by_owner.astype(jnp.bfloat16), "seq", split_axis=1, concat_axis=1, tiled=True
        ).astype(by_owner.dtype)
        first_tap, last_tap = hops[0][0], hops[-1][0]
        kernel_grad = jnp.pad(
            jnp.sum(received, axis=1),
            ((first_tap, tap_count - 1 - last_tap), (0, 0), (0, 0)),
        )
        return (grad_in, kernel_grad)

    hidden_one, saved_one = block_forward_pass(hidden_entry_states, first_kernel, first_hops)
    hidden_two, saved_two = block_forward_pass(hidden_one, second_kernel, second_hops)
    grad_two = loss_grad(hidden_two, targets, head_weight)
    grad_one, second_grad = block_backward_pass(grad_two, saved_two, second_kernel, second_hops)
    grad_zero, first_grad = block_backward_pass(grad_one, saved_one, first_kernel, first_hops)
    return (grad_zero.astype(jnp.bfloat16), first_grad, second_grad)


NN = (((1,), (0,)), ((), ()))
NT = (((1,), (1,)), ((), ()))
TN = (((0,), (0,)), ((), ()))


def dot(a, b, dims=NN):
    return lax.dot_general(a, b, dims, preferred_element_type=jnp.float32)


def swap(block, axis, offset):
    return lax.ppermute(block, axis, [(i, i ^ offset) for i in range(lax.axis_size(axis))])


def block_at(me, offset, width):
    return pl.ds(pl.multiple_of((me ^ offset) * width, width), width)


def stacked(blocks, axis):
    return blocks[0] if len(blocks) == 1 else jnp.concatenate(blocks, axis=axis)


def own_order(me, refs, count):
    width = refs[0].shape[1] // count
    return stacked(
        [stacked([ref[:, block_at(me, o, width)] for o in range(count)], 1) for ref in refs], 0
    )


def matrices_body(centre_tap, first_ref, second_ref, both_ref, sems):
    copies = [
        pltpu.make_async_copy(ref.at[centre_tap], both_ref.at[slot], sems.at[slot])
        for slot, ref in enumerate((first_ref, second_ref))
    ]
    for copy in copies:
        copy.start()
    for copy in copies:
        copy.wait()


def prepare_body(mask_ref, ids_ref, source_ref, own_ref, sent_ref):
    rows = source_ref.shape[0]
    share = rows // 2
    entries = mask_ref.shape[1]
    part = lax.rem(lax.axis_index("mp"), 2)
    square = (entries, entries)
    diagonal = lax.broadcasted_iota(jnp.int32, square, 0) == lax.broadcasted_iota(jnp.int32, square, 1)
    offsets = (mask_ref[...] - lax.axis_index("seq") * rows).astype(jnp.float32)
    column = jnp.sum(jnp.where(diagonal, offsets, 0.0), axis=1, keepdims=True)
    positions = lax.broadcasted_iota(jnp.int32, (entries, rows), 1).astype(jnp.float32)
    masked = jnp.max((positions == column).astype(jnp.float32), axis=0, keepdims=True)
    targets = jnp.where(masked > 0.0, ids_ref[...].astype(jnp.float32), -1.0)
    targets = jnp.broadcast_to(targets, own_ref.shape)
    turned = pltpu.roll(targets, share, 1)
    own_ref[...] = targets.astype(jnp.bfloat16)
    sent_ref[0:share, :] = source_ref[pl.ds(pl.multiple_of(part * share, share), share), :]
    sent_ref[share:, :] = jnp.zeros((SIDE_ROWS, source_ref.shape[1]), jnp.bfloat16)
    sent_ref[share:, 0:rows] = jnp.where(part == 1, turned, targets).astype(jnp.bfloat16)


def blank_body(first_ref, second_ref):
    first_ref[...] = jnp.zeros_like(first_ref)
    second_ref[...] = jnp.zeros_like(second_ref)


def columns_of(me, matrix_refs, slot, count):
    width = matrix_refs[0].shape[2]
    return stacked(
        [
            stacked([ref[slot, block_at(me, o, width), :] for o in range(count)], 0)
            for ref in matrix_refs
        ],
        1,
    )


def row_halves(own_ref, far_ref, near_ref):
    share = own_ref.shape[0] // 2
    return ((own_ref,), (far_ref.at[0:share], near_ref.at[0:share]))


def early_body(count, own_ref, far_ref, near_ref, head_ref, *refs):
    matrix_refs = refs[:-4]
    activation_ref, slope_ref, flip_ref, head_out_ref = refs[-4:]
    me = lax.axis_index("mp")
    half = own_ref.shape[0]
    weights = columns_of(me, matrix_refs, 0, count)
    for part, source_refs in enumerate(row_halves(own_ref, far_ref, near_ref)):
        rows = pl.ds(part * half, half)
        conv_out = dot(own_order(me, source_refs, count), weights)
        activation_ref[rows, :], slope_ref[rows, :] = gelu_and_slope(conv_out)
        flip_ref[:, rows] = stacked([ref[...] for ref in source_refs], 0).T
    head_out_ref[...] = jnp.zeros_like(head_out_ref)
    classes = head_ref.shape[0]
    head_out_ref[0:classes, :] = own_order(me, (head_ref,), count)


def main_body(count, blocks, classes, own_ref, far_ref, near_ref, own_targets_ref, activation_ref, slope_ref, source_flip_ref, head_ref, *refs):
    turns = blocks // 2
    matrix_refs, refs = refs[:count], refs[count:]
    self_ref, sent_refs, refs = refs[0], refs[1:turns], refs[turns:]
    grad_out_ref, grad_conv_out_ref = refs[:2]
    hidden_one_ref, normed_one_ref, scale_one_ref, hidden_flip_ref, normed_two_ref, scale_two_ref, hidden_two_ref, grad_ref, grad_conv_ref = refs[2:]
    me, block = lax.axis_index("mp"), lax.axis_index("seq")
    half = own_ref.shape[0]
    _, depth, width = self_ref.shape
    source_refs = row_halves(own_ref, far_ref, near_ref)
    target_refs = (own_targets_ref, far_ref.at[half // 2 :, 0:half])
    late = columns_of(me, matrix_refs[-1:], 0, count)
    weights = columns_of(me, matrix_refs, 1, count)
    head = head_ref[...]

    def first_block(part):
        rows = pl.ds(part * half, half)
        source = own_order(me, source_refs[part], count)
        activation, gelu_slope = gelu_and_slope(dot(source, late))
        normed, inverse = norm_parts(jnp.concatenate([activation_ref[rows, :], activation], axis=1))
        scale_one_ref[rows, :] = jnp.concatenate([slope_ref[rows, :], gelu_slope], axis=1) * inverse
        normed_one_ref[rows, :] = normed
        hidden_one_ref[rows, :] = (source.astype(jnp.float32) + normed).astype(jnp.bfloat16)

    def second_block(part):
        rows = pl.ds(part * half, half)
        source = hidden_one_ref[rows, :]
        activation, gelu_slope = gelu_and_slope(dot(source, weights))
        normed, inverse = norm_parts(activation)
        scale_two_ref[rows, :] = gelu_slope * inverse
        normed_two_ref[rows, :] = normed
        hidden_two_ref[rows, :] = (source.astype(jnp.float32) + normed).astype(jnp.bfloat16)

    def flip_hidden(part):
        rows = pl.ds(part * half, half)
        for offset in range(count):
            flipped = hidden_one_ref[rows, pl.ds(offset * width, width)].T
            hidden_flip_ref[block_at(me, offset, width), rows] = flipped

    def loss_backward(part):
        rows = pl.ds(part * half, half)
        logits = dot(head, hidden_two_ref[rows, :], NT)
        class_rows = lax.broadcasted_iota(jnp.int32, logits.shape, 0)
        exponent = jnp.where(class_rows < classes, jnp.exp(logits), 0.0)
        probability = exponent / jnp.sum(exponent, axis=0, keepdims=True)
        targets = target_refs[part][...].astype(jnp.float32)
        onehot = (class_rows.astype(jnp.float32) == targets).astype(jnp.float32)
        weight = (targets >= 0.0).astype(jnp.float32)
        rest = jnp.where(class_rows < classes, weight * (probability - onehot), 0.0)
        terms = []
        for _ in range(3):
            term = rest.astype(jnp.bfloat16)
            terms.append(term)
            rest = rest - term.astype(jnp.float32)
        grad_ref[rows, :] = dot(jnp.concatenate(terms, axis=0), jnp.concatenate([head] * 3, axis=0), TN)

    def norm_backward(part, normed_ref, scale_ref):
        rows = pl.ds(part * half, half)
        grad_out, normed = grad_ref[rows, :], normed_ref[rows, :]
        mean_grad = jnp.mean(grad_out, axis=-1, keepdims=True)
        mean_cross = jnp.mean(grad_out * normed, axis=-1, keepdims=True)
        grad_conv_ref[rows, :] = (
            (grad_out - mean_grad - normed * mean_cross) * scale_ref[rows, :]
        ).astype(jnp.bfloat16)

    def input_backward(part):
        rows = pl.ds(part * half, half)
        grad_ref[rows, :] += dot(grad_conv_ref[rows, :], weights, NT)

    def kernel_parts(flip_ref, slot):
        sources = [
            flip_ref[pl.ds(pl.multiple_of((block ^ turn) * depth, depth), depth), :]
            for turn in range(turns)
        ]
        part = dot(stacked(sources, 0), grad_conv_ref[:, 0:width])
        self_ref[slot] = part[0:depth]
        for turn, ref in enumerate(sent_refs, 1):
            ref[slot] = part[turn * depth : (turn + 1) * depth].astype(jnp.bfloat16)

    first_block(0)
    first_block(1)
    second_block(0)
    second_block(1)
    loss_backward(0)
    norm_backward(0, normed_two_ref, scale_two_ref)
    loss_backward(1)
    norm_backward(1, normed_two_ref, scale_two_ref)
    input_backward(0)
    input_backward(1)
    flip_hidden(0)
    flip_hidden(1)
    kernel_parts(hidden_flip_ref, 1)
    norm_backward(0, normed_one_ref, scale_one_ref)
    norm_backward(1, normed_one_ref, scale_one_ref)
    kernel_parts(source_flip_ref, 0)
    grad_out_ref[...] = grad_ref[pl.ds(0, half), :]
    grad_conv_out_ref[...] = grad_conv_ref[pl.ds(0, half), :]


def input_grad_body(count, grad_ref, grad_conv_ref, *refs):
    matrix_refs, input_grad_ref = refs[:count], refs[count]
    me = lax.axis_index("mp")
    width = matrix_refs[0].shape[2]
    total = grad_ref[...] + dot(grad_conv_ref[...], columns_of(me, matrix_refs, 0, count), NT)
    for offset in range(count):
        input_grad_ref[:, block_at(me, offset, width)] = total[
            :, offset * width : (offset + 1) * width
        ].astype(jnp.bfloat16)


def total_body(centre_tap, first_in_ref, second_in_ref, input_grad_ref, self_ref, *refs):
    received = refs[:-5]
    first_ref, second_ref, grad_out_ref, sum_ref, sems = refs[-5:]
    copies = [pltpu.make_async_copy(input_grad_ref, grad_out_ref, sems.at[2])]
    copies[0].start()
    sum_ref[...] = self_ref[...] + sum(ref[...].astype(jnp.float32) for ref in received)
    for slot, ref in enumerate((first_ref, second_ref)):
        copies.append(pltpu.make_async_copy(sum_ref.at[slot], ref.at[centre_tap], sems.at[slot]))
        copies[-1].start()
    for copy in copies:
        copy.wait()


def local_plan(hidden_entry_states, base_ids, mask_index, first_kernel, second_kernel, head_weight):
    seq_count = lax.axis_size("seq")
    mp_count = lax.axis_size("mp")
    rows, channels = hidden_entry_states.shape
    tap_count, _, width = first_kernel.shape
    classes = head_weight.shape[1]
    centre_tap = tap_count // 2
    depth = channels // seq_count

    vmem = pl.BlockSpec(memory_space=pltpu.VMEM)
    hbm = pl.BlockSpec(memory_space=pltpu.HBM)

    def shape(dims, dtype=jnp.bfloat16):
        return jax.ShapeDtypeStruct(dims, dtype)

    def in_hbm(array):
        return pltpu.with_memory_space_constraint(array, pltpu.HBM)

    def call(body, in_specs, out_shape, out_specs=None, scratch=(), aliases={}, flops=0, moved=0):
        return pl.pallas_call(
            body,
            out_shape=out_shape,
            in_specs=in_specs,
            out_specs=(vmem,) * len(out_shape) if out_specs is None else out_specs,
            scratch_shapes=list(scratch),
            input_output_aliases=aliases,
            compiler_params=pltpu.CompilerParams(vmem_limit_bytes=VMEM_LIMIT),
            cost_estimate=pl.CostEstimate(flops=flops, bytes_accessed=moved, transcendentals=0),
        )

    (own,) = call(
        functools.partial(matrices_body, centre_tap),
        [hbm] * 2,
        (shape((2, channels, width)),),
        scratch=[pltpu.SemaphoreType.DMA((2,))],
    )(in_hbm(first_kernel), in_hbm(second_kernel))
    blocks = {0: own}
    bit = mp_count // 2
    while bit:
        for offset in list(blocks):
            blocks[offset ^ bit] = swap(blocks[offset], "mp", bit)
        bit //= 2
    blocks = [blocks[offset] for offset in range(mp_count)]

    own_targets, sent_rows = call(
        prepare_body,
        [vmem] * 3,
        (shape((SIDE_ROWS, rows)), shape((rows // 2 + SIDE_ROWS, channels))),
    )(mask_index[None, :], base_ids[None, :], hidden_entry_states)
    far_rows = swap(sent_rows, "seq", seq_count // 2)
    near_rows = swap(far_rows, "mp", 1)
    whole = shape((tap_count, depth, width), jnp.float32)
    first_grad, second_grad = call(blank_body, [], (whole, whole))()

    pair_rows = 2 * rows
    early = channels - width
    product = 2 * pair_rows * channels * channels
    activation, slope, source_flip, head = call(
        functools.partial(early_body, mp_count),
        [vmem] * (3 + mp_count),
        (
            shape((pair_rows, early), jnp.float32),
            shape((pair_rows, early), jnp.float32),
            shape((channels, pair_rows)),
            shape((SIDE_ROWS, channels)),
        ),
        flops=product,
        moved=8 * pair_rows * channels,
    )(hidden_entry_states, far_rows, near_rows, head_weight.T, *blocks[:-1])

    turns = seq_count // 2
    part = (2, depth, width)
    outs = call(
        functools.partial(main_body, mp_count, seq_count, classes),
        [vmem] * (8 + mp_count),
        (shape(part, jnp.float32),)
        + (shape(part),) * (turns - 1)
        + (shape((rows, channels), jnp.float32), shape((rows, channels))),
        scratch=[
            pltpu.VMEM((pair_rows, channels), jnp.bfloat16),
            pltpu.VMEM((pair_rows, channels), jnp.float32),
            pltpu.VMEM((pair_rows, channels), jnp.float32),
            pltpu.VMEM((channels, pair_rows), jnp.bfloat16),
            pltpu.VMEM((pair_rows, channels), jnp.float32),
            pltpu.VMEM((pair_rows, channels), jnp.float32),
            pltpu.VMEM((pair_rows, channels), jnp.bfloat16),
            pltpu.VMEM((pair_rows, channels), jnp.float32),
            pltpu.VMEM((pair_rows, channels), jnp.bfloat16),
        ],
        flops=3 * product,
        moved=16 * pair_rows * channels,
    )(hidden_entry_states, far_rows, near_rows, own_targets, activation, slope, source_flip, head, *blocks)
    own_part, sent, (grad_one, grad_conv) = outs[0], outs[1:-2], outs[-2:]

    received = [swap(piece, "seq", turn) for turn, piece in enumerate(sent, 1)]
    (input_grad,) = call(
        functools.partial(input_grad_body, mp_count),
        [vmem] * (2 + mp_count),
        (shape((rows, channels)),),
        flops=product // 2,
        moved=8 * rows * channels,
    )(grad_one, grad_conv, *blocks)
    first_grad, second_grad, input_grad = call(
        functools.partial(total_body, centre_tap),
        [hbm, hbm] + [vmem] * (1 + turns),
        (whole, whole, shape((rows, channels))),
        out_specs=(hbm,) * 3,
        scratch=[pltpu.VMEM(part, jnp.float32), pltpu.SemaphoreType.DMA((3,))],
        aliases={0: 0, 1: 1},
    )(first_grad, second_grad, input_grad, own_part, *received)
    return (input_grad, first_grad, second_grad)


def power_of_two(count):
    return count & (count - 1) == 0


def local(hidden_entry_states, base_ids, mask_index, first_kernel, second_kernel, head_weight):
    rows, channels = hidden_entry_states.shape
    tap_count, _, width = first_kernel.shape
    seq_count = lax.axis_size("seq")
    mp_count = lax.axis_size("mp")
    first_hops = active_hops(tap_count, DILATION_FIRST1 // rows, seq_count)
    second_hops = active_hops(tap_count, DILATION_SECOND2 // rows, seq_count)
    args = (hidden_entry_states, base_ids, mask_index, first_kernel, second_kernel, head_weight)
    fits = (
        power_of_two(mp_count)
        and power_of_two(seq_count)
        and mp_count > 1
        and seq_count > 1
        and width % 128 == 0
        and rows % 128 == 0
        and rows <= channels
        and (channels // seq_count) % 16 == 0
        and head_weight.shape[1] <= SIDE_ROWS
    )
    if len(first_hops) == 1 and len(second_hops) == 1 and fits:
        return local_plan(*args)
    return general_plan(*args, first_hops, second_hops)


def solution(mesh):
    placed = (P("seq", None), P("seq"), P("seq"), P(None, None, "mp"), P(None, None, "mp"), P())
    return jax.shard_map(
        local,
        mesh=mesh,
        in_specs=placed,
        out_specs=(P("seq", None), P(None, "seq", "mp"), P(None, "seq", "mp")),
        check_vma=False,
    )
```

```python
import functools

import jax
import jax.numpy as jnp
from jax import lax
from jax.experimental import pallas as pl
from jax.experimental.pallas import tpu as pltpu
from jax.sharding import PartitionSpec as P

DILATION_FIRST1 = 2048
DILATION_SECOND2 = 4096


epsilon = 1e-05
root_half = 0.7071067811865476
inv_root_two_pi = 0.3989422804014327
half_log2_e = -0.7213475204444817
log2_inv_root_two_pi = -1.3257480647361593
SIDE_ROWS = 16
VMEM_LIMIT = 24 * 1024 * 1024


def gelu_parts(conv_out):
    normal_cdf = 0.5 * (1.0 + lax.erf(conv_out * root_half))
    gelu_slope = normal_cdf + conv_out * inv_root_two_pi * jnp.exp(-0.5 * conv_out * conv_out)
    return (conv_out * normal_cdf, gelu_slope)


def norm_parts(activation):
    values = activation.astype(jnp.float32)
    centre = jnp.mean(values, axis=-1, keepdims=True)
    centred = values - centre
    spread = jnp.mean(centred * centred, axis=-1, keepdims=True)
    inverse = lax.rsqrt(spread + epsilon)
    return (centred * inverse, inverse)


def gelu_and_slope(conv_out):
    normal_cdf = 0.5 + 0.5 * lax.erf(conv_out * root_half)
    density = jnp.exp2(conv_out * conv_out * half_log2_e + log2_inv_root_two_pi)
    return (conv_out * normal_cdf, normal_cdf + conv_out * density)


def active_hops(tap_count, dilation_blocks, seq_count):
    centre_tap = tap_count // 2
    hops = [(tap, dilation_blocks * (tap - centre_tap)) for tap in range(tap_count)]
    return [(tap, hop) for tap, hop in hops if abs(hop) < seq_count]


def shifted(x, axis, by):
    if by == 0:
        return x
    peers = lax.axis_size(axis)
    pairs = [(i, i + by) for i in range(peers) if 0 <= i + by < peers]
    return lax.ppermute(x, axis, pairs)


def loss_grad(hidden_top, targets, head_weight):
    logits = lax.dot_general(
        head_weight, hidden_top, (((0,), (1,)), ((), ())), preferred_element_type=jnp.float32
    )
    exponent = jnp.exp(logits)
    probability = exponent / jnp.sum(exponent, axis=0, keepdims=True)
    vocab_rows = lax.broadcasted_iota(jnp.int32, logits.shape, 0)
    onehot = (vocab_rows == targets[None, :]).astype(jnp.float32)
    weight = (targets >= 0).astype(jnp.float32)[None, :]
    dlogits = weight * (probability - onehot)
    return lax.dot_general(
        dlogits,
        head_weight.astype(jnp.float32),
        (((0,), (1,)), ((), ())),
        precision=lax.Precision.HIGHEST,
    )


def general_plan(hidden_entry_states, base_ids, mask_index, first_kernel, second_kernel, head_weight, first_hops, second_hops):
    seq_count = lax.axis_size("seq")
    rows_per_block, channels = hidden_entry_states.shape
    tap_count, _, own_width = first_kernel.shape
    mask_count = mask_index.shape[0]
    offsets = mask_index - lax.axis_index("seq") * rows_per_block
    positions = lax.broadcasted_iota(jnp.int32, (rows_per_block, mask_count), 0)
    masked = jnp.any(positions == offsets[None, :], axis=1)
    targets = jnp.where(masked, base_ids, -1)

    def used(kernel, hops):
        first_tap, last_tap = hops[0][0], hops[-1][0]
        return kernel[first_tap : last_tap + 1]

    def block_forward_pass(source, kernel, hops):
        stacked = jnp.concatenate([shifted(source, "seq", -hop) for _, hop in hops], axis=1)
        conv_out = jnp.dot(
            stacked,
            used(kernel, hops).reshape(len(hops) * channels, own_width),
            preferred_element_type=jnp.float32,
        )
        activation, gelu_slope = gelu_parts(conv_out)
        mixed_all = lax.all_gather(activation.astype(jnp.bfloat16), "mp", axis=1, tiled=True)
        normed, inverse = norm_parts(mixed_all)
        result = (source.astype(jnp.float32) + normed).astype(jnp.bfloat16)
        return (result, (source, normed, inverse, gelu_slope))

    def block_backward_pass(grad_out, saved, kernel, hops):
        source, normed, inverse, gelu_slope = saved
        mean_grad = jnp.mean(grad_out, axis=-1, keepdims=True)
        mean_cross = jnp.mean(grad_out * normed, axis=-1, keepdims=True)
        grad_act = inverse * (grad_out - mean_grad - normed * mean_cross)
        own_cols = lax.dynamic_slice_in_dim(
            grad_act, lax.axis_index("mp") * own_width, own_width, 1
        )
        grad_conv = (own_cols * gelu_slope).astype(jnp.bfloat16)
        tap_stack = jnp.stack([shifted(grad_conv, "seq", hop) for _, hop in hops], axis=0)
        input_part = jnp.einsum(
            "kro,kdo->rd", tap_stack, used(kernel, hops), preferred_element_type=jnp.float32
        )
        grad_in = grad_out + lax.psum(input_part.astype(jnp.bfloat16), "mp").astype(jnp.float32)
        kernel_part = jnp.einsum(
            "rd,kro->kdo", source, tap_stack, preferred_element_type=jnp.float32
        )
        by_owner = kernel_part.reshape(len(hops), seq_count, channels // seq_count, own_width)
        received = lax.all_to_all(
            by_owner.astype(jnp.bfloat16), "seq", split_axis=1, concat_axis=1, tiled=True
        ).astype(by_owner.dtype)
        first_tap, last_tap = hops[0][0], hops[-1][0]
        kernel_grad = jnp.pad(
            jnp.sum(received, axis=1),
            ((first_tap, tap_count - 1 - last_tap), (0, 0), (0, 0)),
        )
        return (grad_in, kernel_grad)

    hidden_one, saved_one = block_forward_pass(hidden_entry_states, first_kernel, first_hops)
    hidden_two, saved_two = block_forward_pass(hidden_one, second_kernel, second_hops)
    grad_two = loss_grad(hidden_two, targets, head_weight)
    grad_one, second_grad = block_backward_pass(grad_two, saved_two, second_kernel, second_hops)
    grad_zero, first_grad = block_backward_pass(grad_one, saved_one, first_kernel, first_hops)
    return (grad_zero.astype(jnp.bfloat16), first_grad, second_grad)


NN = (((1,), (0,)), ((), ()))
NT = (((1,), (1,)), ((), ()))
TN = (((0,), (0,)), ((), ()))


def dot(a, b, dims=NN):
    return lax.dot_general(a, b, dims, preferred_element_type=jnp.float32)


def swap(block, axis, offset):
    return lax.ppermute(block, axis, [(i, i ^ offset) for i in range(lax.axis_size(axis))])


def block_at(me, offset, width):
    return pl.ds(pl.multiple_of((me ^ offset) * width, width), width)


def stacked(blocks, axis):
    return blocks[0] if len(blocks) == 1 else jnp.concatenate(blocks, axis=axis)


def own_order(me, refs, count):
    width = refs[0].shape[1] // count
    return stacked(
        [stacked([ref[:, block_at(me, o, width)] for o in range(count)], 1) for ref in refs], 0
    )


def matrices_body(centre_tap, first_ref, second_ref, both_ref, sems):
    copies = [
        pltpu.make_async_copy(ref.at[centre_tap], both_ref.at[slot], sems.at[slot])
        for slot, ref in enumerate((first_ref, second_ref))
    ]
    for copy in copies:
        copy.start()
    for copy in copies:
        copy.wait()


def prepare_body(mask_ref, ids_ref, source_ref, own_ref, sent_targets_ref, sent_ref):
    rows = source_ref.shape[0]
    share = rows // 2
    entries = mask_ref.shape[1]
    part = lax.rem(lax.axis_index("mp"), 2)
    square = (entries, entries)
    diagonal = lax.broadcasted_iota(jnp.int32, square, 0) == lax.broadcasted_iota(jnp.int32, square, 1)
    offsets = (mask_ref[...] - lax.axis_index("seq") * rows).astype(jnp.float32)
    column = jnp.sum(jnp.where(diagonal, offsets, 0.0), axis=1, keepdims=True)
    positions = lax.broadcasted_iota(jnp.int32, (entries, rows), 1).astype(jnp.float32)
    masked = jnp.max((positions == column).astype(jnp.float32), axis=0, keepdims=True)
    targets = jnp.where(masked > 0.0, ids_ref[...].astype(jnp.float32), -1.0)
    targets = jnp.broadcast_to(targets, own_ref.shape)
    turned = pltpu.roll(targets, share, 1)
    own_ref[...] = targets.astype(jnp.bfloat16)
    sent_targets_ref[...] = jnp.where(part == 1, turned, targets).astype(jnp.bfloat16)
    sent_ref[...] = source_ref[pl.ds(pl.multiple_of(part * share, share), share), :]


def blank_body(first_ref, second_ref):
    first_ref[...] = jnp.zeros_like(first_ref)
    second_ref[...] = jnp.zeros_like(second_ref)


def columns_of(me, matrix_refs, slot, count):
    width = matrix_refs[0].shape[2]
    return stacked(
        [
            stacked([ref[slot, block_at(me, o, width), :] for o in range(count)], 0)
            for ref in matrix_refs
        ],
        1,
    )


def row_halves(own_ref, far_ref, near_ref):
    return ((own_ref,), (far_ref, near_ref))


def early_body(count, own_ref, far_ref, near_ref, head_ref, *refs):
    matrix_refs = refs[:-4]
    activation_ref, slope_ref, flip_ref, head_out_ref = refs[-4:]
    me = lax.axis_index("mp")
    half = own_ref.shape[0]
    weights = columns_of(me, matrix_refs, 0, count)
    for part, source_refs in enumerate(row_halves(own_ref, far_ref, near_ref)):
        rows = pl.ds(part * half, half)
        conv_out = dot(own_order(me, source_refs, count), weights)
        activation_ref[rows, :], slope_ref[rows, :] = gelu_and_slope(conv_out)
        flip_ref[:, rows] = stacked([ref[...] for ref in source_refs], 0).T
    head_out_ref[...] = jnp.zeros_like(head_out_ref)
    classes = head_ref.shape[0]
    head_out_ref[0:classes, :] = own_order(me, (head_ref,), count)


def main_body(count, blocks, classes, own_ref, far_ref, near_ref, own_targets_ref, peer_targets_ref, activation_ref, slope_ref, source_flip_ref, head_ref, *refs):
    turns = blocks // 2
    matrix_refs, refs = refs[:count], refs[count:]
    self_ref, sent_refs, refs = refs[0], refs[1:turns], refs[turns:]
    grad_out_ref, grad_conv_out_ref = refs[:2]
    hidden_one_ref, normed_one_ref, scale_one_ref, hidden_flip_ref, normed_two_ref, scale_two_ref, hidden_two_ref, grad_ref, grad_conv_ref = refs[2:]
    me, block = lax.axis_index("mp"), lax.axis_index("seq")
    half = own_ref.shape[0]
    _, depth, width = self_ref.shape
    source_refs = row_halves(own_ref, far_ref, near_ref)
    target_refs = (own_targets_ref, peer_targets_ref)
    late = columns_of(me, matrix_refs[-1:], 0, count)
    weights = columns_of(me, matrix_refs, 1, count)
    head = head_ref[...]

    def first_block(part):
        rows = pl.ds(part * half, half)
        source = own_order(me, source_refs[part], count)
        activation, gelu_slope = gelu_and_slope(dot(source, late))
        normed, inverse = norm_parts(jnp.concatenate([activation_ref[rows, :], activation], axis=1))
        scale_one_ref[rows, :] = jnp.concatenate([slope_ref[rows, :], gelu_slope], axis=1) * inverse
        normed_one_ref[rows, :] = normed
        hidden_one_ref[rows, :] = (source.astype(jnp.float32) + normed).astype(jnp.bfloat16)

    def second_block(part):
        rows = pl.ds(part * half, half)
        source = hidden_one_ref[rows, :]
        activation, gelu_slope = gelu_and_slope(dot(source, weights))
        normed, inverse = norm_parts(activation)
        scale_two_ref[rows, :] = gelu_slope * inverse
        normed_two_ref[rows, :] = normed
        hidden_two_ref[rows, :] = (source.astype(jnp.float32) + normed).astype(jnp.bfloat16)

    def flip_hidden(part):
        rows = pl.ds(part * half, half)
        for offset in range(count):
            flipped = hidden_one_ref[rows, pl.ds(offset * width, width)].T
            hidden_flip_ref[block_at(me, offset, width), rows] = flipped

    def loss_backward(part):
        rows = pl.ds(part * half, half)
        logits = dot(head, hidden_two_ref[rows, :], NT)
        class_rows = lax.broadcasted_iota(jnp.int32, logits.shape, 0)
        exponent = jnp.where(class_rows < classes, jnp.exp(logits), 0.0)
        probability = exponent / jnp.sum(exponent, axis=0, keepdims=True)
        targets = target_refs[part][...].astype(jnp.float32)
        onehot = (class_rows.astype(jnp.float32) == targets).astype(jnp.float32)
        weight = (targets >= 0.0).astype(jnp.float32)
        rest = jnp.where(class_rows < classes, weight * (probability - onehot), 0.0)
        terms = []
        for _ in range(3):
            term = rest.astype(jnp.bfloat16)
            terms.append(term)
            rest = rest - term.astype(jnp.float32)
        grad_ref[rows, :] = dot(jnp.concatenate(terms, axis=0), jnp.concatenate([head] * 3, axis=0), TN)

    def norm_backward(part, normed_ref, scale_ref):
        rows = pl.ds(part * half, half)
        grad_out, normed = grad_ref[rows, :], normed_ref[rows, :]
        mean_grad = jnp.mean(grad_out, axis=-1, keepdims=True)
        mean_cross = jnp.mean(grad_out * normed, axis=-1, keepdims=True)
        grad_conv_ref[rows, :] = (
            (grad_out - mean_grad - normed * mean_cross) * scale_ref[rows, :]
        ).astype(jnp.bfloat16)

    def input_backward(part):
        rows = pl.ds(part * half, half)
        grad_ref[rows, :] += dot(grad_conv_ref[rows, :], weights, NT)

    def kernel_parts(flip_ref, slot):
        sources = [
            flip_ref[pl.ds(pl.multiple_of((block ^ turn) * depth, depth), depth), :]
            for turn in range(turns)
        ]
        part = dot(stacked(sources, 0), grad_conv_ref[:, 0:width])
        self_ref[slot] = part[0:depth]
        for turn, ref in enumerate(sent_refs, 1):
            ref[slot] = part[turn * depth : (turn + 1) * depth].astype(jnp.bfloat16)

    first_block(0)
    first_block(1)
    second_block(0)
    second_block(1)
    loss_backward(0)
    norm_backward(0, normed_two_ref, scale_two_ref)
    loss_backward(1)
    norm_backward(1, normed_two_ref, scale_two_ref)
    input_backward(0)
    input_backward(1)
    flip_hidden(0)
    flip_hidden(1)
    kernel_parts(hidden_flip_ref, 1)
    norm_backward(0, normed_one_ref, scale_one_ref)
    norm_backward(1, normed_one_ref, scale_one_ref)
    kernel_parts(source_flip_ref, 0)
    grad_out_ref[...] = grad_ref[pl.ds(0, half), :]
    grad_conv_out_ref[...] = grad_conv_ref[pl.ds(0, half), :]


def input_grad_body(count, grad_ref, grad_conv_ref, *refs):
    matrix_refs, input_grad_ref = refs[:count], refs[count]
    me = lax.axis_index("mp")
    width = matrix_refs[0].shape[2]
    total = grad_ref[...] + dot(grad_conv_ref[...], columns_of(me, matrix_refs, 0, count), NT)
    for offset in range(count):
        input_grad_ref[:, block_at(me, offset, width)] = total[
            :, offset * width : (offset + 1) * width
        ].astype(jnp.bfloat16)


def total_body(centre_tap, first_in_ref, second_in_ref, input_grad_ref, self_ref, *refs):
    received = refs[:-5]
    first_ref, second_ref, grad_out_ref, sum_ref, sems = refs[-5:]
    copies = [pltpu.make_async_copy(input_grad_ref, grad_out_ref, sems.at[2])]
    copies[0].start()
    sum_ref[...] = self_ref[...] + sum(ref[...].astype(jnp.float32) for ref in received)
    for slot, ref in enumerate((first_ref, second_ref)):
        copies.append(pltpu.make_async_copy(sum_ref.at[slot], ref.at[centre_tap], sems.at[slot]))
        copies[-1].start()
    for copy in copies:
        copy.wait()


def local_plan(hidden_entry_states, base_ids, mask_index, first_kernel, second_kernel, head_weight):
    seq_count = lax.axis_size("seq")
    mp_count = lax.axis_size("mp")
    rows, channels = hidden_entry_states.shape
    tap_count, _, width = first_kernel.shape
    classes = head_weight.shape[1]
    centre_tap = tap_count // 2
    depth = channels // seq_count

    vmem = pl.BlockSpec(memory_space=pltpu.VMEM)
    hbm = pl.BlockSpec(memory_space=pltpu.HBM)

    def shape(dims, dtype=jnp.bfloat16):
        return jax.ShapeDtypeStruct(dims, dtype)

    def in_hbm(array):
        return pltpu.with_memory_space_constraint(array, pltpu.HBM)

    def call(body, in_specs, out_shape, out_specs=None, scratch=(), aliases={}, flops=0, moved=0):
        return pl.pallas_call(
            body,
            out_shape=out_shape,
            in_specs=in_specs,
            out_specs=(vmem,) * len(out_shape) if out_specs is None else out_specs,
            scratch_shapes=list(scratch),
            input_output_aliases=aliases,
            compiler_params=pltpu.CompilerParams(vmem_limit_bytes=VMEM_LIMIT),
            cost_estimate=pl.CostEstimate(flops=flops, bytes_accessed=moved, transcendentals=0),
        )

    (own,) = call(
        functools.partial(matrices_body, centre_tap),
        [hbm] * 2,
        (shape((2, channels, width)),),
        scratch=[pltpu.SemaphoreType.DMA((2,))],
    )(in_hbm(first_kernel), in_hbm(second_kernel))
    blocks = {0: own}
    bit = mp_count // 2
    while bit:
        for offset in list(blocks):
            blocks[offset ^ bit] = swap(blocks[offset], "mp", bit)
        bit //= 2
    blocks = [blocks[offset] for offset in range(mp_count)]

    own_targets, sent_targets, sent_rows = call(
        prepare_body, [vmem] * 3, (shape((SIDE_ROWS, rows)),) * 2 + (shape((rows // 2, channels)),)
    )(mask_index[None, :], base_ids[None, :], hidden_entry_states)
    far_rows = swap(sent_rows, "seq", seq_count // 2)
    near_rows = swap(far_rows, "mp", 1)
    peer_targets = swap(sent_targets, "seq", seq_count // 2)
    whole = shape((tap_count, depth, width), jnp.float32)
    first_grad, second_grad = call(blank_body, [], (whole, whole))()

    pair_rows = 2 * rows
    early = channels - width
    product = 2 * pair_rows * channels * channels
    activation, slope, source_flip, head = call(
        functools.partial(early_body, mp_count),
        [vmem] * (3 + mp_count),
        (
            shape((pair_rows, early), jnp.float32),
            shape((pair_rows, early), jnp.float32),
            shape((channels, pair_rows)),
            shape((SIDE_ROWS, channels)),
        ),
        flops=product,
        moved=8 * pair_rows * channels,
    )(hidden_entry_states, far_rows, near_rows, head_weight.T, *blocks[:-1])

    turns = seq_count // 2
    part = (2, depth, width)
    outs = call(
        functools.partial(main_body, mp_count, seq_count, classes),
        [vmem] * (9 + mp_count),
        (shape(part, jnp.float32),)
        + (shape(part),) * (turns - 1)
        + (shape((rows, channels), jnp.float32), shape((rows, channels))),
        scratch=[
            pltpu.VMEM((pair_rows, channels), jnp.bfloat16),
            pltpu.VMEM((pair_rows, channels), jnp.float32),
            pltpu.VMEM((pair_rows, channels), jnp.float32),
            pltpu.VMEM((channels, pair_rows), jnp.bfloat16),
            pltpu.VMEM((pair_rows, channels), jnp.float32),
            pltpu.VMEM((pair_rows, channels), jnp.float32),
            pltpu.VMEM((pair_rows, channels), jnp.bfloat16),
            pltpu.VMEM((pair_rows, channels), jnp.float32),
            pltpu.VMEM((pair_rows, channels), jnp.bfloat16),
        ],
        flops=3 * product,
        moved=16 * pair_rows * channels,
    )(hidden_entry_states, far_rows, near_rows, own_targets, peer_targets, activation, slope, source_flip, head, *blocks)
    own_part, sent, (grad_one, grad_conv) = outs[0], outs[1:-2], outs[-2:]

    received = [swap(piece, "seq", turn) for turn, piece in enumerate(sent, 1)]
    (input_grad,) = call(
        functools.partial(input_grad_body, mp_count),
        [vmem] * (2 + mp_count),
        (shape((rows, channels)),),
        flops=product // 2,
        moved=8 * rows * channels,
    )(grad_one, grad_conv, *blocks)
    first_grad, second_grad, input_grad = call(
        functools.partial(total_body, centre_tap),
        [hbm, hbm] + [vmem] * (1 + turns),
        (whole, whole, shape((rows, channels))),
        out_specs=(hbm,) * 3,
        scratch=[pltpu.VMEM(part, jnp.float32), pltpu.SemaphoreType.DMA((3,))],
        aliases={0: 0, 1: 1},
    )(first_grad, second_grad, input_grad, own_part, *received)
    return (input_grad, first_grad, second_grad)


def power_of_two(count):
    return count & (count - 1) == 0


def local(hidden_entry_states, base_ids, mask_index, first_kernel, second_kernel, head_weight):
    rows, channels = hidden_entry_states.shape
    tap_count, _, width = first_kernel.shape
    seq_count = lax.axis_size("seq")
    mp_count = lax.axis_size("mp")
    first_hops = active_hops(tap_count, DILATION_FIRST1 // rows, seq_count)
    second_hops = active_hops(tap_count, DILATION_SECOND2 // rows, seq_count)
    args = (hidden_entry_states, base_ids, mask_index, first_kernel, second_kernel, head_weight)
    fits = (
        power_of_two(mp_count)
        and power_of_two(seq_count)
        and mp_count > 1
        and seq_count > 1
        and width % 128 == 0
        and rows % 128 == 0
        and rows <= channels
        and (channels // seq_count) % 16 == 0
        and head_weight.shape[1] <= SIDE_ROWS
    )
    if len(first_hops) == 1 and len(second_hops) == 1 and fits:
        return local_plan(*args)
    return general_plan(*args, first_hops, second_hops)


def solution(mesh):
    placed = (P("seq", None), P("seq"), P("seq"), P(None, None, "mp"), P(None, None, "mp"), P())
    return jax.shard_map(
        local,
        mesh=mesh,
        in_specs=placed,
        out_specs=(P("seq", None), P(None, "seq", "mp"), P(None, "seq", "mp")),
        check_vma=False,
    )
```

```python
import functools

import jax
import jax.numpy as jnp
from jax import lax
from jax.experimental import pallas as pl
from jax.experimental.pallas import tpu as pltpu
from jax.sharding import PartitionSpec as P

DILATION_FIRST1 = 2048
DILATION_SECOND2 = 4096


epsilon = 1e-05
root_half = 0.7071067811865476
inv_root_two_pi = 0.3989422804014327
half_log2_e = -0.7213475204444817
log2_inv_root_two_pi = -1.3257480647361593
SIDE_ROWS = 16
VMEM_LIMIT = 24 * 1024 * 1024


def gelu_parts(conv_out):
    normal_cdf = 0.5 * (1.0 + lax.erf(conv_out * root_half))
    gelu_slope = normal_cdf + conv_out * inv_root_two_pi * jnp.exp(-0.5 * conv_out * conv_out)
    return (conv_out * normal_cdf, gelu_slope)


def norm_parts(activation):
    values = activation.astype(jnp.float32)
    centre = jnp.mean(values, axis=-1, keepdims=True)
    centred = values - centre
    spread = jnp.mean(centred * centred, axis=-1, keepdims=True)
    inverse = lax.rsqrt(spread + epsilon)
    return (centred * inverse, inverse)


def gelu_and_slope(conv_out):
    normal_cdf = 0.5 + 0.5 * lax.erf(conv_out * root_half)
    density = jnp.exp2(conv_out * conv_out * half_log2_e + log2_inv_root_two_pi)
    return (conv_out * normal_cdf, normal_cdf + conv_out * density)


def active_hops(tap_count, dilation_blocks, seq_count):
    centre_tap = tap_count // 2
    hops = [(tap, dilation_blocks * (tap - centre_tap)) for tap in range(tap_count)]
    return [(tap, hop) for tap, hop in hops if abs(hop) < seq_count]


def shifted(x, axis, by):
    if by == 0:
        return x
    peers = lax.axis_size(axis)
    pairs = [(i, i + by) for i in range(peers) if 0 <= i + by < peers]
    return lax.ppermute(x, axis, pairs)


def loss_grad(hidden_top, targets, head_weight):
    logits = lax.dot_general(
        head_weight, hidden_top, (((0,), (1,)), ((), ())), preferred_element_type=jnp.float32
    )
    exponent = jnp.exp(logits)
    probability = exponent / jnp.sum(exponent, axis=0, keepdims=True)
    vocab_rows = lax.broadcasted_iota(jnp.int32, logits.shape, 0)
    onehot = (vocab_rows == targets[None, :]).astype(jnp.float32)
    weight = (targets >= 0).astype(jnp.float32)[None, :]
    dlogits = weight * (probability - onehot)
    return lax.dot_general(
        dlogits,
        head_weight.astype(jnp.float32),
        (((0,), (1,)), ((), ())),
        precision=lax.Precision.HIGHEST,
    )


def general_plan(hidden_entry_states, base_ids, mask_index, first_kernel, second_kernel, head_weight, first_hops, second_hops):
    seq_count = lax.axis_size("seq")
    rows_per_block, channels = hidden_entry_states.shape
    tap_count, _, own_width = first_kernel.shape
    mask_count = mask_index.shape[0]
    offsets = mask_index - lax.axis_index("seq") * rows_per_block
    positions = lax.broadcasted_iota(jnp.int32, (rows_per_block, mask_count), 0)
    masked = jnp.any(positions == offsets[None, :], axis=1)
    targets = jnp.where(masked, base_ids, -1)

    def used(kernel, hops):
        first_tap, last_tap = hops[0][0], hops[-1][0]
        return kernel[first_tap : last_tap + 1]

    def block_forward_pass(source, kernel, hops):
        stacked = jnp.concatenate([shifted(source, "seq", -hop) for _, hop in hops], axis=1)
        conv_out = jnp.dot(
            stacked,
            used(kernel, hops).reshape(len(hops) * channels, own_width),
            preferred_element_type=jnp.float32,
        )
        activation, gelu_slope = gelu_parts(conv_out)
        mixed_all = lax.all_gather(activation.astype(jnp.bfloat16), "mp", axis=1, tiled=True)
        normed, inverse = norm_parts(mixed_all)
        result = (source.astype(jnp.float32) + normed).astype(jnp.bfloat16)
        return (result, (source, normed, inverse, gelu_slope))

    def block_backward_pass(grad_out, saved, kernel, hops):
        source, normed, inverse, gelu_slope = saved
        mean_grad = jnp.mean(grad_out, axis=-1, keepdims=True)
        mean_cross = jnp.mean(grad_out * normed, axis=-1, keepdims=True)
        grad_act = inverse * (grad_out - mean_grad - normed * mean_cross)
        own_cols = lax.dynamic_slice_in_dim(
            grad_act, lax.axis_index("mp") * own_width, own_width, 1
        )
        grad_conv = (own_cols * gelu_slope).astype(jnp.bfloat16)
        tap_stack = jnp.stack([shifted(grad_conv, "seq", hop) for _, hop in hops], axis=0)
        input_part = jnp.einsum(
            "kro,kdo->rd", tap_stack, used(kernel, hops), preferred_element_type=jnp.float32
        )
        grad_in = grad_out + lax.psum(input_part.astype(jnp.bfloat16), "mp").astype(jnp.float32)
        kernel_part = jnp.einsum(
            "rd,kro->kdo", source, tap_stack, preferred_element_type=jnp.float32
        )
        by_owner = kernel_part.reshape(len(hops), seq_count, channels // seq_count, own_width)
        received = lax.all_to_all(
            by_owner.astype(jnp.bfloat16), "seq", split_axis=1, concat_axis=1, tiled=True
        ).astype(by_owner.dtype)
        first_tap, last_tap = hops[0][0], hops[-1][0]
        kernel_grad = jnp.pad(
            jnp.sum(received, axis=1),
            ((first_tap, tap_count - 1 - last_tap), (0, 0), (0, 0)),
        )
        return (grad_in, kernel_grad)

    hidden_one, saved_one = block_forward_pass(hidden_entry_states, first_kernel, first_hops)
    hidden_two, saved_two = block_forward_pass(hidden_one, second_kernel, second_hops)
    grad_two = loss_grad(hidden_two, targets, head_weight)
    grad_one, second_grad = block_backward_pass(grad_two, saved_two, second_kernel, second_hops)
    grad_zero, first_grad = block_backward_pass(grad_one, saved_one, first_kernel, first_hops)
    return (grad_zero.astype(jnp.bfloat16), first_grad, second_grad)


NN = (((1,), (0,)), ((), ()))
NT = (((1,), (1,)), ((), ()))
TN = (((0,), (0,)), ((), ()))


def dot(a, b, dims=NN):
    return lax.dot_general(a, b, dims, preferred_element_type=jnp.float32)


def swap(block, axis, offset):
    return lax.ppermute(block, axis, [(i, i ^ offset) for i in range(lax.axis_size(axis))])


def block_at(me, offset, width):
    return pl.ds(pl.multiple_of((me ^ offset) * width, width), width)


def stacked(blocks, axis):
    return blocks[0] if len(blocks) == 1 else jnp.concatenate(blocks, axis=axis)


def own_order(me, refs, count):
    width = refs[0].shape[1] // count
    return stacked(
        [stacked([ref[:, block_at(me, o, width)] for o in range(count)], 1) for ref in refs], 0
    )


def matrices_body(centre_tap, first_ref, second_ref, own_first_ref, own_second_ref, both_ref, sems):
    targets = (own_first_ref, own_second_ref, both_ref.at[0], both_ref.at[1])
    copies = [
        pltpu.make_async_copy(source.at[centre_tap], target, sems.at[n])
        for n, (source, target) in enumerate(zip((first_ref, second_ref) * 2, targets))
    ]
    for copy in copies:
        copy.start()
    for copy in copies:
        copy.wait()


def prepare_body(mask_ref, ids_ref, source_ref, own_ref, sent_targets_ref, sent_ref):
    rows = source_ref.shape[0]
    share = rows // 2
    entries = mask_ref.shape[1]
    part = lax.rem(lax.axis_index("mp"), 2)
    square = (entries, entries)
    diagonal = lax.broadcasted_iota(jnp.int32, square, 0) == lax.broadcasted_iota(jnp.int32, square, 1)
    offsets = (mask_ref[...] - lax.axis_index("seq") * rows).astype(jnp.float32)
    column = jnp.sum(jnp.where(diagonal, offsets, 0.0), axis=1, keepdims=True)
    positions = lax.broadcasted_iota(jnp.int32, (entries, rows), 1).astype(jnp.float32)
    masked = jnp.max((positions == column).astype(jnp.float32), axis=0, keepdims=True)
    targets = jnp.where(masked > 0.0, ids_ref[...].astype(jnp.float32), -1.0)
    targets = jnp.broadcast_to(targets, own_ref.shape)
    turned = pltpu.roll(targets, share, 1)
    own_ref[...] = targets.astype(jnp.bfloat16)
    sent_targets_ref[...] = jnp.where(part == 1, turned, targets).astype(jnp.bfloat16)
    sent_ref[...] = source_ref[pl.ds(pl.multiple_of(part * share, share), share), :]


def blank_body(first_ref, second_ref):
    first_ref[...] = jnp.zeros_like(first_ref)
    second_ref[...] = jnp.zeros_like(second_ref)


def square(me, matrix_refs):
    width = matrix_refs[0].shape[1]
    count = len(matrix_refs)
    return stacked(
        [stacked([ref[block_at(me, o, width), :] for o in range(count)], 0) for ref in matrix_refs],
        1,
    )


def row_halves(own_ref, far_ref, near_ref):
    return ((own_ref,), (far_ref, near_ref))


def first_block_body(count, own_ref, far_ref, near_ref, head_ref, *refs):
    matrix_refs = refs[:count]
    hidden_ref, normed_ref, scale_ref, hidden_flip_ref, source_flip_ref, head_out_ref = refs[count:]
    me = lax.axis_index("mp")
    half = own_ref.shape[0]
    width = matrix_refs[0].shape[1]
    weights = square(me, matrix_refs)
    for part, source_refs in enumerate(row_halves(own_ref, far_ref, near_ref)):
        rows = pl.ds(part * half, half)
        source = own_order(me, source_refs, count)
        activation, gelu_slope = gelu_and_slope(dot(source, weights))
        normed, inverse = norm_parts(activation)
        scale_ref[rows, :] = gelu_slope * inverse
        normed_ref[rows, :] = normed
        hidden = (source.astype(jnp.float32) + normed).astype(jnp.bfloat16)
        hidden_ref[rows, :] = hidden
        source_flip_ref[:, rows] = stacked([ref[...] for ref in source_refs], 0).T
        for offset in range(count):
            flipped = hidden[:, offset * width : (offset + 1) * width].T
            hidden_flip_ref[block_at(me, offset, width), rows] = flipped
    head_out_ref[...] = jnp.zeros_like(head_out_ref)
    classes = head_ref.shape[0]
    head_out_ref[0:classes, :] = own_order(me, (head_ref,), count)


def main_body(count, blocks, classes, own_targets_ref, peer_targets_ref, hidden_one_ref, normed_one_ref, scale_one_ref, hidden_flip_ref, source_flip_ref, head_ref, *refs):
    turns = blocks // 2
    matrix_refs, refs = refs[:count], refs[count:]
    self_ref, sent_refs, refs = refs[0], refs[1:turns], refs[turns:]
    grad_out_ref, grad_conv_out_ref = refs[:2]
    normed_two_ref, scale_two_ref, hidden_two_ref, grad_ref, grad_conv_ref = refs[2:]
    me, block = lax.axis_index("mp"), lax.axis_index("seq")
    half = own_targets_ref.shape[1]
    _, depth, width = self_ref.shape
    target_refs = (own_targets_ref, peer_targets_ref)
    weights = square(me, matrix_refs)
    head = head_ref[...]

    def second_block(part):
        rows = pl.ds(part * half, half)
        source = hidden_one_ref[rows, :]
        activation, gelu_slope = gelu_and_slope(dot(source, weights))
        normed, inverse = norm_parts(activation)
        scale_two_ref[rows, :] = gelu_slope * inverse
        normed_two_ref[rows, :] = normed
        hidden_two_ref[rows, :] = (source.astype(jnp.float32) + normed).astype(jnp.bfloat16)

    def loss_backward(part):
        rows = pl.ds(part * half, half)
        logits = dot(head, hidden_two_ref[rows, :], NT)
        class_rows = lax.broadcasted_iota(jnp.int32, logits.shape, 0)
        exponent = jnp.where(class_rows < classes, jnp.exp(logits), 0.0)
        probability = exponent / jnp.sum(exponent, axis=0, keepdims=True)
        targets = target_refs[part][...].astype(jnp.float32)
        onehot = (class_rows.astype(jnp.float32) == targets).astype(jnp.float32)
        weight = (targets >= 0.0).astype(jnp.float32)
        rest = jnp.where(class_rows < classes, weight * (probability - onehot), 0.0)
        terms = []
        for _ in range(3):
            term = rest.astype(jnp.bfloat16)
            terms.append(term)
            rest = rest - term.astype(jnp.float32)
        grad_ref[rows, :] = dot(jnp.concatenate(terms, axis=0), jnp.concatenate([head] * 3, axis=0), TN)

    def norm_backward(part, normed_ref, scale_ref):
        rows = pl.ds(part * half, half)
        grad_out, normed = grad_ref[rows, :], normed_ref[rows, :]
        mean_grad = jnp.mean(grad_out, axis=-1, keepdims=True)
        mean_cross = jnp.mean(grad_out * normed, axis=-1, keepdims=True)
        grad_conv_ref[rows, :] = (
            (grad_out - mean_grad - normed * mean_cross) * scale_ref[rows, :]
        ).astype(jnp.bfloat16)

    def input_backward(part):
        rows = pl.ds(part * half, half)
        grad_ref[rows, :] += dot(grad_conv_ref[rows, :], weights, NT)

    def kernel_parts(flip_ref, slot):
        sources = [
            flip_ref[pl.ds(pl.multiple_of((block ^ turn) * depth, depth), depth), :]
            for turn in range(turns)
        ]
        part = dot(stacked(sources, 0), grad_conv_ref[:, 0:width])
        self_ref[slot] = part[0:depth]
        for turn, ref in enumerate(sent_refs, 1):
            ref[slot] = part[turn * depth : (turn + 1) * depth].astype(jnp.bfloat16)

    second_block(0)
    second_block(1)
    loss_backward(0)
    norm_backward(0, normed_two_ref, scale_two_ref)
    loss_backward(1)
    norm_backward(1, normed_two_ref, scale_two_ref)
    input_backward(0)
    input_backward(1)
    kernel_parts(hidden_flip_ref, 1)
    norm_backward(0, normed_one_ref, scale_one_ref)
    norm_backward(1, normed_one_ref, scale_one_ref)
    kernel_parts(source_flip_ref, 0)
    grad_out_ref[...] = grad_ref[pl.ds(0, half), :]
    grad_conv_out_ref[...] = grad_conv_ref[pl.ds(0, half), :]


def input_grad_body(count, grad_ref, grad_conv_ref, *refs):
    matrix_refs, input_grad_ref = refs[:count], refs[count]
    me = lax.axis_index("mp")
    width = matrix_refs[0].shape[1]
    total = grad_ref[...] + dot(grad_conv_ref[...], square(me, matrix_refs), NT)
    for offset in range(count):
        input_grad_ref[:, block_at(me, offset, width)] = total[
            :, offset * width : (offset + 1) * width
        ].astype(jnp.bfloat16)


def total_body(centre_tap, first_in_ref, second_in_ref, input_grad_ref, self_ref, *refs):
    received = refs[:-5]
    first_ref, second_ref, grad_out_ref, sum_ref, sems = refs[-5:]
    copies = [pltpu.make_async_copy(input_grad_ref, grad_out_ref, sems.at[2])]
    copies[0].start()
    sum_ref[...] = self_ref[...] + sum(ref[...].astype(jnp.float32) for ref in received)
    for slot, ref in enumerate((first_ref, second_ref)):
        copies.append(pltpu.make_async_copy(sum_ref.at[slot], ref.at[centre_tap], sems.at[slot]))
        copies[-1].start()
    for copy in copies:
        copy.wait()


def local_plan(hidden_entry_states, base_ids, mask_index, first_kernel, second_kernel, head_weight):
    seq_count = lax.axis_size("seq")
    mp_count = lax.axis_size("mp")
    rows, channels = hidden_entry_states.shape
    tap_count, _, width = first_kernel.shape
    classes = head_weight.shape[1]
    centre_tap = tap_count // 2
    depth = channels // seq_count

    vmem = pl.BlockSpec(memory_space=pltpu.VMEM)
    hbm = pl.BlockSpec(memory_space=pltpu.HBM)

    def shape(dims, dtype=jnp.bfloat16):
        return jax.ShapeDtypeStruct(dims, dtype)

    def in_hbm(array):
        return pltpu.with_memory_space_constraint(array, pltpu.HBM)

    def call(body, in_specs, out_shape, out_specs=None, scratch=(), aliases={}, flops=0, moved=0):
        return pl.pallas_call(
            body,
            out_shape=out_shape,
            in_specs=in_specs,
            out_specs=(vmem,) * len(out_shape) if out_specs is None else out_specs,
            scratch_shapes=list(scratch),
            input_output_aliases=aliases,
            compiler_params=pltpu.CompilerParams(vmem_limit_bytes=VMEM_LIMIT),
            cost_estimate=pl.CostEstimate(flops=flops, bytes_accessed=moved, transcendentals=0),
        )

    matrix = shape((channels, width))
    own_first, own_second, own_both = call(
        functools.partial(matrices_body, centre_tap),
        [hbm] * 2,
        (matrix, matrix, shape((2, channels, width))),
        scratch=[pltpu.SemaphoreType.DMA((4,))],
    )(in_hbm(first_kernel), in_hbm(second_kernel))
    first, second = {0: own_first}, {0: own_second}
    bit = far = mp_count // 2
    while bit:
        for offset in list(first):
            if offset == 0 and bit != far:
                both = swap(own_both, "mp", bit)
                first[bit], second[bit] = both[0], both[1]
            else:
                first[offset ^ bit] = swap(first[offset], "mp", bit)
                second[offset ^ bit] = swap(second[offset], "mp", bit)
        bit //= 2
    first = [first[offset] for offset in range(mp_count)]
    second = [second[offset] for offset in range(mp_count)]

    own_targets, sent_targets, sent_rows = call(
        prepare_body, [vmem] * 3, (shape((SIDE_ROWS, rows)),) * 2 + (shape((rows // 2, channels)),)
    )(mask_index[None, :], base_ids[None, :], hidden_entry_states)
    far_rows = swap(sent_rows, "seq", seq_count // 2)
    near_rows = swap(far_rows, "mp", 1)
    peer_targets = swap(sent_targets, "seq", seq_count // 2)
    whole = shape((tap_count, depth, width), jnp.float32)
    first_grad, second_grad = call(blank_body, [], (whole, whole))()

    pair_rows = 2 * rows
    wide = shape((pair_rows, channels), jnp.float32)
    flip = shape((channels, pair_rows))
    product = 2 * pair_rows * channels * channels
    hidden_one, normed_one, scale_one, hidden_flip, source_flip, head = call(
        functools.partial(first_block_body, mp_count),
        [vmem] * (4 + mp_count),
        (shape((pair_rows, channels)), wide, wide, flip, flip, shape((SIDE_ROWS, channels))),
        flops=product,
        moved=8 * pair_rows * channels,
    )(hidden_entry_states, far_rows, near_rows, head_weight.T, *first)

    turns = seq_count // 2
    part = (2, depth, width)
    outs = call(
        functools.partial(main_body, mp_count, seq_count, classes),
        [vmem] * (8 + mp_count),
        (shape(part, jnp.float32),)
        + (shape(part),) * (turns - 1)
        + (shape((rows, channels), jnp.float32), shape((rows, channels))),
        scratch=[
            pltpu.VMEM((pair_rows, channels), jnp.float32),
            pltpu.VMEM((pair_rows, channels), jnp.float32),
            pltpu.VMEM((pair_rows, channels), jnp.bfloat16),
            pltpu.VMEM((pair_rows, channels), jnp.float32),
            pltpu.VMEM((pair_rows, channels), jnp.bfloat16),
        ],
        flops=3 * product,
        moved=16 * pair_rows * channels,
    )(own_targets, peer_targets, hidden_one, normed_one, scale_one, hidden_flip, source_flip, head, *second)
    own_part, sent, (grad_one, grad_conv) = outs[0], outs[1:-2], outs[-2:]

    received = [swap(piece, "seq", turn) for turn, piece in enumerate(sent, 1)]
    (input_grad,) = call(
        functools.partial(input_grad_body, mp_count),
        [vmem] * (2 + mp_count),
        (shape((rows, channels)),),
        flops=product // 2,
        moved=8 * rows * channels,
    )(grad_one, grad_conv, *first)
    first_grad, second_grad, input_grad = call(
        functools.partial(total_body, centre_tap),
        [hbm, hbm] + [vmem] * (1 + turns),
        (whole, whole, shape((rows, channels))),
        out_specs=(hbm,) * 3,
        scratch=[pltpu.VMEM(part, jnp.float32), pltpu.SemaphoreType.DMA((3,))],
        aliases={0: 0, 1: 1},
    )(first_grad, second_grad, input_grad, own_part, *received)
    return (input_grad, first_grad, second_grad)


def power_of_two(count):
    return count & (count - 1) == 0


def local(hidden_entry_states, base_ids, mask_index, first_kernel, second_kernel, head_weight):
    rows, channels = hidden_entry_states.shape
    tap_count, _, width = first_kernel.shape
    seq_count = lax.axis_size("seq")
    mp_count = lax.axis_size("mp")
    first_hops = active_hops(tap_count, DILATION_FIRST1 // rows, seq_count)
    second_hops = active_hops(tap_count, DILATION_SECOND2 // rows, seq_count)
    args = (hidden_entry_states, base_ids, mask_index, first_kernel, second_kernel, head_weight)
    fits = (
        power_of_two(mp_count)
        and power_of_two(seq_count)
        and mp_count > 1
        and seq_count > 1
        and width % 128 == 0
        and rows % 128 == 0
        and rows <= channels
        and (channels // seq_count) % 16 == 0
        and head_weight.shape[1] <= SIDE_ROWS
    )
    if len(first_hops) == 1 and len(second_hops) == 1 and fits:
        return local_plan(*args)
    return general_plan(*args, first_hops, second_hops)


def solution(mesh):
    placed = (P("seq", None), P("seq"), P("seq"), P(None, None, "mp"), P(None, None, "mp"), P())
    return jax.shard_map(
        local,
        mesh=mesh,
        in_specs=placed,
        out_specs=(P("seq", None), P(None, "seq", "mp"), P(None, "seq", "mp")),
        check_vma=False,
    )
```

```python
import functools

import jax
import jax.numpy as jnp
from jax import lax
from jax.experimental import pallas as pl
from jax.experimental.pallas import tpu as pltpu
from jax.sharding import PartitionSpec as P

DILATION_FIRST1 = 2048
DILATION_SECOND2 = 4096


epsilon = 1e-05
root_half = 0.7071067811865476
inv_root_two_pi = 0.3989422804014327
half_log2_e = -0.7213475204444817
log2_inv_root_two_pi = -1.3257480647361593
SIDE_ROWS = 16
VMEM_LIMIT = 24 * 1024 * 1024


def gelu_parts(conv_out):
    normal_cdf = 0.5 * (1.0 + lax.erf(conv_out * root_half))
    gelu_slope = normal_cdf + conv_out * inv_root_two_pi * jnp.exp(-0.5 * conv_out * conv_out)
    return (conv_out * normal_cdf, gelu_slope)


def norm_parts(activation):
    values = activation.astype(jnp.float32)
    centre = jnp.mean(values, axis=-1, keepdims=True)
    centred = values - centre
    spread = jnp.mean(centred * centred, axis=-1, keepdims=True)
    inverse = lax.rsqrt(spread + epsilon)
    return (centred * inverse, inverse)


def gelu_and_slope(conv_out):
    normal_cdf = 0.5 + 0.5 * lax.erf(conv_out * root_half)
    density = jnp.exp2(conv_out * conv_out * half_log2_e + log2_inv_root_two_pi)
    return (conv_out * normal_cdf, normal_cdf + conv_out * density)


def active_hops(tap_count, dilation_blocks, seq_count):
    centre_tap = tap_count // 2
    hops = [(tap, dilation_blocks * (tap - centre_tap)) for tap in range(tap_count)]
    return [(tap, hop) for tap, hop in hops if abs(hop) < seq_count]


def shifted(x, axis, by):
    if by == 0:
        return x
    peers = lax.axis_size(axis)
    pairs = [(i, i + by) for i in range(peers) if 0 <= i + by < peers]
    return lax.ppermute(x, axis, pairs)


def loss_grad(hidden_top, targets, head_weight):
    logits = lax.dot_general(
        head_weight, hidden_top, (((0,), (1,)), ((), ())), preferred_element_type=jnp.float32
    )
    exponent = jnp.exp(logits)
    probability = exponent / jnp.sum(exponent, axis=0, keepdims=True)
    vocab_rows = lax.broadcasted_iota(jnp.int32, logits.shape, 0)
    onehot = (vocab_rows == targets[None, :]).astype(jnp.float32)
    weight = (targets >= 0).astype(jnp.float32)[None, :]
    dlogits = weight * (probability - onehot)
    return lax.dot_general(
        dlogits,
        head_weight.astype(jnp.float32),
        (((0,), (1,)), ((), ())),
        precision=lax.Precision.HIGHEST,
    )


def general_plan(hidden_entry_states, base_ids, mask_index, first_kernel, second_kernel, head_weight, first_hops, second_hops):
    seq_count = lax.axis_size("seq")
    rows_per_block, channels = hidden_entry_states.shape
    tap_count, _, own_width = first_kernel.shape
    mask_count = mask_index.shape[0]
    offsets = mask_index - lax.axis_index("seq") * rows_per_block
    positions = lax.broadcasted_iota(jnp.int32, (rows_per_block, mask_count), 0)
    masked = jnp.any(positions == offsets[None, :], axis=1)
    targets = jnp.where(masked, base_ids, -1)

    def used(kernel, hops):
        first_tap, last_tap = hops[0][0], hops[-1][0]
        return kernel[first_tap : last_tap + 1]

    def block_forward_pass(source, kernel, hops):
        stacked = jnp.concatenate([shifted(source, "seq", -hop) for _, hop in hops], axis=1)
        conv_out = jnp.dot(
            stacked,
            used(kernel, hops).reshape(len(hops) * channels, own_width),
            preferred_element_type=jnp.float32,
        )
        activation, gelu_slope = gelu_parts(conv_out)
        mixed_all = lax.all_gather(activation.astype(jnp.bfloat16), "mp", axis=1, tiled=True)
        normed, inverse = norm_parts(mixed_all)
        result = (source.astype(jnp.float32) + normed).astype(jnp.bfloat16)
        return (result, (source, normed, inverse, gelu_slope))

    def block_backward_pass(grad_out, saved, kernel, hops):
        source, normed, inverse, gelu_slope = saved
        mean_grad = jnp.mean(grad_out, axis=-1, keepdims=True)
        mean_cross = jnp.mean(grad_out * normed, axis=-1, keepdims=True)
        grad_act = inverse * (grad_out - mean_grad - normed * mean_cross)
        own_cols = lax.dynamic_slice_in_dim(
            grad_act, lax.axis_index("mp") * own_width, own_width, 1
        )
        grad_conv = (own_cols * gelu_slope).astype(jnp.bfloat16)
        tap_stack = jnp.stack([shifted(grad_conv, "seq", hop) for _, hop in hops], axis=0)
        input_part = jnp.einsum(
            "kro,kdo->rd", tap_stack, used(kernel, hops), preferred_element_type=jnp.float32
        )
        grad_in = grad_out + lax.psum(input_part.astype(jnp.bfloat16), "mp").astype(jnp.float32)
        kernel_part = jnp.einsum(
            "rd,kro->kdo", source, tap_stack, preferred_element_type=jnp.float32
        )
        by_owner = kernel_part.reshape(len(hops), seq_count, channels // seq_count, own_width)
        received = lax.all_to_all(
            by_owner.astype(jnp.bfloat16), "seq", split_axis=1, concat_axis=1, tiled=True
        ).astype(by_owner.dtype)
        first_tap, last_tap = hops[0][0], hops[-1][0]
        kernel_grad = jnp.pad(
            jnp.sum(received, axis=1),
            ((first_tap, tap_count - 1 - last_tap), (0, 0), (0, 0)),
        )
        return (grad_in, kernel_grad)

    hidden_one, saved_one = block_forward_pass(hidden_entry_states, first_kernel, first_hops)
    hidden_two, saved_two = block_forward_pass(hidden_one, second_kernel, second_hops)
    grad_two = loss_grad(hidden_two, targets, head_weight)
    grad_one, second_grad = block_backward_pass(grad_two, saved_two, second_kernel, second_hops)
    grad_zero, first_grad = block_backward_pass(grad_one, saved_one, first_kernel, first_hops)
    return (grad_zero.astype(jnp.bfloat16), first_grad, second_grad)


NN = (((1,), (0,)), ((), ()))
NT = (((1,), (1,)), ((), ()))
TN = (((0,), (0,)), ((), ()))


def dot(a, b, dims=NN):
    return lax.dot_general(a, b, dims, preferred_element_type=jnp.float32)


def swap(block, axis, offset):
    return lax.ppermute(block, axis, [(i, i ^ offset) for i in range(lax.axis_size(axis))])


def block_at(me, offset, width):
    return pl.ds(pl.multiple_of((me ^ offset) * width, width), width)


def stacked(blocks, axis):
    return blocks[0] if len(blocks) == 1 else jnp.concatenate(blocks, axis=axis)


def own_order(me, refs, count):
    width = refs[0].shape[1] // count
    return stacked(
        [stacked([ref[:, block_at(me, o, width)] for o in range(count)], 1) for ref in refs], 0
    )


def matrices_body(centre_tap, first_ref, second_ref, own_first_ref, own_second_ref, sems):
    copies = [
        pltpu.make_async_copy(first_ref.at[centre_tap], own_first_ref, sems.at[0]),
        pltpu.make_async_copy(second_ref.at[centre_tap], own_second_ref, sems.at[1]),
    ]
    for copy in copies:
        copy.start()
    for copy in copies:
        copy.wait()


def prepare_body(mask_ref, ids_ref, source_ref, own_first_ref, own_second_ref, own_ref, sent_targets_ref, sent_ref, both_ref):
    rows = source_ref.shape[0]
    share = rows // 2
    entries = mask_ref.shape[1]
    part = lax.rem(lax.axis_index("mp"), 2)
    square = (entries, entries)
    diagonal = lax.broadcasted_iota(jnp.int32, square, 0) == lax.broadcasted_iota(jnp.int32, square, 1)
    offsets = (mask_ref[...] - lax.axis_index("seq") * rows).astype(jnp.float32)
    column = jnp.sum(jnp.where(diagonal, offsets, 0.0), axis=1, keepdims=True)
    positions = lax.broadcasted_iota(jnp.int32, (entries, rows), 1).astype(jnp.float32)
    masked = jnp.max((positions == column).astype(jnp.float32), axis=0, keepdims=True)
    targets = jnp.where(masked > 0.0, ids_ref[...].astype(jnp.float32), -1.0)
    targets = jnp.broadcast_to(targets, own_ref.shape)
    turned = pltpu.roll(targets, share, 1)
    own_ref[...] = targets.astype(jnp.bfloat16)
    sent_targets_ref[...] = jnp.where(part == 1, turned, targets).astype(jnp.bfloat16)
    both_ref[0] = own_first_ref[...]
    both_ref[1] = own_second_ref[...]
    sent_ref[...] = source_ref[pl.ds(pl.multiple_of(part * share, share), share), :]


def blank_body(first_ref, second_ref):
    first_ref[...] = jnp.zeros_like(first_ref)
    second_ref[...] = jnp.zeros_like(second_ref)


def square(me, matrix_refs):
    width = matrix_refs[0].shape[1]
    count = len(matrix_refs)
    return stacked(
        [stacked([ref[block_at(me, o, width), :] for o in range(count)], 0) for ref in matrix_refs],
        1,
    )


def row_halves(own_ref, far_ref, near_ref):
    return ((own_ref,), (far_ref, near_ref))


def first_block_body(count, own_ref, far_ref, near_ref, head_ref, *refs):
    matrix_refs = refs[:count]
    hidden_ref, normed_ref, scale_ref, hidden_flip_ref, source_flip_ref, head_out_ref = refs[count:]
    me = lax.axis_index("mp")
    half = own_ref.shape[0]
    width = matrix_refs[0].shape[1]
    weights = square(me, matrix_refs)
    for part, source_refs in enumerate(row_halves(own_ref, far_ref, near_ref)):
        rows = pl.ds(part * half, half)
        source = own_order(me, source_refs, count)
        activation, gelu_slope = gelu_and_slope(dot(source, weights))
        normed, inverse = norm_parts(activation)
        scale_ref[rows, :] = gelu_slope * inverse
        normed_ref[rows, :] = normed
        hidden = (source.astype(jnp.float32) + normed).astype(jnp.bfloat16)
        hidden_ref[rows, :] = hidden
        source_flip_ref[:, rows] = stacked([ref[...] for ref in source_refs], 0).T
        for offset in range(count):
            flipped = hidden[:, offset * width : (offset + 1) * width].T
            hidden_flip_ref[block_at(me, offset, width), rows] = flipped
    head_out_ref[...] = jnp.zeros_like(head_out_ref)
    classes = head_ref.shape[0]
    head_out_ref[0:classes, :] = own_order(me, (head_ref,), count)


def main_body(count, blocks, classes, own_targets_ref, peer_targets_ref, hidden_one_ref, normed_one_ref, scale_one_ref, hidden_flip_ref, source_flip_ref, head_ref, *refs):
    turns = blocks // 2
    matrix_refs, refs = refs[:count], refs[count:]
    self_ref, sent_refs, refs = refs[0], refs[1:turns], refs[turns:]
    grad_out_ref, grad_conv_out_ref = refs[:2]
    normed_two_ref, scale_two_ref, hidden_two_ref, grad_ref, grad_conv_ref = refs[2:]
    me, block = lax.axis_index("mp"), lax.axis_index("seq")
    half = own_targets_ref.shape[1]
    _, depth, width = self_ref.shape
    target_refs = (own_targets_ref, peer_targets_ref)
    weights = square(me, matrix_refs)
    head = head_ref[...]

    def second_block(part):
        rows = pl.ds(part * half, half)
        source = hidden_one_ref[rows, :]
        activation, gelu_slope = gelu_and_slope(dot(source, weights))
        normed, inverse = norm_parts(activation)
        scale_two_ref[rows, :] = gelu_slope * inverse
        normed_two_ref[rows, :] = normed
        hidden_two_ref[rows, :] = (source.astype(jnp.float32) + normed).astype(jnp.bfloat16)

    def loss_backward(part):
        rows = pl.ds(part * half, half)
        logits = dot(head, hidden_two_ref[rows, :], NT)
        class_rows = lax.broadcasted_iota(jnp.int32, logits.shape, 0)
        exponent = jnp.where(class_rows < classes, jnp.exp(logits), 0.0)
        probability = exponent / jnp.sum(exponent, axis=0, keepdims=True)
        targets = target_refs[part][...].astype(jnp.float32)
        onehot = (class_rows.astype(jnp.float32) == targets).astype(jnp.float32)
        weight = (targets >= 0.0).astype(jnp.float32)
        rest = jnp.where(class_rows < classes, weight * (probability - onehot), 0.0)
        terms = []
        for _ in range(3):
            term = rest.astype(jnp.bfloat16)
            terms.append(term)
            rest = rest - term.astype(jnp.float32)
        grad_ref[rows, :] = dot(jnp.concatenate(terms, axis=0), jnp.concatenate([head] * 3, axis=0), TN)

    def norm_backward(part, normed_ref, scale_ref):
        rows = pl.ds(part * half, half)
        grad_out, normed = grad_ref[rows, :], normed_ref[rows, :]
        mean_grad = jnp.mean(grad_out, axis=-1, keepdims=True)
        mean_cross = jnp.mean(grad_out * normed, axis=-1, keepdims=True)
        grad_conv_ref[rows, :] = (
            (grad_out - mean_grad - normed * mean_cross) * scale_ref[rows, :]
        ).astype(jnp.bfloat16)

    def input_backward(part):
        rows = pl.ds(part * half, half)
        grad_ref[rows, :] += dot(grad_conv_ref[rows, :], weights, NT)

    def kernel_parts(flip_ref, slot):
        sources = [
            flip_ref[pl.ds(pl.multiple_of((block ^ turn) * depth, depth), depth), :]
            for turn in range(turns)
        ]
        part = dot(stacked(sources, 0), grad_conv_ref[:, 0:width])
        self_ref[slot] = part[0:depth]
        for turn, ref in enumerate(sent_refs, 1):
            ref[slot] = part[turn * depth : (turn + 1) * depth].astype(jnp.bfloat16)

    second_block(0)
    second_block(1)
    loss_backward(0)
    norm_backward(0, normed_two_ref, scale_two_ref)
    loss_backward(1)
    norm_backward(1, normed_two_ref, scale_two_ref)
    input_backward(0)
    input_backward(1)
    kernel_parts(hidden_flip_ref, 1)
    norm_backward(0, normed_one_ref, scale_one_ref)
    norm_backward(1, normed_one_ref, scale_one_ref)
    kernel_parts(source_flip_ref, 0)
    grad_out_ref[...] = grad_ref[pl.ds(0, half), :]
    grad_conv_out_ref[...] = grad_conv_ref[pl.ds(0, half), :]


def input_grad_body(count, grad_ref, grad_conv_ref, *refs):
    matrix_refs, input_grad_ref = refs[:count], refs[count]
    me = lax.axis_index("mp")
    width = matrix_refs[0].shape[1]
    total = grad_ref[...] + dot(grad_conv_ref[...], square(me, matrix_refs), NT)
    for offset in range(count):
        input_grad_ref[:, block_at(me, offset, width)] = total[
            :, offset * width : (offset + 1) * width
        ].astype(jnp.bfloat16)


def total_body(centre_tap, first_in_ref, second_in_ref, input_grad_ref, self_ref, *refs):
    received = refs[:-5]
    first_ref, second_ref, grad_out_ref, sum_ref, sems = refs[-5:]
    copies = [pltpu.make_async_copy(input_grad_ref, grad_out_ref, sems.at[2])]
    copies[0].start()
    sum_ref[...] = self_ref[...] + sum(ref[...].astype(jnp.float32) for ref in received)
    for slot, ref in enumerate((first_ref, second_ref)):
        copies.append(pltpu.make_async_copy(sum_ref.at[slot], ref.at[centre_tap], sems.at[slot]))
        copies[-1].start()
    for copy in copies:
        copy.wait()


def local_plan(hidden_entry_states, base_ids, mask_index, first_kernel, second_kernel, head_weight):
    seq_count = lax.axis_size("seq")
    mp_count = lax.axis_size("mp")
    rows, channels = hidden_entry_states.shape
    tap_count, _, width = first_kernel.shape
    classes = head_weight.shape[1]
    centre_tap = tap_count // 2
    depth = channels // seq_count

    vmem = pl.BlockSpec(memory_space=pltpu.VMEM)
    hbm = pl.BlockSpec(memory_space=pltpu.HBM)

    def shape(dims, dtype=jnp.bfloat16):
        return jax.ShapeDtypeStruct(dims, dtype)

    def in_hbm(array):
        return pltpu.with_memory_space_constraint(array, pltpu.HBM)

    def call(body, in_specs, out_shape, out_specs=None, scratch=(), aliases={}, flops=0, moved=0):
        return pl.pallas_call(
            body,
            out_shape=out_shape,
            in_specs=in_specs,
            out_specs=(vmem,) * len(out_shape) if out_specs is None else out_specs,
            scratch_shapes=list(scratch),
            input_output_aliases=aliases,
            compiler_params=pltpu.CompilerParams(vmem_limit_bytes=VMEM_LIMIT),
            cost_estimate=pl.CostEstimate(flops=flops, bytes_accessed=moved, transcendentals=0),
        )

    matrix = shape((channels, width))
    own_first, own_second = call(
        functools.partial(matrices_body, centre_tap),
        [hbm] * 2,
        (matrix, matrix),
        scratch=[pltpu.SemaphoreType.DMA((2,))],
    )(in_hbm(first_kernel), in_hbm(second_kernel))
    own_targets, sent_targets, sent_rows, own_both = call(
        prepare_body,
        [vmem] * 5,
        (shape((SIDE_ROWS, rows)),) * 2 + (shape((rows // 2, channels)), shape((2, channels, width))),
    )(mask_index[None, :], base_ids[None, :], hidden_entry_states, own_first, own_second)
    first, second = {0: own_first}, {0: own_second}
    bit = far = mp_count // 2
    while bit:
        for offset in list(first):
            if offset == 0 and bit != far:
                both = swap(own_both, "mp", bit)
                first[bit], second[bit] = both[0], both[1]
            else:
                first[offset ^ bit] = swap(first[offset], "mp", bit)
                second[offset ^ bit] = swap(second[offset], "mp", bit)
        bit //= 2
    first = [first[offset] for offset in range(mp_count)]
    second = [second[offset] for offset in range(mp_count)]

    far_rows = swap(sent_rows, "seq", seq_count // 2)
    near_rows = swap(far_rows, "mp", 1)
    peer_targets = swap(sent_targets, "seq", seq_count // 2)
    whole = shape((tap_count, depth, width), jnp.float32)
    first_grad, second_grad = call(blank_body, [], (whole, whole))()

    pair_rows = 2 * rows
    wide = shape((pair_rows, channels), jnp.float32)
    flip = shape((channels, pair_rows))
    product = 2 * pair_rows * channels * channels
    hidden_one, normed_one, scale_one, hidden_flip, source_flip, head = call(
        functools.partial(first_block_body, mp_count),
        [vmem] * (4 + mp_count),
        (shape((pair_rows, channels)), wide, wide, flip, flip, shape((SIDE_ROWS, channels))),
        flops=product,
        moved=8 * pair_rows * channels,
    )(hidden_entry_states, far_rows, near_rows, head_weight.T, *first)

    turns = seq_count // 2
    part = (2, depth, width)
    outs = call(
        functools.partial(main_body, mp_count, seq_count, classes),
        [vmem] * (8 + mp_count),
        (shape(part, jnp.float32),)
        + (shape(part),) * (turns - 1)
        + (shape((rows, channels), jnp.float32), shape((rows, channels))),
        scratch=[
            pltpu.VMEM((pair_rows, channels), jnp.float32),
            pltpu.VMEM((pair_rows, channels), jnp.float32),
            pltpu.VMEM((pair_rows, channels), jnp.bfloat16),
            pltpu.VMEM((pair_rows, channels), jnp.float32),
            pltpu.VMEM((pair_rows, channels), jnp.bfloat16),
        ],
        flops=3 * product,
        moved=16 * pair_rows * channels,
    )(own_targets, peer_targets, hidden_one, normed_one, scale_one, hidden_flip, source_flip, head, *second)
    own_part, sent, (grad_one, grad_conv) = outs[0], outs[1:-2], outs[-2:]

    received = [swap(piece, "seq", turn) for turn, piece in enumerate(sent, 1)]
    (input_grad,) = call(
        functools.partial(input_grad_body, mp_count),
        [vmem] * (2 + mp_count),
        (shape((rows, channels)),),
        flops=product // 2,
        moved=8 * rows * channels,
    )(grad_one, grad_conv, *first)
    first_grad, second_grad, input_grad = call(
        functools.partial(total_body, centre_tap),
        [hbm, hbm] + [vmem] * (1 + turns),
        (whole, whole, shape((rows, channels))),
        out_specs=(hbm,) * 3,
        scratch=[pltpu.VMEM(part, jnp.float32), pltpu.SemaphoreType.DMA((3,))],
        aliases={0: 0, 1: 1},
    )(first_grad, second_grad, input_grad, own_part, *received)
    return (input_grad, first_grad, second_grad)


def power_of_two(count):
    return count & (count - 1) == 0


def local(hidden_entry_states, base_ids, mask_index, first_kernel, second_kernel, head_weight):
    rows, channels = hidden_entry_states.shape
    tap_count, _, width = first_kernel.shape
    seq_count = lax.axis_size("seq")
    mp_count = lax.axis_size("mp")
    first_hops = active_hops(tap_count, DILATION_FIRST1 // rows, seq_count)
    second_hops = active_hops(tap_count, DILATION_SECOND2 // rows, seq_count)
    args = (hidden_entry_states, base_ids, mask_index, first_kernel, second_kernel, head_weight)
    fits = (
        power_of_two(mp_count)
        and power_of_two(seq_count)
        and mp_count > 1
        and seq_count > 1
        and width % 128 == 0
        and rows % 128 == 0
        and rows <= channels
        and (channels // seq_count) % 16 == 0
        and head_weight.shape[1] <= SIDE_ROWS
    )
    if len(first_hops) == 1 and len(second_hops) == 1 and fits:
        return local_plan(*args)
    return general_plan(*args, first_hops, second_hops)


def solution(mesh):
    placed = (P("seq", None), P("seq"), P("seq"), P(None, None, "mp"), P(None, None, "mp"), P())
    return jax.shard_map(
        local,
        mesh=mesh,
        in_specs=placed,
        out_specs=(P("seq", None), P(None, "seq", "mp"), P(None, "seq", "mp")),
        check_vma=False,
    )
```
